128 devices in a mesh: dp: 4 (over x), gx: 4 (over y_lo, core), gy: 8 (over z, y_hi).
Axes of the slice: x: 4, y: 4 (y_hi: 2, y_lo: 2; y = y_hi * 2 + y_lo), z: 4, core: 2. Of those that a mesh axis runs over, the one named last changes fastest.
Arguments:
- field: bfloat16 [4, 20, 256, 16384], P('dp', None, 'gx', 'gy'), may hold values from -6 to 6
- spectral_weight: bfloat16 [12, 20, 20, 2, 4096], P('dp', None, None, None, ('gx', 'gy')), may hold values from -6 to 6
- bypass_weight: bfloat16 [20, 20], replicated, may hold values from -1.25 to 1.25
- bias: float32 [20], replicated, may hold values from -3 to 3
- cotangent: bfloat16 [4, 20, 256, 16384], P('dp', None, 'gx', 'gy'), may hold values from -6 to 6
Outputs:
- activation: bfloat16 [4, 20, 256, 16384], P('dp', None, 'gx', 'gy')
- field_grad: bfloat16 [4, 20, 256, 16384], P('dp', None, 'gx', 'gy')
- weight_grad: float32 [12, 20, 20, 2, 4096], P('dp', None, None, None, ('gx', 'gy'))
The draws below stay inside these ranges and needn't reach their ends.
All inputs are finite; a program needn't handle non-finite values.
Results may differ from the reference program's by a relative error of at most 0.024.
Values may be sent and summed in bfloat16 or wider, within the bound.
No kernel may reach another device: no remote copies, remote signals or barrier semaphores. Data moves between devices by JAX's collectives and lax.ppermute only.
A program may use at most 192 MiB of HBM per device.

```python
import math
import jax
import jax.numpy as jnp
from jax import lax

CH = 20
NX = 256
NY = 256
NZ = 64
KX = 64
KY = 64
KZ = 12
SAMPLES = 4


def level_of(rng, dims, shards, low, largest):
    loudness, own = 1.0, jax.random.fold_in(rng, 6)
    for dim, shards_of in shards:
        steps = jnp.exp(jax.random.uniform(jax.random.fold_in(own, dim), (shards_of,), jnp.float32, low / len(shards), largest / len(shards)))
        loudness = loudness * jnp.repeat(steps, dims[dim] // shards_of).reshape([-1 if axis == dim else 1 for axis in range(len(dims))])
    return loudness


def bell_draw(stream_key, shape, deviation, limit, split=(), held_as=jnp.bfloat16):
    array = jax.random.normal(stream_key, shape, jnp.float32) * deviation
    if len(split) > 0:
        array = level_of(stream_key, shape, split, -0.22, 0.18) * array
    return jnp.clip(array, min=-limit, max=limit).astype(held_as)


def setup_inputs(seed: int = 0) -> dict:
    arg_keys = jax.random.split(jax.random.key(seed), 6)
    field = bell_draw(arg_keys[0], (SAMPLES, CH, NX, NY * NZ), 1.0, 6.0, ((0, 4), (2, 4), (3, 8)))
    spectral_weight = bell_draw(arg_keys[1], (KZ, CH, CH, 2, KY * KX), 1.0, 6.0, ((0, 4), (4, 32)))
    bypass_weight = bell_draw(arg_keys[2], (CH, CH), CH ** -0.5, 1.25)
    bias = bell_draw(arg_keys[3], (CH,), 0.5, 3.0, (), jnp.float32)
    cotangent = bell_draw(arg_keys[4], (SAMPLES, CH, NX, NY * NZ), 1.0, 6.0, ((0, 4), (2, 4), (3, 8)))
    return dict(field=field, spectral_weight=spectral_weight, bypass_weight=bypass_weight, bias=bias, cotangent=cotangent)


def kept_freqs(count):
    index = jnp.arange(count, dtype=jnp.int32)
    return jnp.where(index < count // 2, index, index - count)

def phases(freqs, length):
    points = jnp.arange(length, dtype=jnp.int32)
    offsets = jnp.mod(freqs[:, None] * points[None, :], length)
    return offsets.astype(jnp.float32) * (2.0 * math.pi / length)

def contract(form, left, right):
    return jnp.einsum(form, left.astype(jnp.float32), right.astype(jnp.float32), precision=lax.Precision.HIGHEST)

def depth_columns(factors):
    angle = phases(jnp.arange(KZ, dtype=jnp.int32), NZ)
    cosine = (jnp.cos(angle) * factors[:, None]).T
    sine = (-jnp.sin(angle) * factors[:, None]).T
    return jnp.concatenate([cosine, sine], axis=1).astype(jnp.bfloat16)

def depth_rows(factors):
    angle = phases(jnp.arange(KZ, dtype=jnp.int32), NZ)
    return jnp.stack([jnp.cos(angle) * factors[:, None], -jnp.sin(angle) * factors[:, None]]).astype(jnp.bfloat16)

def wave_tables(count, length):
    angle = phases(kept_freqs(count), length)
    return (jnp.cos(angle).astype(jnp.bfloat16), jnp.sin(angle).astype(jnp.bfloat16))

def forward_type(values, depth_table):
    channels = values.shape[0]
    depth_modes = contract('cxyz,zk->kcxy', values, depth_table).astype(jnp.bfloat16)
    depth_modes = depth_modes.reshape(2, KZ * channels, NX, NY)
    real_in = depth_modes[0]
    imag_in = depth_modes[1]
    cos_y, sin_y = wave_tables(KY, NY)
    form_y = 'rxy,qy->rxq'
    line_real = (contract(form_y, real_in, cos_y) + contract(form_y, imag_in, sin_y)).astype(jnp.bfloat16)
    line_imag = (contract(form_y, imag_in, cos_y) - contract(form_y, real_in, sin_y)).astype(jnp.bfloat16)
    cos_x, sin_x = wave_tables(KX, NX)
    form_x = 'rxq,kx->rqk'
    spec_real = contract(form_x, line_real, cos_x) + contract(form_x, line_imag, sin_x)
    spec_imag = contract(form_x, line_imag, cos_x) - contract(form_x, line_real, sin_x)
    spectrum = jnp.stack([spec_real, spec_imag], axis=1).astype(jnp.bfloat16)
    return spectrum.reshape(KZ, channels, 2, KY, KX)

def inverse_type(modes, depth_table):
    channels = modes.shape[1]
    spectrum = modes.reshape(KZ * channels, 2, KY, KX)
    real_in = spectrum[:, 0]
    imag_in = spectrum[:, 1]
    cos_x, sin_x = wave_tables(KX, NX)
    form_x = 'rqk,kx->rxq'
    line_real = (contract(form_x, real_in, cos_x) - contract(form_x, imag_in, sin_x)).astype(jnp.bfloat16)
    line_imag = (contract(form_x, real_in, sin_x) + contract(form_x, imag_in, cos_x)).astype(jnp.bfloat16)
    cos_y, sin_y = wave_tables(KY, NY)
    form_y = 'rxq,qy->rxy'
    plane_real = (contract(form_y, line_real, cos_y) - contract(form_y, line_imag, sin_y)).astype(jnp.bfloat16)
    plane_imag = (contract(form_y, line_real, sin_y) + contract(form_y, line_imag, cos_y)).astype(jnp.bfloat16)
    form_z = 'kcxy,kz->cxyz'
    result = contract(form_z, plane_real.reshape(KZ, channels, NX, NY), depth_table[0])
    return result + contract(form_z, plane_imag.reshape(KZ, channels, NX, NY), depth_table[1])

def mix_modes(spectrum, weight):
    form = 'zcqk,zcoqk->zoqk'
    spec_real = spectrum[:, :, 0]
    spec_imag = spectrum[:, :, 1]
    weight_real = weight[:, :, :, 0]
    weight_imag = weight[:, :, :, 1]
    real = contract(form, spec_real, weight_real) - contract(form, spec_imag, weight_imag)
    imag = contract(form, spec_real, weight_imag) + contract(form, spec_imag, weight_real)
    return jnp.stack([real, imag], axis=2).astype(jnp.bfloat16)

def weight_term(spectrum, gradient):
    form = 'zcqk,zoqk->zcoqk'
    spec_real = spectrum[:, :, 0]
    spec_imag = spectrum[:, :, 1]
    grad_real = gradient[:, :, 0]
    grad_imag = gradient[:, :, 1]
    real = contract(form, spec_real, grad_real) + contract(form, spec_imag, grad_imag)
    imag = contract(form, spec_real, grad_imag) - contract(form, spec_imag, grad_real)
    return jnp.stack([real, imag], axis=3)

def modes_back(gradient, weight):
    form = 'zoqk,zcoqk->zcqk'
    grad_real = gradient[:, :, 0]
    grad_imag = gradient[:, :, 1]
    weight_real = weight[:, :, :, 0]
    weight_imag = weight[:, :, :, 1]
    real = contract(form, grad_real, weight_real) + contract(form, grad_imag, weight_imag)
    imag = contract(form, grad_imag, weight_real) - contract(form, grad_real, weight_imag)
    return jnp.stack([real, imag], axis=2).astype(jnp.bfloat16)

def reference(field, spectral_weight, bypass_weight, bias, cotangent):
    weight = spectral_weight.reshape(KZ, CH, CH, 2, KY, KX)
    kz_index = jnp.arange(KZ, dtype=jnp.int32)
    fold_factors = jnp.where(kz_index == 0, 1.0, 2.0).astype(jnp.float32) / float(NX * NY * NZ)
    flat_factors = jnp.ones((KZ,), jnp.float32)
    activations = []
    field_grads = []
    weight_grad = jnp.zeros((KZ, CH, CH, 2, KY, KX), jnp.float32)
    for sample in range(SAMPLES):
        values = field[sample].reshape(CH, NX, NY, NZ)
        spectral_in = forward_type(values, depth_columns(flat_factors))
        mode_out = mix_modes(spectral_in, weight)
        preact = inverse_type(mode_out, depth_rows(fold_factors))
        preact = preact + contract('oc,cxyz->oxyz', bypass_weight, values) + bias[:, None, None, None]
        activation, pullback = jax.vjp(jax.nn.gelu, preact)
        upstream = cotangent[sample].reshape(CH, NX, NY, NZ).astype(jnp.float32)
        preact_grad = pullback(upstream)[0].astype(jnp.bfloat16)
        mode_grad = forward_type(preact_grad, depth_columns(fold_factors))
        weight_grad = weight_grad + weight_term(spectral_in, mode_grad)
        spectral_grad = modes_back(mode_grad, weight)
        field_grad = inverse_type(spectral_grad, depth_rows(flat_factors))
        field_grad = field_grad + contract('oc,oxyz->cxyz', bypass_weight, preact_grad)
        activations.append(activation.astype(jnp.bfloat16).reshape(CH, NX, NY * NZ))
        field_grads.append(field_grad.astype(jnp.bfloat16).reshape(CH, NX, NY * NZ))
    return (jnp.stack(activations), jnp.stack(field_grads), weight_grad.reshape(KZ, CH, CH, 2, KY * KX))
```

```python
import functools
import math

import jax
import jax.numpy as jnp
import ml_dtypes
import numpy as np
from jax import lax
from jax.experimental import pallas as pl
from jax.experimental.pallas import tpu as pltpu
from jax.sharding import PartitionSpec as P

CH = 20
NX = 256
NY = 256
NZ = 64
KX = 64
KY = 64
KZ = 12
GX = 4
GY = 8
DP = 4
XL = NX // GX
YL = NY // GY
YB = 8
STEPS = YL // YB
LANES = YB * NZ
KB = KZ // GX
ROWS = 2 * KB * YB
GROUP = 4
GROUPS = CH // GROUP
GL = GROUP * KX
WIDE = CH * KX
XB = 16
ORDER = (0, 2, 1, 3)

BF = jnp.bfloat16
F32 = jnp.float32


def wave(freqs, points, length):
    offsets = np.mod(freqs[:, None] * points[None, :], length)
    angle = offsets.astype(np.float32) * np.float32(2.0 * math.pi / length)
    return np.cos(angle), np.sin(angle)


def kept(count):
    index = np.arange(count)
    return np.where(index < count // 2, index, index - count)


def depth_tables():
    out = np.zeros((GX, 2, GX, KB, YB, YB, NZ), np.float32)
    for b in range(GX):
        for pos, delta in enumerate(ORDER):
            freqs = (b ^ delta) * KB + np.arange(KB)
            cosine, sine = wave(freqs, np.arange(NZ), NZ)
            for y in range(YB):
                out[b, 0, pos, :, y, y] = cosine
                out[b, 1, pos, :, y, y] = -sine
    return out.reshape(GX, 2 * KZ * YB, LANES).astype(ml_dtypes.bfloat16)


def width_tables():
    out = np.zeros((GX, 2, XL, GL), np.float32)
    for b in range(GX):
        cosine, sine = wave(kept(KX), b * XL + np.arange(XL), NX)
        out[b, 0] = np.tile(cosine.T, (1, GROUP))
        out[b, 1] = np.tile(sine.T, (1, GROUP))
    return out.astype(ml_dtypes.bfloat16)


def line_tables():
    out = np.zeros((GY, GY, 2, 2, GX, KB, STEPS, 2, KB, YB), np.float32)
    fy = kept(KY)
    for g in range(GY):
        cosine, sine = wave(fy, g * YL + np.arange(YL), NY)
        cosine = cosine.reshape(GX, GY, 2, STEPS, YB)
        sine = sine.reshape(GX, GY, 2, STEPS, YB)
        for i in range(KB):
            for owner in range(GY):
                for q in range(2):
                    c = cosine[:, owner, q]
                    s = sine[:, owner, q]
                    out[g, owner, q, 0, :, i, :, 0, i] = c
                    out[g, owner, q, 0, :, i, :, 1, i] = s
                    out[g, owner, q, 1, :, i, :, 0, i] = -s
                    out[g, owner, q, 1, :, i, :, 1, i] = c
    return out.reshape(GY, GY * 48, STEPS * ROWS).astype(ml_dtypes.bfloat16)


DEPTH = depth_tables()
WIDTH = width_tables()
LINE = line_tables()
SPREAD = np.kron(np.eye(CH), np.ones((XB, 1))).astype(ml_dtypes.bfloat16)
SAME = np.kron(np.ones((CH, CH)), np.eye(XB)).astype(ml_dtypes.bfloat16)


def dot(left, right, left_dim=1, right_dim=0):
    return lax.dot_general(
        left, right, (((left_dim,), (right_dim,)), ((), ())), preferred_element_type=F32
    )


def fill_width(wide_ref, blocks_ref):
    rows = lax.broadcasted_iota(jnp.int32, (GL, GL), 0) // XL
    columns = lax.broadcasted_iota(jnp.int32, (GL, GL), 1) // KX
    for part in range(2):
        strip = wide_ref[0, part].astype(F32)
        full = jnp.concatenate([strip] * GROUP, axis=0)
        blocks_ref[part] = jnp.where(rows == columns, full, 0.0).astype(BF)


def forward_columns(source_ref, depth_ref, blocks_ref, outs):
    half = KZ * YB
    for j in range(GROUPS):
        rows = source_ref[GROUP * j : GROUP * (j + 1)].reshape(GROUP * XL, LANES)
        planes = dot(depth_ref[0], rows, 1, 1).astype(BF)
        by_cos = dot(planes, blocks_ref[0])
        by_sin = dot(planes, blocks_ref[1])
        real = by_cos[:half] + by_sin[half:]
        imag = by_cos[half:] - by_sin[:half]
        for pos in range(GX):
            lo = pos * KB * YB
            piece = jnp.concatenate([real[lo : lo + KB * YB], imag[lo : lo + KB * YB]], axis=0)
            outs[pos][0, :, GL * j : GL * (j + 1)] = piece.astype(BF)


def inverse_columns(ins, depth_ref, blocks_ref, total_ref):
    half = KZ * YB
    part = KB * YB
    for j in range(GROUPS):
        pieces = [ref[0, :, GL * j : GL * (j + 1)].astype(F32) for ref in ins]
        stacked = jnp.concatenate(
            [piece[:part] for piece in pieces] + [piece[part:] for piece in pieces], axis=0
        ).astype(BF)
        by_cos = dot(stacked, blocks_ref[0], 1, 1)
        by_sin = dot(stacked, blocks_ref[1], 1, 1)
        real = by_cos[:half] - by_sin[half:]
        imag = by_sin[:half] + by_cos[half:]
        planes = jnp.concatenate([real, imag], axis=0).astype(BF)
        values = dot(planes, depth_ref[0], 0, 0)
        total_ref[GROUP * j : GROUP * (j + 1)] = values.reshape(GROUP, XL, LANES)


def add_bypass(source_ref, mixer_ref, total_ref):
    @pl.loop(0, XL // XB)
    def _(i):
        span = pl.ds(pl.multiple_of(i * XB, XB), XB)
        rows = source_ref[:, span, :].reshape(CH * XB, LANES)
        mixed = dot(mixer_ref[...], rows).reshape(CH, XB, LANES)
        total_ref[:, span, :] = total_ref[:, span, :] + mixed


def start_kernel(where_ref, field_ref, depth_ref, wide_ref, o0, o1, o2, o3, blocks_ref):
    @pl.when(pl.program_id(0) == 0)
    def _():
        fill_width(wide_ref, blocks_ref)

    forward_columns(field_ref, depth_ref, blocks_ref, (o0, o1, o2, o3))


ROOT = math.sqrt(2.0 / math.pi)
CUBE = 0.044715


def middle_kernel(
    where_ref, bias_ref, i0, i1, i2, i3, field_ref, upstream_ref, mixer_ref, depth_ref, wide_ref,
    act_ref, grad_ref, o0, o1, o2, o3, blocks_ref, total_ref,
):
    @pl.when(pl.program_id(0) == 0)
    def _():
        fill_width(wide_ref, blocks_ref)

    inverse_columns((i0, i1, i2, i3), depth_ref, blocks_ref, total_ref)
    add_bypass(field_ref, mixer_ref, total_ref)

    @pl.loop(0, CH)
    def _(channel):
        shift = bias_ref[channel]
        for i in range(XL // XB):
            span = slice(i * XB, (i + 1) * XB)
            x = total_ref[channel, span, :] + shift
            square = x * x
            t = jnp.tanh(x * (ROOT + (ROOT * CUBE) * square))
            h = 0.5 * t + 0.5
            act = x * h
            slope = h + act * (1.0 - h) * (2.0 * ROOT + (6.0 * ROOT * CUBE) * square)
            act_ref[channel, span, :] = act.astype(BF)
            up = upstream_ref[channel, span, :].astype(F32)
            grad_ref[channel, span, :] = (up * slope).astype(BF)

    forward_columns(grad_ref, depth_ref, blocks_ref, (o0, o1, o2, o3))


def end_kernel(
    where_ref, i0, i1, i2, i3, grad_ref, mixer_ref, depth_ref, wide_ref, out_ref,
    blocks_ref, total_ref,
):
    @pl.when(pl.program_id(0) == 0)
    def _():
        fill_width(wide_ref, blocks_ref)

    inverse_columns((i0, i1, i2, i3), depth_ref, blocks_ref, total_ref)
    add_bypass(grad_ref, mixer_ref, total_ref)

    @pl.loop(0, CH)
    def _(channel):
        out_ref[channel] = total_ref[channel].astype(BF)


def column_specs():
    columns = pl.BlockSpec((CH, XL, LANES), lambda i, w: (0, 0, i))
    coeffs = pl.BlockSpec((1, ROWS, WIDE), lambda i, w: (i, 0, 0))
    depth = pl.BlockSpec((1, 2 * KZ * YB, LANES), lambda i, w: (w[1], 0, 0))
    wide = pl.BlockSpec((1, 2, XL, GL), lambda i, w: (w[1], 0, 0, 0))
    mixer = pl.BlockSpec((CH * XB, CH * XB), lambda i, w: (0, 0))
    return columns, coeffs, depth, wide, mixer


COEFFS = jax.ShapeDtypeStruct((STEPS, ROWS, WIDE), BF)
COLUMNS = jax.ShapeDtypeStruct((CH, XL, YL * NZ), BF)
BLOCKS = pltpu.VMEM((2, GL, GL), BF)
TOTAL = pltpu.VMEM((CH, XL, LANES), F32)
PARAMS = pltpu.CompilerParams(vmem_limit_bytes=56 * 1024 * 1024)


def start_columns(where, field):
    columns, coeffs, depth, wide, _ = column_specs()
    return pl.pallas_call(
        start_kernel,
        grid_spec=pltpu.PrefetchScalarGridSpec(
            num_scalar_prefetch=1,
            grid=(STEPS,),
            in_specs=[columns, depth, wide],
            out_specs=[coeffs] * 4,
            scratch_shapes=[BLOCKS],
        ),
        out_shape=[COEFFS] * 4,
        compiler_params=PARAMS,
        name="start_columns",
    )(where, field, jnp.asarray(DEPTH), jnp.asarray(WIDTH))


def middle_columns(where, bias, coeffs_in, field, upstream, mixer):
    columns, coeffs, depth, wide, mix = column_specs()
    return pl.pallas_call(
        middle_kernel,
        grid_spec=pltpu.PrefetchScalarGridSpec(
            num_scalar_prefetch=1,
            grid=(STEPS,),
            in_specs=[pl.BlockSpec(memory_space=pltpu.SMEM)]
            + [coeffs] * 4
            + [columns, columns, mix, depth, wide],
            out_specs=[columns, columns] + [coeffs] * 4,
            scratch_shapes=[BLOCKS, TOTAL],
        ),
        out_shape=[COLUMNS, COLUMNS] + [COEFFS] * 4,
        compiler_params=PARAMS,
        name="middle_columns",
    )(where, bias, *coeffs_in, field, upstream, mixer, jnp.asarray(DEPTH), jnp.asarray(WIDTH))


def end_columns(where, coeffs_in, grad, mixer):
    columns, coeffs, depth, wide, mix = column_specs()
    return pl.pallas_call(
        end_kernel,
        grid_spec=pltpu.PrefetchScalarGridSpec(
            num_scalar_prefetch=1,
            grid=(STEPS,),
            in_specs=[coeffs] * 4 + [columns, mix, depth, wide],
            out_specs=columns,
            scratch_shapes=[BLOCKS, TOTAL],
        ),
        out_shape=COLUMNS,
        compiler_params=PARAMS,
        name="end_columns",
    )(where, *coeffs_in, grad, mixer, jnp.asarray(DEPTH), jnp.asarray(WIDTH))


def line_kernel(where_ref, a_ref, b_ref, c_ref, table_ref, out_ref):
    total = a_ref[...].astype(F32) + b_ref[...].astype(F32) + c_ref[...].astype(F32)
    rows = total.astype(BF).reshape(STEPS * ROWS, GL)
    out_ref[...] = dot(table_ref[0], rows).astype(BF).reshape(GY, 48, GL)


def to_lines(where, own, from_core, from_chip):
    piece = pl.BlockSpec((STEPS, ROWS, GL), lambda i, w: (0, 0, i))
    table = pl.BlockSpec((1, GY * 48, STEPS * ROWS), lambda i, w: (w[2], 0, 0))
    return pl.pallas_call(
        line_kernel,
        grid_spec=pltpu.PrefetchScalarGridSpec(
            num_scalar_prefetch=1,
            grid=(GROUPS,),
            in_specs=[piece] * 3 + [table],
            out_specs=pl.BlockSpec((GY, 48, GL), lambda i, w: (0, 0, i)),
        ),
        out_shape=jax.ShapeDtypeStruct((GY, 48, WIDE), BF),
        name="to_lines",
    )(where, own, from_core, from_chip, jnp.asarray(LINE))


def unline_kernel(where_ref, modes_ref, table_ref, out_ref):
    rows = modes_ref[...].reshape(GY * 48, GL)
    out_ref[...] = dot(table_ref[0], rows, 0, 0).astype(BF).reshape(STEPS, ROWS, GL)


def from_lines(where, modes):
    table = pl.BlockSpec((1, GY * 48, STEPS * ROWS), lambda i, w: (w[2], 0, 0))
    return pl.pallas_call(
        unline_kernel,
        grid_spec=pltpu.PrefetchScalarGridSpec(
            num_scalar_prefetch=1,
            grid=(GROUPS,),
            in_specs=[pl.BlockSpec((GY, 48, GL), lambda i, w: (0, 0, i)), table],
            out_specs=pl.BlockSpec((STEPS, ROWS, GL), lambda i, w: (0, 0, i)),
        ),
        out_shape=COEFFS,
        name="from_lines",
    )(where, modes, jnp.asarray(LINE))


SETS = GX * KB
PAIR = 2 * CH
HALF = KX


def low_lanes():
    return lax.broadcasted_iota(jnp.int32, (SETS, 2 * HALF), 1) < HALF


def gather_modes(arrived_ref, sum_ref, modes_ref, scale=None):
    total = arrived_ref[0].astype(F32)
    for i in range(1, GY):
        total = total + arrived_ref[i].astype(F32)
    sum_ref[...] = total.astype(BF).astype(F32)
    low = low_lanes()
    for j in range(CH // 2):
        lanes = slice(2 * HALF * j, 2 * HALF * (j + 1))
        for part in range(2):
            first = sum_ref[part * SETS : (part + 1) * SETS, lanes]
            second = sum_ref[(2 + part) * SETS : (3 + part) * SETS, lanes]
            if scale is not None:
                first = first * scale
                second = second * scale
            even = jnp.where(low, first, pltpu.roll(second, HALF, 1))
            odd = jnp.where(low, pltpu.roll(first, HALF, 1), second)
            modes_ref[pl.ds(4 * j + part, SETS, stride=PAIR), :] = even
            modes_ref[pl.ds(4 * j + 2 + part, SETS, stride=PAIR), :] = odd


def spread_modes(modes_ref, sum_ref, out_ref, scale=None):
    low = low_lanes()
    for j in range(CH // 2):
        lanes = slice(2 * HALF * j, 2 * HALF * (j + 1))
        for part in range(2):
            even = modes_ref[pl.ds(4 * j + part, SETS, stride=PAIR), :]
            odd = modes_ref[pl.ds(4 * j + 2 + part, SETS, stride=PAIR), :]
            if scale is not None:
                even = even * scale
                odd = odd * scale
            sum_ref[part * SETS : (part + 1) * SETS, lanes] = jnp.where(
                low, even, pltpu.roll(odd, HALF, 1)
            )
            sum_ref[(2 + part) * SETS : (3 + part) * SETS, lanes] = jnp.where(
                low, pltpu.roll(even, HALF, 1), odd
            )
    out_ref[...] = sum_ref[...].astype(BF)


def fold_scale(where_ref):
    kz = where_ref[1] * KB + lax.broadcasted_iota(jnp.int32, (SETS, 2 * HALF), 0) % KB
    return jnp.where(kz == 0, 1.0, 2.0).astype(F32) / float(NX * NY * NZ)


def turned(rows):
    even = lax.broadcasted_iota(jnp.int32, rows.shape, 0) % 2 == 0
    up = pltpu.roll(rows, PAIR - 1, 0)
    down = pltpu.roll(rows, 1, 0)
    return jnp.where(even, -up, down)


def hand_out(where_ref, modes_ref, outs):
    for k in range(DP):
        chunk = lax.rem(where_ref[0] + k, DP)
        start = pl.multiple_of(chunk * KB * PAIR, 8)
        outs[k][...] = modes_ref[pl.ds(start, KB * PAIR), :].astype(BF)


def mix_kernel(where_ref, arrived_ref, weight_ref, out_ref, u0, u1, u2, u3, sum_ref, in_ref, mix_ref):
    step = pl.program_id(0)

    @pl.when(step == 0)
    def _():
        gather_modes(arrived_ref, sum_ref, in_ref)
        hand_out(where_ref, in_ref, (u0, u1, u2, u3))

    @pl.loop(0, KB)
    def _(i):
        base = pl.multiple_of((step * KB + i) * PAIR, 8)
        by_real = jnp.zeros((PAIR, 2 * HALF), F32)
        by_imag = jnp.zeros((PAIR, 2 * HALF), F32)
        for c in range(CH):
            weight = weight_ref[i, c].astype(F32)
            by_real = by_real + weight * in_ref[pl.ds(base + 2 * c, 1), :]
            by_imag = by_imag + weight * in_ref[pl.ds(base + 2 * c + 1, 1), :]
        mix_ref[pl.ds(base, PAIR), :] = (by_real + turned(by_imag)).astype(BF).astype(F32)

    @pl.when(step == DP - 1)
    def _():
        spread_modes(mix_ref, sum_ref, out_ref, fold_scale(where_ref))


def back_kernel(where_ref, arrived_ref, weight_ref, out_ref, u0, u1, u2, u3, sum_ref, in_ref, mix_ref):
    step = pl.program_id(0)

    @pl.when(step == 0)
    def _():
        gather_modes(arrived_ref, sum_ref, in_ref, fold_scale(where_ref))
        hand_out(where_ref, in_ref, (u0, u1, u2, u3))

    @pl.loop(0, KB)
    def _(i):
        base = pl.multiple_of((step * KB + i) * PAIR, 8)
        grad = in_ref[pl.ds(base, PAIR), :]
        other = -turned(grad)
        for c in range(CH):
            weight = weight_ref[i, c].astype(F32)
            mix_ref[pl.ds(base + 2 * c, 1), :] = jnp.sum(weight * grad, axis=0, keepdims=True)
            mix_ref[pl.ds(base + 2 * c + 1, 1), :] = jnp.sum(weight * other, axis=0, keepdims=True)

    @pl.when(step == DP - 1)
    def _():
        spread_modes(mix_ref, sum_ref, out_ref)


def mode_call(kernel, name, where, arrived, weight):
    chunk = pl.BlockSpec((KB * PAIR, 2 * HALF), lambda i, w: (0, 0))
    return pl.pallas_call(
        kernel,
        grid_spec=pltpu.PrefetchScalarGridSpec(
            num_scalar_prefetch=1,
            grid=(DP,),
            in_specs=[
                pl.BlockSpec((GY, 48, WIDE), lambda i, w: (0, 0, 0)),
                pl.BlockSpec((KB, CH, PAIR, 2 * HALF), lambda i, w: (i, 0, 0, 0)),
            ],
            out_specs=[pl.BlockSpec((48, WIDE), lambda i, w: (0, 0))] + [chunk] * 4,
            scratch_shapes=[
                pltpu.VMEM((48, WIDE), F32),
                pltpu.VMEM((SETS * PAIR, 2 * HALF), F32),
                pltpu.VMEM((SETS * PAIR, 2 * HALF), F32),
            ],
        ),
        out_shape=[jax.ShapeDtypeStruct((48, WIDE), BF)]
        + [jax.ShapeDtypeStruct((KB * PAIR, 2 * HALF), BF)] * 4,
        name=name,
    )(where, arrived, weight)


def outer_kernel(s0, s1, s2, s3, g0, g1, g2, g3, out_ref, spec_ref):
    for k, ref in enumerate((s0, s1, s2, s3)):
        spec_ref[k] = ref[...].astype(F32)
    for i in range(KB):
        grads = []
        others = []
        for ref in (g0, g1, g2, g3):
            grad = ref[...].astype(F32)[i * PAIR : (i + 1) * PAIR]
            grads.append(grad)
            others.append(-turned(grad))

        @pl.loop(0, CH)
        def _(c):
            row = i * PAIR + 2 * c
            total = jnp.zeros((PAIR, 2 * HALF), F32)
            for k in range(DP):
                total = total + spec_ref[k, pl.ds(row, 1), :] * grads[k]
                total = total + spec_ref[k, pl.ds(row + 1, 1), :] * others[k]
            out_ref[i, c] = total


def outer_sum(spectra, grads):
    return pl.pallas_call(
        outer_kernel,
        out_shape=jax.ShapeDtypeStruct((KB, CH, PAIR, 2 * HALF), F32),
        scratch_shapes=[pltpu.VMEM((DP, KB * PAIR, 2 * HALF), F32)],
        name="outer_sum",
    )(*spectra, *grads)


def swap(values, bit):
    return lax.ppermute(values, "gx", [(i, i ^ bit) for i in range(GX)])


def reduce_slabs(where, pieces):
    own, far, near, across = pieces
    far_sum = (far.astype(F32) + swap(across, 1).astype(F32)).astype(BF)
    return to_lines(where, own, swap(near, 1), swap(far_sum, 2))


def share_slabs(own):
    far = swap(own, 2)
    return own, far, swap(own, 1), swap(far, 1)


def exchange_lines(parts):
    return lax.all_to_all(parts, "gy", split_axis=0, concat_axis=0, tiled=True)


def to_owners(chunks):
    moved = []
    for k, chunk in enumerate(chunks):
        pairs = [
            (a * GX + b, b * GX + (a + k) % DP) for a in range(DP) for b in range(GX)
        ]
        moved.append(lax.ppermute(chunk, ("dp", "gx"), pairs))
    return moved


def per_device(field, spectral_weight, bypass_weight, bias, cotangent):
    where = jnp.stack(
        [lax.axis_index("dp"), lax.axis_index("gx"), lax.axis_index("gy")]
    ).astype(jnp.int32)
    turn = [(a * GX + b, b * GX + a) for a in range(DP) for b in range(GX)]
    weight = lax.ppermute(spectral_weight, ("dp", "gx"), turn)
    weight = lax.all_gather(weight, "dp", axis=0, tiled=True)
    weight = weight.reshape(KZ, CH, PAIR, 2 * HALF)
    spread = jnp.asarray(SPREAD)

    def mixer_of(matrix):
        wide = dot(dot(spread, matrix).astype(BF), spread, 1, 1)
        return wide.astype(BF) * jnp.asarray(SAME)

    values = field[0]
    lines = reduce_slabs(where, start_columns(where, values))
    mode_out, *spectra = mode_call(mix_kernel, "mix_modes", where, exchange_lines(lines), weight)
    coeffs = share_slabs(from_lines(where, lax.all_gather(mode_out, "gy", axis=0)))
    spectra = to_owners(spectra)
    activation, grad, *pieces = middle_columns(
        where, bias, coeffs, values, cotangent[0], mixer_of(bypass_weight)
    )
    lines = reduce_slabs(where, pieces)
    mode_back, *grads = mode_call(back_kernel, "back_modes", where, exchange_lines(lines), weight)
    coeffs = share_slabs(from_lines(where, lax.all_gather(mode_back, "gy", axis=0)))
    weight_grad = outer_sum(spectra, to_owners(grads))
    field_grad = end_columns(where, coeffs, grad, mixer_of(bypass_weight.T))
    return (
        activation[None],
        field_grad[None],
        weight_grad.reshape(KB, CH, CH, 2, 2 * HALF),
    )


def solution(mesh):
    placed = (
        P("dp", None, "gx", "gy"),
        P("dp", None, None, None, ("gx", "gy")),
        P(),
        P(),
        P("dp", None, "gx", "gy"),
    )
    return jax.shard_map(
        per_device,
        mesh=mesh,
        in_specs=placed,
        out_specs=(
            P("dp", None, "gx", "gy"),
            P("dp", None, "gx", "gy"),
            P("dp", None, None, None, ("gx", "gy")),
        ),
        check_vma=False,
    )
```

```python
import functools
import math

import jax
import jax.numpy as jnp
import ml_dtypes
import numpy as np
from jax import lax
from jax.experimental import pallas as pl
from jax.experimental.pallas import tpu as pltpu
from jax.sharding import PartitionSpec as P

CH = 20
NX = 256
NY = 256
NZ = 64
KX = 64
KY = 64
KZ = 12
GX = 4
GY = 8
DP = 4
XL = NX // GX
YL = NY // GY
YB = 8
STEPS = YL // YB
LANES = YB * NZ
KB = KZ // GX
ROWS = 2 * KB * YB
GROUP = 4
GROUPS = CH // GROUP
GL = GROUP * KX
WIDE = CH * KX
XB = 16
ORDER = (0, 2, 1, 3)

BF = jnp.bfloat16
F32 = jnp.float32


def wave(freqs, points, length):
    offsets = np.mod(freqs[:, None] * points[None, :], length)
    angle = offsets.astype(np.float32) * np.float32(2.0 * math.pi / length)
    return np.cos(angle), np.sin(angle)


def kept(count):
    index = np.arange(count)
    return np.where(index < count // 2, index, index - count)


def depth_tables():
    out = np.zeros((GX, 2, GX, KB, YB, YB, NZ), np.float32)
    for b in range(GX):
        for pos, delta in enumerate(ORDER):
            freqs = (b ^ delta) * KB + np.arange(KB)
            cosine, sine = wave(freqs, np.arange(NZ), NZ)
            for y in range(YB):
                out[b, 0, pos, :, y, y] = cosine
                out[b, 1, pos, :, y, y] = -sine
    return out.reshape(GX, 2 * KZ * YB, LANES).astype(ml_dtypes.bfloat16)


def width_tables():
    out = np.zeros((GX, 2, XL, GL), np.float32)
    for b in range(GX):
        cosine, sine = wave(kept(KX), b * XL + np.arange(XL), NX)
        out[b, 0] = np.tile(cosine.T, (1, GROUP))
        out[b, 1] = np.tile(sine.T, (1, GROUP))
    return out.astype(ml_dtypes.bfloat16)


def line_tables():
    out = np.zeros((GY, GY, 2, 2, GX, KB, STEPS, 2, KB, YB), np.float32)
    fy = kept(KY)
    for g in range(GY):
        cosine, sine = wave(fy, g * YL + np.arange(YL), NY)
        cosine = cosine.reshape(GX, GY, 2, STEPS, YB)
        sine = sine.reshape(GX, GY, 2, STEPS, YB)
        for i in range(KB):
            for owner in range(GY):
                for q in range(2):
                    c = cosine[:, owner, q]
                    s = sine[:, owner, q]
                    out[g, owner, q, 0, :, i, :, 0, i] = c
                    out[g, owner, q, 0, :, i, :, 1, i] = s
                    out[g, owner, q, 1, :, i, :, 0, i] = -s
                    out[g, owner, q, 1, :, i, :, 1, i] = c
    return out.reshape(GY, GY * 48, STEPS * ROWS).astype(ml_dtypes.bfloat16)


DEPTH = depth_tables()
WIDTH = width_tables()
LINE = line_tables()
SPREAD = np.kron(np.eye(CH), np.ones((XB, 1))).astype(ml_dtypes.bfloat16)
SAME = np.kron(np.ones((CH, CH)), np.eye(XB)).astype(ml_dtypes.bfloat16)


def dot(left, right, left_dim=1, right_dim=0):
    return lax.dot_general(
        left, right, (((left_dim,), (right_dim,)), ((), ())), preferred_element_type=F32
    )


def fill_width(wide_ref, blocks_ref):
    rows = lax.broadcasted_iota(jnp.int32, (GL, GL), 0) // XL
    columns = lax.broadcasted_iota(jnp.int32, (GL, GL), 1) // KX
    for part in range(2):
        strip = wide_ref[0, part].astype(F32)
        full = jnp.concatenate([strip] * GROUP, axis=0)
        blocks_ref[part] = jnp.where(rows == columns, full, 0.0).astype(BF)


def forward_columns(source_ref, depth_ref, blocks_ref, outs):
    half = KZ * YB
    for j in range(GROUPS):
        rows = source_ref[GROUP * j : GROUP * (j + 1)].reshape(GROUP * XL, LANES)
        planes = dot(depth_ref[0], rows, 1, 1).astype(BF)
        by_cos = dot(planes, blocks_ref[0])
        by_sin = dot(planes, blocks_ref[1])
        real = by_cos[:half] + by_sin[half:]
        imag = by_cos[half:] - by_sin[:half]
        for pos in range(GX):
            lo = pos * KB * YB
            piece = jnp.concatenate([real[lo : lo + KB * YB], imag[lo : lo + KB * YB]], axis=0)
            outs[pos][0, :, GL * j : GL * (j + 1)] = piece.astype(BF)


def inverse_columns(ins, depth_ref, blocks_ref, total_ref):
    half = KZ * YB
    part = KB * YB
    for j in range(GROUPS):
        pieces = [ref[0, :, GL * j : GL * (j + 1)].astype(F32) for ref in ins]
        stacked = jnp.concatenate(
            [piece[:part] for piece in pieces] + [piece[part:] for piece in pieces], axis=0
        ).astype(BF)
        by_cos = dot(stacked, blocks_ref[0], 1, 1)
        by_sin = dot(stacked, blocks_ref[1], 1, 1)
        real = by_cos[:half] - by_sin[half:]
        imag = by_sin[:half] + by_cos[half:]
        planes = jnp.concatenate([real, imag], axis=0).astype(BF)
        values = dot(planes, depth_ref[0], 0, 0)
        total_ref[GROUP * j : GROUP * (j + 1)] = values.reshape(GROUP, XL, LANES)


def add_bypass(source_ref, mixer_ref, total_ref):
    @pl.loop(0, XL // XB)
    def _(i):
        span = pl.ds(pl.multiple_of(i * XB, XB), XB)
        rows = source_ref[:, span, :].reshape(CH * XB, LANES)
        mixed = dot(mixer_ref[...], rows).reshape(CH, XB, LANES)
        total_ref[:, span, :] = total_ref[:, span, :] + mixed


def start_kernel(where_ref, field_ref, depth_ref, wide_ref, o0, o1, o2, o3, blocks_ref):
    @pl.when(pl.program_id(0) == 0)
    def _():
        fill_width(wide_ref, blocks_ref)

    forward_columns(field_ref, depth_ref, blocks_ref, (o0, o1, o2, o3))


ROOT = math.sqrt(2.0 / math.pi)
CUBE = 0.044715


def middle_kernel(
    where_ref, bias_ref, i0, i1, i2, i3, field_ref, upstream_ref, mixer_ref, depth_ref, wide_ref,
    act_ref, grad_ref, o0, o1, o2, o3, blocks_ref, total_ref,
):
    @pl.when(pl.program_id(0) == 0)
    def _():
        fill_width(wide_ref, blocks_ref)

    inverse_columns((i0, i1, i2, i3), depth_ref, blocks_ref, total_ref)
    add_bypass(field_ref, mixer_ref, total_ref)

    @pl.loop(0, CH)
    def _(channel):
        shift = bias_ref[channel]
        for i in range(XL // XB):
            span = slice(i * XB, (i + 1) * XB)
            x = total_ref[channel, span, :] + shift
            square = x * x
            t = jnp.tanh(x * (ROOT + (ROOT * CUBE) * square))
            h = 0.5 * t + 0.5
            act = x * h
            slope = h + act * (1.0 - h) * (2.0 * ROOT + (6.0 * ROOT * CUBE) * square)
            act_ref[channel, span, :] = act.astype(BF)
            up = upstream_ref[channel, span, :].astype(F32)
            grad_ref[channel, span, :] = (up * slope).astype(BF)

    forward_columns(grad_ref, depth_ref, blocks_ref, (o0, o1, o2, o3))


def end_kernel(
    where_ref, i0, i1, i2, i3, grad_ref, mixer_ref, depth_ref, wide_ref, out_ref,
    blocks_ref, total_ref,
):
    @pl.when(pl.program_id(0) == 0)
    def _():
        fill_width(wide_ref, blocks_ref)

    inverse_columns((i0, i1, i2, i3), depth_ref, blocks_ref, total_ref)
    add_bypass(grad_ref, mixer_ref, total_ref)

    @pl.loop(0, CH)
    def _(channel):
        out_ref[channel] = total_ref[channel].astype(BF)


def column_specs():
    columns = pl.BlockSpec((CH, XL, LANES), lambda i, w: (0, 0, i))
    coeffs = pl.BlockSpec((1, ROWS, WIDE), lambda i, w: (i, 0, 0))
    depth = pl.BlockSpec((1, 2 * KZ * YB, LANES), lambda i, w: (w[1], 0, 0))
    wide = pl.BlockSpec((1, 2, XL, GL), lambda i, w: (w[1], 0, 0, 0))
    mixer = pl.BlockSpec((CH * XB, CH * XB), lambda i, w: (0, 0))
    return columns, coeffs, depth, wide, mixer


COEFFS = jax.ShapeDtypeStruct((STEPS, ROWS, WIDE), BF)
COLUMNS = jax.ShapeDtypeStruct((CH, XL, YL * NZ), BF)
BLOCKS = pltpu.VMEM((2, GL, GL), BF)
TOTAL = pltpu.VMEM((CH, XL, LANES), F32)
PARAMS = pltpu.CompilerParams(vmem_limit_bytes=56 * 1024 * 1024)


def start_columns(where, field):
    columns, coeffs, depth, wide, _ = column_specs()
    return pl.pallas_call(
        start_kernel,
        grid_spec=pltpu.PrefetchScalarGridSpec(
            num_scalar_prefetch=1,
            grid=(STEPS,),
            in_specs=[columns, depth, wide],
            out_specs=[coeffs] * 4,
            scratch_shapes=[BLOCKS],
        ),
        out_shape=[COEFFS] * 4,
        compiler_params=PARAMS,
        name="start_columns",
    )(where, field, jnp.asarray(DEPTH), jnp.asarray(WIDTH))


def middle_columns(where, bias, coeffs_in, field, upstream, mixer):
    columns, coeffs, depth, wide, mix = column_specs()
    return pl.pallas_call(
        middle_kernel,
        grid_spec=pltpu.PrefetchScalarGridSpec(
            num_scalar_prefetch=1,
            grid=(STEPS,),
            in_specs=[pl.BlockSpec(memory_space=pltpu.SMEM)]
            + [coeffs] * 4
            + [columns, columns, mix, depth, wide],
            out_specs=[columns, columns] + [coeffs] * 4,
            scratch_shapes=[BLOCKS, TOTAL],
        ),
        out_shape=[COLUMNS, COLUMNS] + [COEFFS] * 4,
        compiler_params=PARAMS,
        name="middle_columns",
    )(where, bias, *coeffs_in, field, upstream, mixer, jnp.asarray(DEPTH), jnp.asarray(WIDTH))


def end_columns(where, coeffs_in, grad, mixer):
    columns, coeffs, depth, wide, mix = column_specs()
    return pl.pallas_call(
        end_kernel,
        grid_spec=pltpu.PrefetchScalarGridSpec(
            num_scalar_prefetch=1,
            grid=(STEPS,),
            in_specs=[coeffs] * 4 + [columns, mix, depth, wide],
            out_specs=columns,
            scratch_shapes=[BLOCKS, TOTAL],
        ),
        out_shape=COLUMNS,
        compiler_params=PARAMS,
        name="end_columns",
    )(where, *coeffs_in, grad, mixer, jnp.asarray(DEPTH), jnp.asarray(WIDTH))


def line_kernel(where_ref, a_ref, b_ref, c_ref, table_ref, out_ref):
    total = a_ref[...].astype(F32) + b_ref[...].astype(F32) + c_ref[...].astype(F32)
    rows = total.astype(BF).reshape(STEPS * ROWS, GL)
    out_ref[...] = dot(table_ref[0], rows).astype(BF).reshape(GY, 48, GL)


def to_lines(where, own, from_core, from_chip):
    piece = pl.BlockSpec((STEPS, ROWS, GL), lambda i, w: (0, 0, i))
    table = pl.BlockSpec((1, GY * 48, STEPS * ROWS), lambda i, w: (w[2], 0, 0))
    return pl.pallas_call(
        line_kernel,
        grid_spec=pltpu.PrefetchScalarGridSpec(
            num_scalar_prefetch=1,
            grid=(GROUPS,),
            in_specs=[piece] * 3 + [table],
            out_specs=pl.BlockSpec((GY, 48, GL), lambda i, w: (0, 0, i)),
        ),
        out_shape=jax.ShapeDtypeStruct((GY, 48, WIDE), BF),
        name="to_lines",
    )(where, own, from_core, from_chip, jnp.asarray(LINE))


def unline_kernel(where_ref, modes_ref, table_ref, out_ref):
    rows = modes_ref[...].reshape(GY * 48, GL)
    out_ref[...] = dot(table_ref[0], rows, 0, 0).astype(BF).reshape(STEPS, ROWS, GL)


def from_lines(where, modes):
    table = pl.BlockSpec((1, GY * 48, STEPS * ROWS), lambda i, w: (w[2], 0, 0))
    return pl.pallas_call(
        unline_kernel,
        grid_spec=pltpu.PrefetchScalarGridSpec(
            num_scalar_prefetch=1,
            grid=(GROUPS,),
            in_specs=[pl.BlockSpec((GY, 48, GL), lambda i, w: (0, 0, i)), table],
            out_specs=pl.BlockSpec((STEPS, ROWS, GL), lambda i, w: (0, 0, i)),
        ),
        out_shape=COEFFS,
        name="from_lines",
    )(where, modes, jnp.asarray(LINE))


SETS = GX * KB
PAIR = 2 * CH
HALF = KX


def low_lanes():
    return lax.broadcasted_iota(jnp.int32, (SETS, 2 * HALF), 1) < HALF


def gather_modes(arrived_ref, sum_ref, modes_ref, scale=None):
    total = arrived_ref[0].astype(F32)
    for i in range(1, GY):
        total = total + arrived_ref[i].astype(F32)
    sum_ref[...] = total.astype(BF).astype(F32)
    low = low_lanes()
    for j in range(CH // 2):
        lanes = slice(2 * HALF * j, 2 * HALF * (j + 1))
        for part in range(2):
            first = sum_ref[part * SETS : (part + 1) * SETS, lanes]
            second = sum_ref[(2 + part) * SETS : (3 + part) * SETS, lanes]
            if scale is not None:
                first = first * scale
                second = second * scale
            even = jnp.where(low, first, pltpu.roll(second, HALF, 1))
            odd = jnp.where(low, pltpu.roll(first, HALF, 1), second)
            modes_ref[pl.ds(4 * j + part, SETS, stride=PAIR), :] = even
            modes_ref[pl.ds(4 * j + 2 + part, SETS, stride=PAIR), :] = odd


def spread_modes(modes_ref, sum_ref, out_ref, scale=None):
    low = low_lanes()
    for j in range(CH // 2):
        lanes = slice(2 * HALF * j, 2 * HALF * (j + 1))
        for part in range(2):
            even = modes_ref[pl.ds(4 * j + part, SETS, stride=PAIR), :]
            odd = modes_ref[pl.ds(4 * j + 2 + part, SETS, stride=PAIR), :]
            if scale is not None:
                even = even * scale
                odd = odd * scale
            sum_ref[part * SETS : (part + 1) * SETS, lanes] = jnp.where(
                low, even, pltpu.roll(odd, HALF, 1)
            )
            sum_ref[(2 + part) * SETS : (3 + part) * SETS, lanes] = jnp.where(
                low, pltpu.roll(even, HALF, 1), odd
            )
    modes = sum_ref[...].astype(BF)
    for owner in range(GY):
        out_ref[owner] = modes


def fold_scale(where_ref):
    kz = where_ref[1] * KB + lax.broadcasted_iota(jnp.int32, (SETS, 2 * HALF), 0) % KB
    return jnp.where(kz == 0, 1.0, 2.0).astype(F32) / float(NX * NY * NZ)


def turned(rows):
    even = lax.broadcasted_iota(jnp.int32, rows.shape, 0) % 2 == 0
    up = pltpu.roll(rows, PAIR - 1, 0)
    down = pltpu.roll(rows, 1, 0)
    return jnp.where(even, -up, down)


def hand_out(where_ref, modes_ref, outs):
    for k in range(DP):
        chunk = lax.rem(where_ref[0] + k, DP)
        start = pl.multiple_of(chunk * KB * PAIR, 8)
        outs[k][...] = modes_ref[pl.ds(start, KB * PAIR), :].astype(BF)


def set_row(where_ref, k):
    block = lax.rem(where_ref[0] + k, DP) * KB + pl.program_id(0)
    return pl.multiple_of(block * PAIR, 8)


def mix_kernel(
    where_ref, arrived_ref, w0, w1, w2, w3, out_ref, u0, u1, u2, u3, sum_ref, in_ref, mix_ref
):
    step = pl.program_id(0)

    @pl.when(step == 0)
    def _():
        gather_modes(arrived_ref, sum_ref, in_ref)
        hand_out(where_ref, in_ref, (u0, u1, u2, u3))

    for k, weight_ref in enumerate((w0, w1, w2, w3)):
        base = set_row(where_ref, k)
        by_real = jnp.zeros((PAIR, 2 * HALF), F32)
        by_imag = jnp.zeros((PAIR, 2 * HALF), F32)
        for c in range(CH):
            weight = weight_ref[0, c].astype(F32)
            by_real = by_real + weight * in_ref[pl.ds(base + 2 * c, 1), :]
            by_imag = by_imag + weight * in_ref[pl.ds(base + 2 * c + 1, 1), :]
        mix_ref[pl.ds(base, PAIR), :] = (by_real + turned(by_imag)).astype(BF).astype(F32)

    @pl.when(step == KB - 1)
    def _():
        spread_modes(mix_ref, sum_ref, out_ref, fold_scale(where_ref))


def back_kernel(
    where_ref, arrived_ref, w0, w1, w2, w3, out_ref, u0, u1, u2, u3, sum_ref, in_ref, mix_ref
):
    step = pl.program_id(0)

    @pl.when(step == 0)
    def _():
        gather_modes(arrived_ref, sum_ref, in_ref, fold_scale(where_ref))
        hand_out(where_ref, in_ref, (u0, u1, u2, u3))

    for k, weight_ref in enumerate((w0, w1, w2, w3)):
        base = set_row(where_ref, k)
        grad = in_ref[pl.ds(base, PAIR), :]
        other = -turned(grad)
        for c in range(CH):
            weight = weight_ref[0, c].astype(F32)
            mix_ref[pl.ds(base + 2 * c, 1), :] = jnp.sum(weight * grad, axis=0, keepdims=True)
            mix_ref[pl.ds(base + 2 * c + 1, 1), :] = jnp.sum(weight * other, axis=0, keepdims=True)

    @pl.when(step == KB - 1)
    def _():
        spread_modes(mix_ref, sum_ref, out_ref)


def mode_call(kernel, name, where, arrived, weights):
    chunk = pl.BlockSpec((KB * PAIR, 2 * HALF), lambda i, w: (0, 0))
    return pl.pallas_call(
        kernel,
        grid_spec=pltpu.PrefetchScalarGridSpec(
            num_scalar_prefetch=1,
            grid=(KB,),
            in_specs=[pl.BlockSpec((GY, 48, WIDE), lambda i, w: (0, 0, 0))]
            + [pl.BlockSpec((1, CH, PAIR, 2 * HALF), lambda i, w: (i, 0, 0, 0))] * 4,
            out_specs=[pl.BlockSpec((GY, 48, WIDE), lambda i, w: (0, 0, 0))] + [chunk] * 4,
            scratch_shapes=[
                pltpu.VMEM((48, WIDE), F32),
                pltpu.VMEM((SETS * PAIR, 2 * HALF), F32),
                pltpu.VMEM((SETS * PAIR, 2 * HALF), F32),
            ],
        ),
        out_shape=[jax.ShapeDtypeStruct((GY, 48, WIDE), BF)]
        + [jax.ShapeDtypeStruct((KB * PAIR, 2 * HALF), BF)] * 4,
        name=name,
    )(where, arrived, *weights)


def outer_kernel(s0, s1, s2, s3, g0, g1, g2, g3, out_ref, spec_ref):
    for k, ref in enumerate((s0, s1, s2, s3)):
        spec_ref[k] = ref[...].astype(F32)
    for i in range(KB):
        grads = []
        others = []
        for ref in (g0, g1, g2, g3):
            grad = ref[...].astype(F32)[i * PAIR : (i + 1) * PAIR]
            grads.append(grad)
            others.append(-turned(grad))

        @pl.loop(0, CH)
        def _(c):
            row = i * PAIR + 2 * c
            total = jnp.zeros((PAIR, 2 * HALF), F32)
            for k in range(DP):
                total = total + spec_ref[k, pl.ds(row, 1), :] * grads[k]
                total = total + spec_ref[k, pl.ds(row + 1, 1), :] * others[k]
            out_ref[i, c] = total


def outer_sum(spectra, grads):
    return pl.pallas_call(
        outer_kernel,
        out_shape=jax.ShapeDtypeStruct((KB, CH, PAIR, 2 * HALF), F32),
        scratch_shapes=[pltpu.VMEM((DP, KB * PAIR, 2 * HALF), F32)],
        name="outer_sum",
    )(*spectra, *grads)


def swap(values, bit):
    return lax.ppermute(values, "gx", [(i, i ^ bit) for i in range(GX)])


def start_slabs(pieces):
    own, far, near, across = pieces
    far_sum = (far.astype(F32) + swap(across, 1).astype(F32)).astype(BF)
    return own, swap(near, 1), swap(far_sum, 2)


def gather_weights(weight):
    held = [weight]
    for k in range(1, DP):
        held.append(lax.ppermute(weight, "dp", [((a + k) % DP, a) for a in range(DP)]))
    return [part.reshape(KB, CH, PAIR, 2 * HALF) for part in held]


def share_slabs(own):
    far = swap(own, 2)
    return own, far, swap(own, 1), swap(far, 1)


def exchange_lines(parts):
    return lax.all_to_all(parts, "gy", split_axis=0, concat_axis=0, tiled=True)


def to_owners(chunks):
    moved = []
    for k, chunk in enumerate(chunks):
        pairs = [
            (a * GX + b, b * GX + (a + k) % DP) for a in range(DP) for b in range(GX)
        ]
        moved.append(lax.ppermute(chunk, ("dp", "gx"), pairs))
    return moved


def per_device(field, spectral_weight, bypass_weight, bias, cotangent):
    where = jnp.stack(
        [lax.axis_index("dp"), lax.axis_index("gx"), lax.axis_index("gy")]
    ).astype(jnp.int32)
    turn = [(a * GX + b, b * GX + a) for a in range(DP) for b in range(GX)]
    weight = lax.ppermute(spectral_weight, ("dp", "gx"), turn)
    spread = jnp.asarray(SPREAD)

    def mixer_of(matrix):
        wide = dot(dot(spread, matrix).astype(BF), spread, 1, 1)
        return wide.astype(BF) * jnp.asarray(SAME)

    values = field[0]
    own, *others = start_slabs(start_columns(where, values))
    weight, *others = lax.optimization_barrier((weight, *others))
    weights = gather_weights(weight)
    arrived = exchange_lines(to_lines(where, own, *others))
    modes, *spectra = mode_call(mix_kernel, "mix_modes", where, arrived, weights)
    modes, *spectra = lax.optimization_barrier((exchange_lines(modes), *to_owners(spectra)))
    coeffs = share_slabs(from_lines(where, modes))
    activation, grad, *pieces = middle_columns(
        where, bias, coeffs, values, cotangent[0], mixer_of(bypass_weight)
    )
    arrived = exchange_lines(to_lines(where, *start_slabs(pieces)))
    modes, *grads = mode_call(back_kernel, "back_modes", where, arrived, weights)
    modes, *grads = lax.optimization_barrier((exchange_lines(modes), *to_owners(grads)))
    coeffs = share_slabs(from_lines(where, modes))
    weight_grad = outer_sum(spectra, grads)
    field_grad = end_columns(where, coeffs, grad, mixer_of(bypass_weight.T))
    return (
        activation[None],
        field_grad[None],
        weight_grad.reshape(KB, CH, CH, 2, 2 * HALF),
    )


def solution(mesh):
    placed = (
        P("dp", None, "gx", "gy"),
        P("dp", None, None, None, ("gx", "gy")),
        P(),
        P(),
        P("dp", None, "gx", "gy"),
    )
    return jax.shard_map(
        per_device,
        mesh=mesh,
        in_specs=placed,
        out_specs=(
            P("dp", None, "gx", "gy"),
            P("dp", None, "gx", "gy"),
            P("dp", None, None, None, ("gx", "gy")),
        ),
        check_vma=False,
    )
```

```python
import functools
import math

import jax
import jax.numpy as jnp
import ml_dtypes
import numpy as np
from jax import lax
from jax.experimental import pallas as pl
from jax.experimental.pallas import tpu as pltpu
from jax.sharding import PartitionSpec as P

CH = 20
NX = 256
NY = 256
NZ = 64
KX = 64
KY = 64
KZ = 12
GX = 4
GY = 8
DP = 4
XL = NX // GX
YL = NY // GY
YB = 8
STEPS = YL // YB
LANES = YB * NZ
KB = KZ // GX
ROWS = 2 * KB * YB
GROUP = 4
GROUPS = CH // GROUP
GL = GROUP * KX
WIDE = CH * KX
XB = 8
EB = 16
ORDER = (0, 2, 1, 3)

BF = jnp.bfloat16
F32 = jnp.float32


def wave(freqs, points, length):
    offsets = np.mod(freqs[:, None] * points[None, :], length)
    angle = offsets.astype(np.float32) * np.float32(2.0 * math.pi / length)
    return np.cos(angle), np.sin(angle)


def kept(count):
    index = np.arange(count)
    return np.where(index < count // 2, index, index - count)


def depth_tables():
    out = np.zeros((GX, 2, GX, KB, YB, YB, NZ), np.float32)
    for b in range(GX):
        for pos, delta in enumerate(ORDER):
            freqs = (b ^ delta) * KB + np.arange(KB)
            cosine, sine = wave(freqs, np.arange(NZ), NZ)
            for y in range(YB):
                out[b, 0, pos, :, y, y] = cosine
                out[b, 1, pos, :, y, y] = -sine
    return out.reshape(GX, 2 * KZ * YB, LANES).astype(ml_dtypes.bfloat16)


def width_tables():
    out = np.zeros((GX, 2, XL, GL), np.float32)
    for b in range(GX):
        cosine, sine = wave(kept(KX), b * XL + np.arange(XL), NX)
        out[b, 0] = np.tile(cosine.T, (1, GROUP))
        out[b, 1] = np.tile(sine.T, (1, GROUP))
    return out.astype(ml_dtypes.bfloat16)


def line_tables():
    out = np.zeros((GY, GY, 2, 2, GX, KB, STEPS, 2, KB, YB), np.float32)
    fy = kept(KY)
    for g in range(GY):
        cosine, sine = wave(fy, g * YL + np.arange(YL), NY)
        cosine = cosine.reshape(GX, GY, 2, STEPS, YB)
        sine = sine.reshape(GX, GY, 2, STEPS, YB)
        for i in range(KB):
            for owner in range(GY):
                for q in range(2):
                    c = cosine[:, owner, q]
                    s = sine[:, owner, q]
                    out[g, owner, q, 0, :, i, :, 0, i] = c
                    out[g, owner, q, 0, :, i, :, 1, i] = s
                    out[g, owner, q, 1, :, i, :, 0, i] = -s
                    out[g, owner, q, 1, :, i, :, 1, i] = c
    return out.reshape(GY, GY * 48, STEPS * ROWS).astype(ml_dtypes.bfloat16)


DEPTH = depth_tables()
WIDTH = width_tables()
LINE = line_tables()
SPREAD = np.kron(np.eye(CH), np.ones((XB, 1))).astype(ml_dtypes.bfloat16)
SAME = np.kron(np.ones((CH, CH)), np.eye(XB)).astype(ml_dtypes.bfloat16)


def dot(left, right, left_dim=1, right_dim=0):
    return lax.dot_general(
        left, right, (((left_dim,), (right_dim,)), ((), ())), preferred_element_type=F32
    )


def fill_width(wide_ref, tall_ref, long_ref):
    rows = lax.broadcasted_iota(jnp.int32, (GL, GL), 0) // XL
    columns = lax.broadcasted_iota(jnp.int32, (GL, GL), 1) // KX
    for part in range(2):
        strip = wide_ref[0, part].astype(F32)
        full = jnp.concatenate([strip] * GROUP, axis=0)
        block = jnp.where(rows == columns, full, 0.0).astype(BF)
        tall_ref[GL * part : GL * (part + 1), :] = block
        long_ref[:, GL * part : GL * (part + 1)] = block


def forward_group(rows, depth_ref, tall_ref, outs, j):
    half = KZ * YB
    planes = dot(depth_ref[0], rows, 1, 1)
    real = planes[:half]
    imag = planes[half:]
    sides = jnp.concatenate(
        [jnp.concatenate([real, imag], axis=1), jnp.concatenate([imag, -real], axis=1)], axis=0
    ).astype(BF)
    lines = dot(sides, tall_ref[...])
    for pos in range(GX):
        lo = pos * KB * YB
        piece = jnp.concatenate(
            [lines[lo : lo + KB * YB], lines[half + lo : half + lo + KB * YB]], axis=0
        )
        outs[pos][0, :, GL * j : GL * (j + 1)] = piece.astype(BF)


def inverse_group(ins, depth_ref, long_ref, j):
    part = KB * YB
    pieces = [ref[0, :, GL * j : GL * (j + 1)].astype(F32) for ref in ins]
    real = jnp.concatenate([piece[:part] for piece in pieces], axis=0)
    imag = jnp.concatenate([piece[part:] for piece in pieces], axis=0)
    sides = jnp.concatenate(
        [jnp.concatenate([real, -imag], axis=1), jnp.concatenate([imag, real], axis=1)], axis=0
    ).astype(BF)
    planes = dot(long_ref[...], sides, 1, 1).astype(BF)
    return dot(planes, depth_ref[0])


def set_bypass(source_ref, mixer_ref, total_ref):
    for i in range(XL // XB):
        span = slice(i * XB, (i + 1) * XB)
        rows = source_ref[:, span, :].reshape(CH * XB, LANES)
        total_ref[:, span, :] = dot(mixer_ref[...], rows).reshape(CH, XB, LANES)


def group_rows(ref, j):
    return ref[GROUP * j : GROUP * (j + 1)].reshape(GROUP * XL, LANES)


def start_kernel(where_ref, field_ref, depth_ref, wide_ref, o0, o1, o2, o3, tall_ref, long_ref):
    @pl.when(pl.program_id(0) == 0)
    def _():
        fill_width(wide_ref, tall_ref, long_ref)

    for j in range(GROUPS):
        forward_group(group_rows(field_ref, j), depth_ref, tall_ref, (o0, o1, o2, o3), j)


ROOT = math.sqrt(2.0 / math.pi)
CUBE = 0.044715


def activate(bias_ref, upstream_ref, total_ref, act_ref, grad_ref, j):
    for channel in range(GROUP * j, GROUP * (j + 1)):
        shift = bias_ref[channel]
        for i in range(XL // EB):
            span = slice(i * EB, (i + 1) * EB)
            x = total_ref[channel, span, :] + shift
            square = x * x
            t = jnp.tanh(x * (ROOT + (ROOT * CUBE) * square))
            h = 0.5 * t + 0.5
            act = x * h
            slope = h + act * (1.0 - h) * (2.0 * ROOT + (6.0 * ROOT * CUBE) * square)
            act_ref[channel, span, :] = act.astype(BF)
            up = upstream_ref[channel, span, :].astype(F32)
            grad_ref[channel, span, :] = (up * slope).astype(BF)


def middle_kernel(
    where_ref, bias_ref, i0, i1, i2, i3, field_ref, upstream_ref, mixer_ref, depth_ref, wide_ref,
    act_ref, grad_ref, o0, o1, o2, o3, tall_ref, long_ref, total_ref,
):
    @pl.when(pl.program_id(0) == 0)
    def _():
        fill_width(wide_ref, tall_ref, long_ref)

    set_bypass(field_ref, mixer_ref, total_ref)

    def inverse(j):
        group = slice(GROUP * j, GROUP * (j + 1))
        values = inverse_group((i0, i1, i2, i3), depth_ref, long_ref, j)
        total_ref[group] = total_ref[group] + values.reshape(GROUP, XL, LANES)

    def forward(j):
        forward_group(group_rows(grad_ref, j), depth_ref, tall_ref, (o0, o1, o2, o3), j)

    inverse(0)
    for j in range(GROUPS):
        if j + 1 < GROUPS:
            inverse(j + 1)
        activate(bias_ref, upstream_ref, total_ref, act_ref, grad_ref, j)
        if j > 0:
            forward(j - 1)
    forward(GROUPS - 1)


def end_kernel(
    where_ref, i0, i1, i2, i3, grad_ref, mixer_ref, depth_ref, wide_ref, out_ref,
    tall_ref, long_ref, total_ref,
):
    @pl.when(pl.program_id(0) == 0)
    def _():
        fill_width(wide_ref, tall_ref, long_ref)

    set_bypass(grad_ref, mixer_ref, total_ref)
    for j in range(GROUPS):
        group = slice(GROUP * j, GROUP * (j + 1))
        values = inverse_group((i0, i1, i2, i3), depth_ref, long_ref, j)
        out_ref[group] = (total_ref[group] + values.reshape(GROUP, XL, LANES)).astype(BF)


def column_specs():
    columns = pl.BlockSpec((CH, XL, LANES), lambda i, w: (0, 0, i))
    coeffs = pl.BlockSpec((1, ROWS, WIDE), lambda i, w: (i, 0, 0))
    depth = pl.BlockSpec((1, 2 * KZ * YB, LANES), lambda i, w: (w[1], 0, 0))
    wide = pl.BlockSpec((1, 2, XL, GL), lambda i, w: (w[1], 0, 0, 0))
    mixer = pl.BlockSpec((CH * XB, CH * XB), lambda i, w: (0, 0))
    return columns, coeffs, depth, wide, mixer


COEFFS = jax.ShapeDtypeStruct((STEPS, ROWS, WIDE), BF)
COLUMNS = jax.ShapeDtypeStruct((CH, XL, YL * NZ), BF)
BLOCKS = [pltpu.VMEM((2 * GL, GL), BF), pltpu.VMEM((GL, 2 * GL), BF)]
TOTAL = pltpu.VMEM((CH, XL, LANES), F32)
PARAMS = pltpu.CompilerParams(vmem_limit_bytes=56 * 1024 * 1024)


def start_columns(where, field):
    columns, coeffs, depth, wide, _ = column_specs()
    return pl.pallas_call(
        start_kernel,
        grid_spec=pltpu.PrefetchScalarGridSpec(
            num_scalar_prefetch=1,
            grid=(STEPS,),
            in_specs=[columns, depth, wide],
            out_specs=[coeffs] * 4,
            scratch_shapes=BLOCKS,
        ),
        out_shape=[COEFFS] * 4,
        compiler_params=PARAMS,
        name="start_columns",
    )(where, field, jnp.asarray(DEPTH), jnp.asarray(WIDTH))


def middle_columns(where, bias, coeffs_in, field, upstream, mixer):
    columns, coeffs, depth, wide, mix = column_specs()
    return pl.pallas_call(
        middle_kernel,
        grid_spec=pltpu.PrefetchScalarGridSpec(
            num_scalar_prefetch=1,
            grid=(STEPS,),
            in_specs=[pl.BlockSpec(memory_space=pltpu.SMEM)]
            + [coeffs] * 4
            + [columns, columns, mix, depth, wide],
            out_specs=[columns, columns] + [coeffs] * 4,
            scratch_shapes=BLOCKS + [TOTAL],
        ),
        out_shape=[COLUMNS, COLUMNS] + [COEFFS] * 4,
        compiler_params=PARAMS,
        name="middle_columns",
    )(where, bias, *coeffs_in, field, upstream, mixer, jnp.asarray(DEPTH), jnp.asarray(WIDTH))


def end_columns(where, coeffs_in, grad, mixer):
    columns, coeffs, depth, wide, mix = column_specs()
    return pl.pallas_call(
        end_kernel,
        grid_spec=pltpu.PrefetchScalarGridSpec(
            num_scalar_prefetch=1,
            grid=(STEPS,),
            in_specs=[coeffs] * 4 + [columns, mix, depth, wide],
            out_specs=columns,
            scratch_shapes=BLOCKS + [TOTAL],
        ),
        out_shape=COLUMNS,
        compiler_params=PARAMS,
        name="end_columns",
    )(where, *coeffs_in, grad, mixer, jnp.asarray(DEPTH), jnp.asarray(WIDTH))


def line_kernel(where_ref, a_ref, b_ref, c_ref, table_ref, out_ref):
    for j in range(GROUPS):
        lanes = slice(GL * j, GL * (j + 1))
        parts = [ref[:, :, lanes].astype(F32) for ref in (a_ref, b_ref, c_ref)]
        rows = (parts[0] + parts[1] + parts[2]).astype(BF).reshape(STEPS * ROWS, GL)
        out_ref[:, :, lanes] = dot(table_ref[0], rows).astype(BF).reshape(GY, 48, GL)


def unline_kernel(where_ref, modes_ref, table_ref, out_ref):
    for j in range(GROUPS):
        lanes = slice(GL * j, GL * (j + 1))
        rows = modes_ref[:, :, lanes].reshape(GY * 48, GL)
        out_ref[:, :, lanes] = dot(table_ref[0], rows, 0, 0).astype(BF).reshape(STEPS, ROWS, GL)


def line_call(kernel, name, where, ins, out_shape):
    whole = pl.BlockSpec(ins[0].shape, lambda i, w: (0, 0, 0))
    table = pl.BlockSpec((1, GY * 48, STEPS * ROWS), lambda i, w: (w[2], 0, 0))
    return pl.pallas_call(
        kernel,
        grid_spec=pltpu.PrefetchScalarGridSpec(
            num_scalar_prefetch=1,
            grid=(1,),
            in_specs=[whole] * len(ins) + [table],
            out_specs=pl.BlockSpec(out_shape.shape, lambda i, w: (0, 0, 0)),
        ),
        out_shape=out_shape,
        name=name,
    )(where, *ins, jnp.asarray(LINE))


def to_lines(where, *parts):
    out = jax.ShapeDtypeStruct((GY, 48, WIDE), BF)
    return line_call(line_kernel, "to_lines", where, parts, out)


def from_lines(where, modes):
    return line_call(unline_kernel, "from_lines", where, (modes,), COEFFS)


SETS = GX * KB
PAIR = 2 * CH
HALF = KX


def low_lanes():
    return lax.broadcasted_iota(jnp.int32, (SETS, 2 * HALF), 1) < HALF


def gather_modes(arrived_ref, sum_ref, modes_ref, scale=None):
    total = arrived_ref[0].astype(F32)
    for i in range(1, GY):
        total = total + arrived_ref[i].astype(F32)
    sum_ref[...] = total.astype(BF).astype(F32)
    low = low_lanes()
    for j in range(CH // 2):
        lanes = slice(2 * HALF * j, 2 * HALF * (j + 1))
        for part in range(2):
            first = sum_ref[part * SETS : (part + 1) * SETS, lanes]
            second = sum_ref[(2 + part) * SETS : (3 + part) * SETS, lanes]
            if scale is not None:
                first = first * scale
                second = second * scale
            even = jnp.where(low, first, pltpu.roll(second, HALF, 1))
            odd = jnp.where(low, pltpu.roll(first, HALF, 1), second)
            modes_ref[pl.ds(4 * j + part, SETS, stride=PAIR), :] = even
            modes_ref[pl.ds(4 * j + 2 + part, SETS, stride=PAIR), :] = odd


def spread_modes(modes_ref, sum_ref, out_ref, scale=None):
    low = low_lanes()
    for j in range(CH // 2):
        lanes = slice(2 * HALF * j, 2 * HALF * (j + 1))
        for part in range(2):
            even = modes_ref[pl.ds(4 * j + part, SETS, stride=PAIR), :]
            odd = modes_ref[pl.ds(4 * j + 2 + part, SETS, stride=PAIR), :]
            if scale is not None:
                even = even * scale
                odd = odd * scale
            sum_ref[part * SETS : (part + 1) * SETS, lanes] = jnp.where(
                low, even, pltpu.roll(odd, HALF, 1)
            )
            sum_ref[(2 + part) * SETS : (3 + part) * SETS, lanes] = jnp.where(
                low, pltpu.roll(even, HALF, 1), odd
            )
    modes = sum_ref[...].astype(BF)
    for owner in range(GY):
        out_ref[owner] = modes


def fold_scale(where_ref):
    kz = where_ref[1] * KB + lax.broadcasted_iota(jnp.int32, (SETS, 2 * HALF), 0) % KB
    return jnp.where(kz == 0, 1.0, 2.0).astype(F32) / float(NX * NY * NZ)


def turned(rows):
    even = lax.broadcasted_iota(jnp.int32, rows.shape, 0) % 2 == 0
    up = pltpu.roll(rows, PAIR - 1, 0)
    down = pltpu.roll(rows, 1, 0)
    return jnp.where(even, -up, down)


def hand_out(where_ref, modes_ref, outs):
    for k in range(DP):
        chunk = lax.rem(where_ref[0] + k, DP)
        start = pl.multiple_of(chunk * KB * PAIR, 8)
        outs[k][...] = modes_ref[pl.ds(start, KB * PAIR), :].astype(BF)


def set_row(where_ref, k):
    block = lax.rem(where_ref[0] + k, DP) * KB + pl.program_id(0)
    return pl.multiple_of(block * PAIR, 8)


def mix_kernel(
    where_ref, arrived_ref, w0, w1, w2, w3, out_ref, u0, u1, u2, u3, sum_ref, in_ref, mix_ref
):
    step = pl.program_id(0)

    @pl.when(step == 0)
    def _():
        gather_modes(arrived_ref, sum_ref, in_ref)
        hand_out(where_ref, in_ref, (u0, u1, u2, u3))

    for k, weight_ref in enumerate((w0, w1, w2, w3)):
        base = set_row(where_ref, k)
        by_real = jnp.zeros((PAIR, 2 * HALF), F32)
        by_imag = jnp.zeros((PAIR, 2 * HALF), F32)
        for c in range(CH):
            weight = weight_ref[0, c].astype(F32)
            by_real = by_real + weight * in_ref[pl.ds(base + 2 * c, 1), :]
            by_imag = by_imag + weight * in_ref[pl.ds(base + 2 * c + 1, 1), :]
        mix_ref[pl.ds(base, PAIR), :] = (by_real + turned(by_imag)).astype(BF).astype(F32)

    @pl.when(step == KB - 1)
    def _():
        spread_modes(mix_ref, sum_ref, out_ref, fold_scale(where_ref))


def back_kernel(
    where_ref, arrived_ref, w0, w1, w2, w3, out_ref, u0, u1, u2, u3, sum_ref, in_ref, mix_ref
):
    step = pl.program_id(0)

    @pl.when(step == 0)
    def _():
        gather_modes(arrived_ref, sum_ref, in_ref, fold_scale(where_ref))
        hand_out(where_ref, in_ref, (u0, u1, u2, u3))

    for k, weight_ref in enumerate((w0, w1, w2, w3)):
        base = set_row(where_ref, k)
        grad = in_ref[pl.ds(base, PAIR), :]
        other = -turned(grad)
        for c in range(CH):
            weight = weight_ref[0, c].astype(F32)
            mix_ref[pl.ds(base + 2 * c, 1), :] = jnp.sum(weight * grad, axis=0, keepdims=True)
            mix_ref[pl.ds(base + 2 * c + 1, 1), :] = jnp.sum(weight * other, axis=0, keepdims=True)

    @pl.when(step == KB - 1)
    def _():
        spread_modes(mix_ref, sum_ref, out_ref)


def mode_call(kernel, name, where, arrived, weights):
    chunk = pl.BlockSpec((KB * PAIR, 2 * HALF), lambda i, w: (0, 0))
    return pl.pallas_call(
        kernel,
        grid_spec=pltpu.PrefetchScalarGridSpec(
            num_scalar_prefetch=1,
            grid=(KB,),
            in_specs=[pl.BlockSpec((GY, 48, WIDE), lambda i, w: (0, 0, 0))]
            + [pl.BlockSpec((1, CH, PAIR, 2 * HALF), lambda i, w: (i, 0, 0, 0))] * 4,
            out_specs=[pl.BlockSpec((GY, 48, WIDE), lambda i, w: (0, 0, 0))] + [chunk] * 4,
            scratch_shapes=[
                pltpu.VMEM((48, WIDE), F32),
                pltpu.VMEM((SETS * PAIR, 2 * HALF), F32),
                pltpu.VMEM((SETS * PAIR, 2 * HALF), F32),
            ],
        ),
        out_shape=[jax.ShapeDtypeStruct((GY, 48, WIDE), BF)]
        + [jax.ShapeDtypeStruct((KB * PAIR, 2 * HALF), BF)] * 4,
        name=name,
    )(where, arrived, *weights)


def outer_kernel(s0, s1, s2, s3, g0, g1, g2, g3, out_ref, spec_ref):
    for k, ref in enumerate((s0, s1, s2, s3)):
        spec_ref[k] = ref[...].astype(F32)
    for i in range(KB):
        grads = []
        others = []
        for ref in (g0, g1, g2, g3):
            grad = ref[...].astype(F32)[i * PAIR : (i + 1) * PAIR]
            grads.append(grad)
            others.append(-turned(grad))

        @pl.loop(0, CH)
        def _(c):
            row = i * PAIR + 2 * c
            total = jnp.zeros((PAIR, 2 * HALF), F32)
            for k in range(DP):
                total = total + spec_ref[k, pl.ds(row, 1), :] * grads[k]
                total = total + spec_ref[k, pl.ds(row + 1, 1), :] * others[k]
            out_ref[i, c] = total


def outer_sum(spectra, grads):
    return pl.pallas_call(
        outer_kernel,
        out_shape=jax.ShapeDtypeStruct((KB, CH, PAIR, 2 * HALF), F32),
        scratch_shapes=[pltpu.VMEM((DP, KB * PAIR, 2 * HALF), F32)],
        name="outer_sum",
    )(*spectra, *grads)


def swap(values, bit):
    return lax.ppermute(values, "gx", [(i, i ^ bit) for i in range(GX)])


def start_slabs(pieces, *waiting):
    own, far, near, across = pieces
    far_sum = (far.astype(F32) + swap(across, 1).astype(F32)).astype(BF)
    far_sum, *waiting = lax.optimization_barrier((far_sum, *waiting))
    return own, swap(near, 1), swap(far_sum, 2), *waiting


def share_slabs(own, *waiting):
    far = swap(own, 2)
    far, *waiting = lax.optimization_barrier((far, *waiting))
    return own, far, swap(own, 1), swap(far, 1), *waiting


def gather_weights(weight):
    held = [weight]
    for k in range(1, DP):
        held.append(lax.ppermute(weight, "dp", [((a + k) % DP, a) for a in range(DP)]))
    return [part.reshape(KB, CH, PAIR, 2 * HALF) for part in held]


def exchange_lines(parts):
    return lax.all_to_all(parts, "gy", split_axis=0, concat_axis=0, tiled=True)


def to_owners(chunks):
    moved = []
    for k, chunk in enumerate(chunks):
        pairs = [
            (a * GX + b, b * GX + (a + k) % DP) for a in range(DP) for b in range(GX)
        ]
        moved.append(lax.ppermute(chunk, ("dp", "gx"), pairs))
    return moved


def per_device(field, spectral_weight, bypass_weight, bias, cotangent):
    where = jnp.stack(
        [lax.axis_index("dp"), lax.axis_index("gx"), lax.axis_index("gy")]
    ).astype(jnp.int32)
    turn = [(a * GX + b, b * GX + a) for a in range(DP) for b in range(GX)]
    weight = lax.ppermute(spectral_weight, ("dp", "gx"), turn)
    spread = jnp.asarray(SPREAD)

    def mixer_of(matrix):
        wide = dot(dot(spread, matrix).astype(BF), spread, 1, 1)
        return wide.astype(BF) * jnp.asarray(SAME)

    values = field[0]
    *parts, weight = start_slabs(start_columns(where, values), weight)
    weights = gather_weights(weight)
    arrived = exchange_lines(to_lines(where, *parts))
    modes, *spectra = mode_call(mix_kernel, "mix_modes", where, arrived, weights)
    modes, *spectra = lax.optimization_barrier((exchange_lines(modes), *to_owners(spectra)))
    coeffs = share_slabs(from_lines(where, modes))
    activation, grad, *pieces = middle_columns(
        where, bias, coeffs, values, cotangent[0], mixer_of(bypass_weight)
    )
    arrived = exchange_lines(to_lines(where, *start_slabs(pieces)))
    modes, *grads = mode_call(back_kernel, "back_modes", where, arrived, weights)
    modes, *grads = lax.optimization_barrier((exchange_lines(modes), *to_owners(grads)))
    *coeffs, weight_grad = share_slabs(from_lines(where, modes), outer_sum(spectra, grads))
    field_grad = end_columns(where, coeffs, grad, mixer_of(bypass_weight.T))
    return (
        activation[None],
        field_grad[None],
        weight_grad.reshape(KB, CH, CH, 2, 2 * HALF),
    )


def solution(mesh):
    placed = (
        P("dp", None, "gx", "gy"),
        P("dp", None, None, None, ("gx", "gy")),
        P(),
        P(),
        P("dp", None, "gx", "gy"),
    )
    return jax.shard_map(
        per_device,
        mesh=mesh,
        in_specs=placed,
        out_specs=(
            P("dp", None, "gx", "gy"),
            P("dp", None, "gx", "gy"),
            P("dp", None, None, None, ("gx", "gy")),
        ),
        check_vma=False,
    )
```

```python
import functools
import math

import jax
import jax.numpy as jnp
import ml_dtypes
import numpy as np
from jax import lax
from jax.experimental import pallas as pl
from jax.experimental.pallas import tpu as pltpu
from jax.sharding import PartitionSpec as P

CH = 20
NX = 256
NY = 256
NZ = 64
KX = 64
KY = 64
KZ = 12
GX = 4
GY = 8
DP = 4
XL = NX // GX
YL = NY // GY
YB = 8
STEPS = YL // YB
LANES = YB * NZ
KB = KZ // GX
ROWS = 2 * KB * YB
GROUP = 4
GROUPS = CH // GROUP
GL = GROUP * KX
WIDE = CH * KX
XB = 8
EB = 16
ORDER = (0, 2, 1, 3)

BF = jnp.bfloat16
F32 = jnp.float32


def wave(freqs, points, length):
    offsets = np.mod(freqs[:, None] * points[None, :], length)
    angle = offsets.astype(np.float32) * np.float32(2.0 * math.pi / length)
    return np.cos(angle), np.sin(angle)


def kept(count):
    index = np.arange(count)
    return np.where(index < count // 2, index, index - count)


def depth_tables():
    out = np.zeros((GX, 2, GX, KB, LANES), np.float32)
    for b in range(GX):
        for pos, delta in enumerate(ORDER):
            freqs = (b ^ delta) * KB + np.arange(KB)
            cosine, sine = wave(freqs, np.arange(NZ), NZ)
            out[b, 0, pos] = np.tile(cosine, (1, YB))
            out[b, 1, pos] = np.tile(-sine, (1, YB))
    return out.reshape(GX, 2 * KZ, LANES).astype(ml_dtypes.bfloat16)


def width_tables():
    out = np.zeros((GX, 2, XL, KX), np.float32)
    for b in range(GX):
        cosine, sine = wave(kept(KX), b * XL + np.arange(XL), NX)
        out[b, 0] = cosine.T
        out[b, 1] = sine.T
    return out.astype(ml_dtypes.bfloat16)


def line_tables():
    out = np.zeros((GY, GY, 2, 2, GX, KB, STEPS, 2, KB, YB), np.float32)
    fy = kept(KY)
    for g in range(GY):
        cosine, sine = wave(fy, g * YL + np.arange(YL), NY)
        cosine = cosine.reshape(GX, GY, 2, STEPS, YB)
        sine = sine.reshape(GX, GY, 2, STEPS, YB)
        for i in range(KB):
            for owner in range(GY):
                for q in range(2):
                    c = cosine[:, owner, q]
                    s = sine[:, owner, q]
                    out[g, owner, q, 0, :, i, :, 0, i] = c
                    out[g, owner, q, 0, :, i, :, 1, i] = s
                    out[g, owner, q, 1, :, i, :, 0, i] = -s
                    out[g, owner, q, 1, :, i, :, 1, i] = c
    return out.reshape(GY, GY * 48, STEPS * ROWS).astype(ml_dtypes.bfloat16)


DEPTH = depth_tables()
WIDTH = width_tables()
LINE = line_tables()
SPREAD = np.kron(np.eye(CH), np.ones((XB, 1))).astype(ml_dtypes.bfloat16)
SAME = np.kron(np.ones((CH, CH)), np.eye(XB)).astype(ml_dtypes.bfloat16)


def dot(left, right, left_dim=1, right_dim=0):
    return lax.dot_general(
        left, right, (((left_dim,), (right_dim,)), ((), ())), preferred_element_type=F32
    )


def fill_tables(strip_ref, wide_ref, depth_ref, tall_ref, long_ref):
    strips = jnp.broadcast_to(strip_ref[0].astype(F32)[:, None, :], (2 * KZ, YB, LANES))
    row = lax.broadcasted_iota(jnp.int32, (2 * KZ, YB, LANES), 1)
    column = lax.broadcasted_iota(jnp.int32, (2 * KZ, YB, LANES), 2) // NZ
    blocks = jnp.where(row == column, strips, 0.0)
    depth_ref[...] = blocks.reshape(2 * KZ * YB, LANES).astype(BF)
    rows = lax.broadcasted_iota(jnp.int32, (GL, GL), 0) // XL
    columns = lax.broadcasted_iota(jnp.int32, (GL, GL), 1) // KX
    for part in range(2):
        strip = wide_ref[0, part].astype(F32)
        full = jnp.concatenate([jnp.concatenate([strip] * GROUP, axis=1)] * GROUP, axis=0)
        block = jnp.where(rows == columns, full, 0.0).astype(BF)
        tall_ref[GL * part : GL * (part + 1), :] = block
        long_ref[:, GL * part : GL * (part + 1)] = block


def forward_group(rows, depth_ref, tall_ref, outs, j):
    half = KZ * YB
    planes = dot(depth_ref[...], rows, 1, 1)
    real = planes[:half]
    imag = planes[half:]
    sides = jnp.concatenate(
        [jnp.concatenate([real, imag], axis=1), jnp.concatenate([imag, -real], axis=1)], axis=0
    ).astype(BF)
    lines = dot(sides, tall_ref[...])
    for pos in range(GX):
        lo = pos * KB * YB
        piece = jnp.concatenate(
            [lines[lo : lo + KB * YB], lines[half + lo : half + lo + KB * YB]], axis=0
        )
        outs[pos][0, :, GL * j : GL * (j + 1)] = piece.astype(BF)


def inverse_group(ins, depth_ref, long_ref, j):
    part = KB * YB
    pieces = [ref[0, :, GL * j : GL * (j + 1)].astype(F32) for ref in ins]
    real = jnp.concatenate([piece[:part] for piece in pieces], axis=0)
    imag = jnp.concatenate([piece[part:] for piece in pieces], axis=0)
    sides = jnp.concatenate(
        [jnp.concatenate([real, -imag], axis=1), jnp.concatenate([imag, real], axis=1)], axis=0
    ).astype(BF)
    planes = dot(long_ref[...], sides, 1, 1).astype(BF)
    return dot(planes, depth_ref[...])


def set_bypass(source_ref, mixer_ref, total_ref):
    for i in range(XL // XB):
        span = slice(i * XB, (i + 1) * XB)
        rows = source_ref[:, span, :].reshape(CH * XB, LANES)
        total_ref[:, span, :] = dot(mixer_ref[...], rows).reshape(CH, XB, LANES)


def group_rows(ref, j):
    return ref[GROUP * j : GROUP * (j + 1)].reshape(GROUP * XL, LANES)


def start_kernel(
    where_ref, field_ref, strip_ref, wide_ref, o0, o1, o2, o3, depth_ref, tall_ref, long_ref
):
    @pl.when(pl.program_id(0) == 0)
    def _():
        fill_tables(strip_ref, wide_ref, depth_ref, tall_ref, long_ref)

    for j in range(GROUPS):
        forward_group(group_rows(field_ref, j), depth_ref, tall_ref, (o0, o1, o2, o3), j)


ROOT = math.sqrt(2.0 / math.pi)
CUBE = 0.044715


def activate(bias_ref, upstream_ref, total_ref, act_ref, grad_ref, j):
    for channel in range(GROUP * j, GROUP * (j + 1)):
        shift = bias_ref[channel]
        for i in range(XL // EB):
            span = slice(i * EB, (i + 1) * EB)
            x = total_ref[channel, span, :] + shift
            square = x * x
            t = jnp.tanh(x * (ROOT + (ROOT * CUBE) * square))
            h = 0.5 * t + 0.5
            act = x * h
            slope = h + act * (1.0 - h) * (2.0 * ROOT + (6.0 * ROOT * CUBE) * square)
            act_ref[channel, span, :] = act.astype(BF)
            up = upstream_ref[channel, span, :].astype(F32)
            grad_ref[channel, span, :] = (up * slope).astype(BF)


def middle_kernel(
    where_ref, bias_ref, i0, i1, i2, i3, field_ref, upstream_ref, mixer_ref, strip_ref, wide_ref,
    act_ref, grad_ref, o0, o1, o2, o3, depth_ref, tall_ref, long_ref, total_ref,
):
    @pl.when(pl.program_id(0) == 0)
    def _():
        fill_tables(strip_ref, wide_ref, depth_ref, tall_ref, long_ref)

    set_bypass(field_ref, mixer_ref, total_ref)

    def inverse(j):
        group = slice(GROUP * j, GROUP * (j + 1))
        values = inverse_group((i0, i1, i2, i3), depth_ref, long_ref, j)
        total_ref[group] = total_ref[group] + values.reshape(GROUP, XL, LANES)

    def forward(j):
        forward_group(group_rows(grad_ref, j), depth_ref, tall_ref, (o0, o1, o2, o3), j)

    inverse(0)
    for j in range(GROUPS):
        if j + 1 < GROUPS:
            inverse(j + 1)
        activate(bias_ref, upstream_ref, total_ref, act_ref, grad_ref, j)
        if j > 0:
            forward(j - 1)
    forward(GROUPS - 1)


def end_kernel(
    where_ref, i0, i1, i2, i3, grad_ref, mixer_ref, strip_ref, wide_ref, out_ref,
    depth_ref, tall_ref, long_ref, total_ref,
):
    @pl.when(pl.program_id(0) == 0)
    def _():
        fill_tables(strip_ref, wide_ref, depth_ref, tall_ref, long_ref)

    set_bypass(grad_ref, mixer_ref, total_ref)
    for j in range(GROUPS):
        group = slice(GROUP * j, GROUP * (j + 1))
        values = inverse_group((i0, i1, i2, i3), depth_ref, long_ref, j)
        out_ref[group] = (total_ref[group] + values.reshape(GROUP, XL, LANES)).astype(BF)


def cost(micros):
    return pl.CostEstimate(flops=0, bytes_accessed=micros * 3_000_000, transcendentals=0)


def column_specs():
    columns = pl.BlockSpec((CH, XL, LANES), lambda i, w: (0, 0, i))
    coeffs = pl.BlockSpec((1, ROWS, WIDE), lambda i, w: (i, 0, 0))
    depth = pl.BlockSpec((1, 2 * KZ, LANES), lambda i, w: (w[1], 0, 0))
    wide = pl.BlockSpec((1, 2, XL, KX), lambda i, w: (w[1], 0, 0, 0))
    mixer = pl.BlockSpec((CH * XB, CH * XB), lambda i, w: (0, 0))
    return columns, coeffs, depth, wide, mixer


COEFFS = jax.ShapeDtypeStruct((STEPS, ROWS, WIDE), BF)
COLUMNS = jax.ShapeDtypeStruct((CH, XL, YL * NZ), BF)
BLOCKS = [
    pltpu.VMEM((2 * KZ * YB, LANES), BF),
    pltpu.VMEM((2 * GL, GL), BF),
    pltpu.VMEM((GL, 2 * GL), BF),
]
TOTAL = pltpu.VMEM((CH, XL, LANES), F32)
PARAMS = pltpu.CompilerParams(vmem_limit_bytes=56 * 1024 * 1024)


def start_columns(where, field):
    columns, coeffs, depth, wide, _ = column_specs()
    return pl.pallas_call(
        start_kernel,
        grid_spec=pltpu.PrefetchScalarGridSpec(
            num_scalar_prefetch=1,
            grid=(STEPS,),
            in_specs=[columns, depth, wide],
            out_specs=[coeffs] * 4,
            scratch_shapes=BLOCKS,
        ),
        out_shape=[COEFFS] * 4,
        compiler_params=PARAMS,
        cost_estimate=cost(8),
        name="start_columns",
    )(where, field, jnp.asarray(DEPTH), jnp.asarray(WIDTH))


def middle_columns(where, bias, coeffs_in, field, upstream, mixer):
    columns, coeffs, depth, wide, mix = column_specs()
    return pl.pallas_call(
        middle_kernel,
        grid_spec=pltpu.PrefetchScalarGridSpec(
            num_scalar_prefetch=1,
            grid=(STEPS,),
            in_specs=[pl.BlockSpec(memory_space=pltpu.SMEM)]
            + [coeffs] * 4
            + [columns, columns, mix, depth, wide],
            out_specs=[columns, columns] + [coeffs] * 4,
            scratch_shapes=BLOCKS + [TOTAL],
        ),
        out_shape=[COLUMNS, COLUMNS] + [COEFFS] * 4,
        compiler_params=PARAMS,
        cost_estimate=cost(19),
        name="middle_columns",
    )(where, bias, *coeffs_in, field, upstream, mixer, jnp.asarray(DEPTH), jnp.asarray(WIDTH))


def end_columns(where, coeffs_in, grad, mixer):
    columns, coeffs, depth, wide, mix = column_specs()
    return pl.pallas_call(
        end_kernel,
        grid_spec=pltpu.PrefetchScalarGridSpec(
            num_scalar_prefetch=1,
            grid=(STEPS,),
            in_specs=[coeffs] * 4 + [columns, mix, depth, wide],
            out_specs=columns,
            scratch_shapes=BLOCKS + [TOTAL],
        ),
        out_shape=COLUMNS,
        compiler_params=PARAMS,
        cost_estimate=cost(10),
        name="end_columns",
    )(where, *coeffs_in, grad, mixer, jnp.asarray(DEPTH), jnp.asarray(WIDTH))


def line_kernel(where_ref, a_ref, b_ref, c_ref, table_ref, out_ref):
    for j in range(GROUPS):
        lanes = slice(GL * j, GL * (j + 1))
        parts = [ref[:, :, lanes].astype(F32) for ref in (a_ref, b_ref, c_ref)]
        rows = (parts[0] + parts[1] + parts[2]).astype(BF).reshape(STEPS * ROWS, GL)
        out_ref[:, :, lanes] = dot(table_ref[0], rows).astype(BF).reshape(GY, 48, GL)


def unline_kernel(where_ref, modes_ref, table_ref, out_ref):
    for j in range(GROUPS):
        lanes = slice(GL * j, GL * (j + 1))
        rows = modes_ref[:, :, lanes].reshape(GY * 48, GL)
        out_ref[:, :, lanes] = dot(table_ref[0], rows, 0, 0).astype(BF).reshape(STEPS, ROWS, GL)


def line_call(kernel, name, where, ins, out_shape):
    whole = pl.BlockSpec(ins[0].shape, lambda i, w: (0, 0, 0))
    table = pl.BlockSpec((1, GY * 48, STEPS * ROWS), lambda i, w: (w[2], 0, 0))
    return pl.pallas_call(
        kernel,
        grid_spec=pltpu.PrefetchScalarGridSpec(
            num_scalar_prefetch=1,
            grid=(1,),
            in_specs=[whole] * len(ins) + [table],
            out_specs=pl.BlockSpec(out_shape.shape, lambda i, w: (0, 0, 0)),
        ),
        out_shape=out_shape,
        cost_estimate=cost(3),
        name=name,
    )(where, *ins, jnp.asarray(LINE))


def to_lines(where, *parts):
    out = jax.ShapeDtypeStruct((GY, 48, WIDE), BF)
    return line_call(line_kernel, "to_lines", where, parts, out)


def from_lines(where, modes):
    return line_call(unline_kernel, "from_lines", where, (modes,), COEFFS)


UNROLL = 4
SETS = GX * KB
PAIR = 2 * CH
HALF = KX


def low_lanes():
    return lax.broadcasted_iota(jnp.int32, (SETS, 2 * HALF), 1) < HALF


def gather_modes(arrived_ref, sum_ref, modes_ref, scale=None):
    total = arrived_ref[0].astype(F32)
    for i in range(1, GY):
        total = total + arrived_ref[i].astype(F32)
    sum_ref[...] = total.astype(BF).astype(F32)
    low = low_lanes()
    for j in range(CH // 2):
        lanes = slice(2 * HALF * j, 2 * HALF * (j + 1))
        for part in range(2):
            first = sum_ref[part * SETS : (part + 1) * SETS, lanes]
            second = sum_ref[(2 + part) * SETS : (3 + part) * SETS, lanes]
            if scale is not None:
                first = first * scale
                second = second * scale
            even = jnp.where(low, first, pltpu.roll(second, HALF, 1))
            odd = jnp.where(low, pltpu.roll(first, HALF, 1), second)
            modes_ref[pl.ds(4 * j + part, SETS, stride=PAIR), :] = even
            modes_ref[pl.ds(4 * j + 2 + part, SETS, stride=PAIR), :] = odd


def spread_modes(modes_ref, sum_ref, out_ref, scale=None):
    low = low_lanes()
    for j in range(CH // 2):
        lanes = slice(2 * HALF * j, 2 * HALF * (j + 1))
        for part in range(2):
            even = modes_ref[pl.ds(4 * j + part, SETS, stride=PAIR), :]
            odd = modes_ref[pl.ds(4 * j + 2 + part, SETS, stride=PAIR), :]
            if scale is not None:
                even = even * scale
                odd = odd * scale
            sum_ref[part * SETS : (part + 1) * SETS, lanes] = jnp.where(
                low, even, pltpu.roll(odd, HALF, 1)
            )
            sum_ref[(2 + part) * SETS : (3 + part) * SETS, lanes] = jnp.where(
                low, pltpu.roll(even, HALF, 1), odd
            )
    modes = sum_ref[...].astype(BF)
    for owner in range(GY):
        out_ref[owner] = modes


def fold_scale(where_ref):
    kz = where_ref[1] * KB + lax.broadcasted_iota(jnp.int32, (SETS, 2 * HALF), 0) % KB
    return jnp.where(kz == 0, 1.0, 2.0).astype(F32) / float(NX * NY * NZ)


def turned(rows):
    even = lax.broadcasted_iota(jnp.int32, rows.shape, 0) % 2 == 0
    up = pltpu.roll(rows, PAIR - 1, 0)
    down = pltpu.roll(rows, 1, 0)
    return jnp.where(even, -up, down)


def hand_out(where_ref, modes_ref, outs):
    for k in range(DP):
        chunk = lax.rem(where_ref[0] + k, DP)
        start = pl.multiple_of(chunk * KB * PAIR, 8)
        outs[k][...] = modes_ref[pl.ds(start, KB * PAIR), :].astype(BF)


def set_row(where_ref, k):
    block = (lax.rem(where_ref[0] + k, DP) ^ (2 * (where_ref[1] & 1))) * KB + pl.program_id(0)
    return pl.multiple_of(block * PAIR, 8)


def mix_kernel(
    where_ref, arrived_ref, w0, w1, w2, w3, out_ref, u0, u1, u2, u3, sum_ref, in_ref, mix_ref
):
    step = pl.program_id(0)

    @pl.when(step == 0)
    def _():
        gather_modes(arrived_ref, sum_ref, in_ref)
        hand_out(where_ref, in_ref, (u0, u1, u2, u3))

    for k, weight_ref in enumerate((w0, w1, w2, w3)):
        base = set_row(where_ref, k)

        def add(i, totals, weight_ref=weight_ref, base=base):
            by_real, by_imag = totals
            for r in range(UNROLL):
                c = i * UNROLL + r
                weight = weight_ref[0, c].astype(F32)
                by_real = by_real + weight * in_ref[pl.ds(base + 2 * c, 1), :]
                by_imag = by_imag + weight * in_ref[pl.ds(base + 2 * c + 1, 1), :]
            return by_real, by_imag

        zero = jnp.zeros((PAIR, 2 * HALF), F32)
        by_real, by_imag = lax.fori_loop(0, CH // UNROLL, add, (zero, zero))
        mix_ref[pl.ds(base, PAIR), :] = (by_real + turned(by_imag)).astype(BF).astype(F32)

    @pl.when(step == KB - 1)
    def _():
        spread_modes(mix_ref, sum_ref, out_ref, fold_scale(where_ref))


def back_kernel(
    where_ref, arrived_ref, w0, w1, w2, w3, out_ref, u0, u1, u2, u3, sum_ref, in_ref, mix_ref
):
    step = pl.program_id(0)

    @pl.when(step == 0)
    def _():
        gather_modes(arrived_ref, sum_ref, in_ref, fold_scale(where_ref))
        hand_out(where_ref, in_ref, (u0, u1, u2, u3))

    for k, weight_ref in enumerate((w0, w1, w2, w3)):
        base = set_row(where_ref, k)
        grad = in_ref[pl.ds(base, PAIR), :]
        other = -turned(grad)

        @pl.loop(0, CH // UNROLL)
        def _(i, weight_ref=weight_ref, base=base, grad=grad, other=other):
            for r in range(UNROLL):
                c = i * UNROLL + r
                weight = weight_ref[0, c].astype(F32)
                mix_ref[pl.ds(base + 2 * c, 1), :] = jnp.sum(weight * grad, axis=0, keepdims=True)
                mix_ref[pl.ds(base + 2 * c + 1, 1), :] = jnp.sum(
                    weight * other, axis=0, keepdims=True
                )

    @pl.when(step == KB - 1)
    def _():
        spread_modes(mix_ref, sum_ref, out_ref)


def mode_call(kernel, name, where, arrived, weights):
    chunk = pl.BlockSpec((KB * PAIR, 2 * HALF), lambda i, w: (0, 0))
    return pl.pallas_call(
        kernel,
        grid_spec=pltpu.PrefetchScalarGridSpec(
            num_scalar_prefetch=1,
            grid=(KB,),
            in_specs=[pl.BlockSpec((GY, 48, WIDE), lambda i, w: (0, 0, 0))]
            + [pl.BlockSpec((1, CH, PAIR, 2 * HALF), lambda i, w: (i, 0, 0, 0))] * 4,
            out_specs=[pl.BlockSpec((GY, 48, WIDE), lambda i, w: (0, 0, 0))] + [chunk] * 4,
            scratch_shapes=[
                pltpu.VMEM((48, WIDE), F32),
                pltpu.VMEM((SETS * PAIR, 2 * HALF), F32),
                pltpu.VMEM((SETS * PAIR, 2 * HALF), F32),
            ],
        ),
        out_shape=[jax.ShapeDtypeStruct((GY, 48, WIDE), BF)]
        + [jax.ShapeDtypeStruct((KB * PAIR, 2 * HALF), BF)] * 4,
        cost_estimate=cost(5),
        name=name,
    )(where, arrived, *weights)


def outer_kernel(s0, s1, s2, s3, g0, g1, g2, g3, out_ref, spec_ref):
    for k, ref in enumerate((s0, s1, s2, s3)):
        spec_ref[k] = ref[...].astype(F32)
    for i in range(KB):
        grads = []
        others = []
        for ref in (g0, g1, g2, g3):
            grad = ref[...].astype(F32)[i * PAIR : (i + 1) * PAIR]
            grads.append(grad)
            others.append(-turned(grad))

        @pl.loop(0, CH)
        def _(c):
            row = i * PAIR + 2 * c
            total = jnp.zeros((PAIR, 2 * HALF), F32)
            for k in range(DP):
                total = total + spec_ref[k, pl.ds(row, 1), :] * grads[k]
                total = total + spec_ref[k, pl.ds(row + 1, 1), :] * others[k]
            out_ref[i, c] = total


def outer_sum(spectra, grads):
    return pl.pallas_call(
        outer_kernel,
        out_shape=jax.ShapeDtypeStruct((KB, CH, PAIR, 2 * HALF), F32),
        scratch_shapes=[pltpu.VMEM((DP, KB * PAIR, 2 * HALF), F32)],
        cost_estimate=cost(3),
        name="outer_sum",
    )(*spectra, *grads)


def swap(values, bit):
    return lax.ppermute(values, "gx", [(i, i ^ bit) for i in range(GX)])


def start_slabs(pieces):
    own, far, near, across = pieces
    far_sum = (far.astype(F32) + swap(across, 1).astype(F32)).astype(BF)
    return own, swap(near, 1), swap(far_sum, 2)


def share_slabs(own, *waiting):
    far = swap(own, 2)
    far, *waiting = lax.optimization_barrier((far, *waiting))
    return own, far, swap(own, 1), swap(far, 1), *waiting


def gather_weights(weight):
    held = [weight]
    for k in range(1, DP):
        held.append(lax.ppermute(weight, "dp", [((a + k) % DP, a) for a in range(DP)]))
    return [part.reshape(KB, CH, PAIR, 2 * HALF) for part in held]


def exchange_lines(parts):
    return lax.all_to_all(parts, "gy", split_axis=0, concat_axis=0, tiled=True)


def to_owners(chunks):
    moved = []
    for k, chunk in enumerate(chunks):
        pairs = [
            (a * GX + b, b * GX + (a + k) % DP) for a in range(DP) for b in range(GX)
        ]
        moved.append(lax.ppermute(chunk, ("dp", "gx"), pairs))
    return moved


def per_device(field, spectral_weight, bypass_weight, bias, cotangent):
    where = jnp.stack(
        [lax.axis_index("dp"), lax.axis_index("gx"), lax.axis_index("gy")]
    ).astype(jnp.int32)
    turn = [(a * GX + b, (b ^ (2 * (a % 2))) * GX + a) for a in range(DP) for b in range(GX)]
    weight = lax.ppermute(spectral_weight, ("dp", "gx"), turn)
    spread = jnp.asarray(SPREAD)

    def mixer_of(matrix):
        wide = dot(dot(spread, matrix).astype(BF), spread, 1, 1)
        return wide.astype(BF) * jnp.asarray(SAME)

    values = field[0]
    *pieces, weight = lax.optimization_barrier((*start_columns(where, values), weight))
    parts = start_slabs(pieces)
    weights = gather_weights(weight)
    lines, weights[1], weights[3] = lax.optimization_barrier(
        (to_lines(where, *parts), weights[1], weights[3])
    )
    arrived = exchange_lines(lines)
    modes, *spectra = mode_call(mix_kernel, "mix_modes", where, arrived, weights)
    modes, *spectra = lax.optimization_barrier((exchange_lines(modes), *to_owners(spectra)))
    coeffs = share_slabs(from_lines(where, modes))
    activation, grad, *pieces = middle_columns(
        where, bias, coeffs, values, cotangent[0], mixer_of(bypass_weight)
    )
    arrived = exchange_lines(to_lines(where, *start_slabs(pieces)))
    modes, *grads = mode_call(back_kernel, "back_modes", where, arrived, weights)
    modes, *grads = lax.optimization_barrier((exchange_lines(modes), *to_owners(grads)))
    *coeffs, weight_grad = share_slabs(from_lines(where, modes), outer_sum(spectra, grads))
    field_grad = end_columns(where, coeffs, grad, mixer_of(bypass_weight.T))
    return (
        activation[None],
        field_grad[None],
        weight_grad.reshape(KB, CH, CH, 2, 2 * HALF),
    )


def solution(mesh):
    placed = (
        P("dp", None, "gx", "gy"),
        P("dp", None, None, None, ("gx", "gy")),
        P(),
        P(),
        P("dp", None, "gx", "gy"),
    )
    return jax.shard_map(
        per_device,
        mesh=mesh,
        in_specs=placed,
        out_specs=(
            P("dp", None, "gx", "gy"),
            P("dp", None, "gx", "gy"),
            P("dp", None, None, None, ("gx", "gy")),
        ),
        check_vma=False,
    )
```

```python
import functools
import math

import jax
import jax.numpy as jnp
import ml_dtypes
import numpy as np
from jax import lax
from jax.experimental import pallas as pl
from jax.experimental.pallas import tpu as pltpu
from jax.sharding import PartitionSpec as P

CH = 20
NX = 256
NY = 256
NZ = 64
KX = 64
KY = 64
KZ = 12
GX = 4
GY = 8
DP = 4
XL = NX // GX
YL = NY // GY
YB = 8
STEPS = YL // YB
LANES = YB * NZ
KB = KZ // GX
ROWS = 2 * KB * YB
GROUP = 4
GROUPS = CH // GROUP
GL = GROUP * KX
WIDE = CH * KX
XB = 8
EB = 16
ORDER = (0, 2, 1, 3)

BF = jnp.bfloat16
F32 = jnp.float32


def wave(freqs, points, length):
    offsets = np.mod(freqs[:, None] * points[None, :], length)
    angle = offsets.astype(np.float32) * np.float32(2.0 * math.pi / length)
    return np.cos(angle), np.sin(angle)


def kept(count):
    index = np.arange(count)
    return np.where(index < count // 2, index, index - count)


def depth_tables():
    out = np.zeros((GX, 2, GX, KB, LANES), np.float32)
    for b in range(GX):
        for pos, delta in enumerate(ORDER):
            freqs = (b ^ delta) * KB + np.arange(KB)
            cosine, sine = wave(freqs, np.arange(NZ), NZ)
            out[b, 0, pos] = np.tile(cosine, (1, YB))
            out[b, 1, pos] = np.tile(-sine, (1, YB))
    return out.reshape(GX, 2 * KZ, LANES).astype(ml_dtypes.bfloat16)


def width_tables():
    out = np.zeros((GX, 2, XL, KX), np.float32)
    for b in range(GX):
        cosine, sine = wave(kept(KX), b * XL + np.arange(XL), NX)
        out[b, 0] = cosine.T
        out[b, 1] = sine.T
    return out.astype(ml_dtypes.bfloat16)


def line_tables():
    out = np.zeros((GY, GY, 2, 2, GX, KB, STEPS, 2, KB, YB), np.float32)
    fy = kept(KY)
    for g in range(GY):
        cosine, sine = wave(fy, g * YL + np.arange(YL), NY)
        cosine = cosine.reshape(GX, GY, 2, STEPS, YB)
        sine = sine.reshape(GX, GY, 2, STEPS, YB)
        for i in range(KB):
            for owner in range(GY):
                for q in range(2):
                    c = cosine[:, owner, q]
                    s = sine[:, owner, q]
                    out[g, owner, q, 0, :, i, :, 0, i] = c
                    out[g, owner, q, 0, :, i, :, 1, i] = s
                    out[g, owner, q, 1, :, i, :, 0, i] = -s
                    out[g, owner, q, 1, :, i, :, 1, i] = c
    return out.reshape(GY, GY * 48, STEPS * ROWS).astype(ml_dtypes.bfloat16)


DEPTH = depth_tables()
WIDTH = width_tables()
LINE = line_tables()
SPREAD = np.kron(np.eye(CH), np.ones((XB, 1))).astype(ml_dtypes.bfloat16)
SAME = np.kron(np.ones((CH, CH)), np.eye(XB)).astype(ml_dtypes.bfloat16)


def dot(left, right, left_dim=1, right_dim=0):
    return lax.dot_general(
        left, right, (((left_dim,), (right_dim,)), ((), ())), preferred_element_type=F32
    )


def fill_tables(strip_ref, wide_ref, depth_ref, tall_ref, long_ref):
    strips = jnp.broadcast_to(strip_ref[0].astype(F32)[:, None, :], (2 * KZ, YB, LANES))
    row = lax.broadcasted_iota(jnp.int32, (2 * KZ, YB, LANES), 1)
    column = lax.broadcasted_iota(jnp.int32, (2 * KZ, YB, LANES), 2) // NZ
    blocks = jnp.where(row == column, strips, 0.0)
    depth_ref[...] = blocks.reshape(2 * KZ * YB, LANES).astype(BF)
    rows = lax.broadcasted_iota(jnp.int32, (GL, GL), 0) // XL
    columns = lax.broadcasted_iota(jnp.int32, (GL, GL), 1) // KX
    for part in range(2):
        strip = wide_ref[0, part].astype(F32)
        full = jnp.concatenate([jnp.concatenate([strip] * GROUP, axis=1)] * GROUP, axis=0)
        block = jnp.where(rows == columns, full, 0.0).astype(BF)
        tall_ref[GL * part : GL * (part + 1), :] = block
        long_ref[:, GL * part : GL * (part + 1)] = block


def forward_group(rows, depth_ref, tall_ref, outs, y):
    half = KZ * YB
    planes = dot(depth_ref[...], rows, 1, 1)
    real = planes[:half]
    imag = planes[half:]
    sides = jnp.concatenate(
        [jnp.concatenate([real, imag], axis=1), jnp.concatenate([imag, -real], axis=1)], axis=0
    ).astype(BF)
    lines = dot(sides, tall_ref[...])
    for pos in range(GX):
        lo = pos * KB * YB
        piece = jnp.concatenate(
            [lines[lo : lo + KB * YB], lines[half + lo : half + lo + KB * YB]], axis=0
        )
        outs[pos][y] = piece.astype(BF)


def inverse_group(ins, depth_ref, long_ref, y):
    part = KB * YB
    pieces = [ref[y].astype(F32) for ref in ins]
    real = jnp.concatenate([piece[:part] for piece in pieces], axis=0)
    imag = jnp.concatenate([piece[part:] for piece in pieces], axis=0)
    sides = jnp.concatenate(
        [jnp.concatenate([real, -imag], axis=1), jnp.concatenate([imag, real], axis=1)], axis=0
    ).astype(BF)
    planes = dot(long_ref[...], sides, 1, 1).astype(BF)
    return dot(planes, depth_ref[...])


def run_rows(ref, y):
    return ref[:, :, LANES * y : LANES * (y + 1)].reshape(GROUP * XL, LANES)


def bypass_kernel(source_ref, mixer_ref, out_ref):
    for i in range(XL // XB):
        span = slice(i * XB, (i + 1) * XB)
        rows = source_ref[:, span, :].reshape(CH * XB, LANES)
        out_ref[:, span, :] = dot(mixer_ref[...], rows).reshape(CH, XB, LANES)


def start_kernel(
    where_ref, field_ref, strip_ref, wide_ref, o0, o1, o2, o3, depth_ref, tall_ref, long_ref
):
    @pl.when(pl.program_id(0) == 0)
    def _():
        fill_tables(strip_ref, wide_ref, depth_ref, tall_ref, long_ref)

    for y in range(STEPS):
        forward_group(run_rows(field_ref, y), depth_ref, tall_ref, (o0, o1, o2, o3), y)


ROOT = math.sqrt(2.0 / math.pi)
CUBE = 0.044715


def activate(bias_ref, upstream_ref, total_ref, act_ref, grad_ref, y):
    lanes = slice(LANES * y, LANES * (y + 1))
    for channel in range(GROUP):
        shift = bias_ref[GROUP * pl.program_id(0) + channel]
        for i in range(XL // EB):
            span = slice(i * EB, (i + 1) * EB)
            x = total_ref[y, channel, span, :] + shift
            square = x * x
            t = jnp.tanh(x * (ROOT + (ROOT * CUBE) * square))
            h = 0.5 * t + 0.5
            act = x * h
            slope = h + act * (1.0 - h) * (2.0 * ROOT + (6.0 * ROOT * CUBE) * square)
            act_ref[channel, span, lanes] = act.astype(BF)
            up = upstream_ref[channel, span, lanes].astype(F32)
            grad_ref[channel, span, lanes] = (up * slope).astype(BF)


def middle_kernel(
    where_ref, bias_ref, i0, i1, i2, i3, bypass_ref, upstream_ref, strip_ref, wide_ref,
    act_ref, grad_ref, o0, o1, o2, o3, depth_ref, tall_ref, long_ref, total_ref,
):
    @pl.when(pl.program_id(0) == 0)
    def _():
        fill_tables(strip_ref, wide_ref, depth_ref, tall_ref, long_ref)

    def inverse(y):
        values = inverse_group((i0, i1, i2, i3), depth_ref, long_ref, y)
        lanes = slice(LANES * y, LANES * (y + 1))
        total_ref[y] = bypass_ref[:, :, lanes] + values.reshape(GROUP, XL, LANES)

    def forward(y):
        forward_group(run_rows(grad_ref, y), depth_ref, tall_ref, (o0, o1, o2, o3), y)

    inverse(0)
    for y in range(STEPS):
        if y + 1 < STEPS:
            inverse(y + 1)
        activate(bias_ref, upstream_ref, total_ref, act_ref, grad_ref, y)
        if y > 0:
            forward(y - 1)
    forward(STEPS - 1)


def end_kernel(
    where_ref, i0, i1, i2, i3, bypass_ref, strip_ref, wide_ref, out_ref,
    depth_ref, tall_ref, long_ref,
):
    @pl.when(pl.program_id(0) == 0)
    def _():
        fill_tables(strip_ref, wide_ref, depth_ref, tall_ref, long_ref)

    for y in range(STEPS):
        values = inverse_group((i0, i1, i2, i3), depth_ref, long_ref, y)
        lanes = slice(LANES * y, LANES * (y + 1))
        out_ref[:, :, lanes] = (
            bypass_ref[:, :, lanes] + values.reshape(GROUP, XL, LANES)
        ).astype(BF)


def cost(micros):
    return pl.CostEstimate(flops=0, bytes_accessed=micros * 3_000_000, transcendentals=0)


def column_specs():
    columns = pl.BlockSpec((GROUP, XL, YL * NZ), lambda j, w: (j, 0, 0))
    coeffs = pl.BlockSpec((STEPS, ROWS, GL), lambda j, w: (0, 0, j))
    depth = pl.BlockSpec((1, 2 * KZ, LANES), lambda j, w: (w[1], 0, 0))
    wide = pl.BlockSpec((1, 2, XL, KX), lambda j, w: (w[1], 0, 0, 0))
    return columns, coeffs, depth, wide


COEFFS = jax.ShapeDtypeStruct((STEPS, ROWS, WIDE), BF)
COLUMNS = jax.ShapeDtypeStruct((CH, XL, YL * NZ), BF)
BLOCKS = [
    pltpu.VMEM((2 * KZ * YB, LANES), BF),
    pltpu.VMEM((2 * GL, GL), BF),
    pltpu.VMEM((GL, 2 * GL), BF),
]
TOTAL = pltpu.VMEM((STEPS, GROUP, XL, LANES), F32)
PARAMS = pltpu.CompilerParams(vmem_limit_bytes=63 * 1024 * 1024)


def bypass_columns(source, mixer):
    columns = pl.BlockSpec((CH, XL, LANES), lambda i: (0, 0, i))
    return pl.pallas_call(
        bypass_kernel,
        grid=(STEPS,),
        in_specs=[columns, pl.BlockSpec((CH * XB, CH * XB), lambda i: (0, 0))],
        out_specs=columns,
        out_shape=jax.ShapeDtypeStruct((CH, XL, YL * NZ), F32),
        compiler_params=PARAMS,
        cost_estimate=cost(6),
        name="bypass_columns",
    )(source, mixer)


def start_columns(where, field):
    columns, coeffs, depth, wide = column_specs()
    return pl.pallas_call(
        start_kernel,
        grid_spec=pltpu.PrefetchScalarGridSpec(
            num_scalar_prefetch=1,
            grid=(GROUPS,),
            in_specs=[columns, depth, wide],
            out_specs=[coeffs] * 4,
            scratch_shapes=BLOCKS,
        ),
        out_shape=[COEFFS] * 4,
        compiler_params=PARAMS,
        cost_estimate=cost(8),
        name="start_columns",
    )(where, field, jnp.asarray(DEPTH), jnp.asarray(WIDTH))


def middle_columns(where, bias, coeffs_in, bypass, upstream):
    columns, coeffs, depth, wide = column_specs()
    return pl.pallas_call(
        middle_kernel,
        grid_spec=pltpu.PrefetchScalarGridSpec(
            num_scalar_prefetch=1,
            grid=(GROUPS,),
            in_specs=[pl.BlockSpec(memory_space=pltpu.SMEM)]
            + [coeffs] * 4
            + [columns, columns, depth, wide],
            out_specs=[columns, columns] + [coeffs] * 4,
            scratch_shapes=BLOCKS + [TOTAL],
        ),
        out_shape=[COLUMNS, COLUMNS] + [COEFFS] * 4,
        compiler_params=PARAMS,
        cost_estimate=cost(19),
        name="middle_columns",
    )(where, bias, *coeffs_in, bypass, upstream, jnp.asarray(DEPTH), jnp.asarray(WIDTH))


def end_columns(where, coeffs_in, bypass):
    columns, coeffs, depth, wide = column_specs()
    return pl.pallas_call(
        end_kernel,
        grid_spec=pltpu.PrefetchScalarGridSpec(
            num_scalar_prefetch=1,
            grid=(GROUPS,),
            in_specs=[coeffs] * 4 + [columns, depth, wide],
            out_specs=columns,
            scratch_shapes=BLOCKS,
        ),
        out_shape=COLUMNS,
        compiler_params=PARAMS,
        cost_estimate=cost(10),
        name="end_columns",
    )(where, *coeffs_in, bypass, jnp.asarray(DEPTH), jnp.asarray(WIDTH))


def line_kernel(where_ref, a_ref, b_ref, c_ref, table_ref, out_ref):
    for j in range(GROUPS):
        lanes = slice(GL * j, GL * (j + 1))
        parts = [ref[:, :, lanes].astype(F32) for ref in (a_ref, b_ref, c_ref)]
        rows = (parts[0] + parts[1] + parts[2]).astype(BF).reshape(STEPS * ROWS, GL)
        out_ref[:, :, lanes] = dot(table_ref[0], rows).astype(BF).reshape(GY, 48, GL)


def unline_kernel(where_ref, modes_ref, table_ref, out_ref):
    for j in range(GROUPS):
        lanes = slice(GL * j, GL * (j + 1))
        rows = modes_ref[:, :, lanes].reshape(GY * 48, GL)
        out_ref[:, :, lanes] = dot(table_ref[0], rows, 0, 0).astype(BF).reshape(STEPS, ROWS, GL)


def line_call(kernel, name, where, ins, out_shape):
    whole = pl.BlockSpec(ins[0].shape, lambda i, w: (0, 0, 0))
    table = pl.BlockSpec((1, GY * 48, STEPS * ROWS), lambda i, w: (w[2], 0, 0))
    return pl.pallas_call(
        kernel,
        grid_spec=pltpu.PrefetchScalarGridSpec(
            num_scalar_prefetch=1,
            grid=(1,),
            in_specs=[whole] * len(ins) + [table],
            out_specs=pl.BlockSpec(out_shape.shape, lambda i, w: (0, 0, 0)),
        ),
        out_shape=out_shape,
        compiler_params=PARAMS,
        cost_estimate=cost(3),
        name=name,
    )(where, *ins, jnp.asarray(LINE))


def to_lines(where, *parts):
    out = jax.ShapeDtypeStruct((GY, 48, WIDE), BF)
    return line_call(line_kernel, "to_lines", where, parts, out)


def from_lines(where, modes):
    return line_call(unline_kernel, "from_lines", where, (modes,), COEFFS)


UNROLL = 4
SETS = GX * KB
PAIR = 2 * CH
HALF = KX


def low_lanes():
    return lax.broadcasted_iota(jnp.int32, (SETS, 2 * HALF), 1) < HALF


def gather_modes(arrived_ref, sum_ref, modes_ref, scale=None):
    total = arrived_ref[0].astype(F32)
    for i in range(1, GY):
        total = total + arrived_ref[i].astype(F32)
    sum_ref[...] = total.astype(BF).astype(F32)
    low = low_lanes()
    for j in range(CH // 2):
        lanes = slice(2 * HALF * j, 2 * HALF * (j + 1))
        for part in range(2):
            first = sum_ref[part * SETS : (part + 1) * SETS, lanes]
            second = sum_ref[(2 + part) * SETS : (3 + part) * SETS, lanes]
            if scale is not None:
                first = first * scale
                second = second * scale
            even = jnp.where(low, first, pltpu.roll(second, HALF, 1))
            odd = jnp.where(low, pltpu.roll(first, HALF, 1), second)
            modes_ref[pl.ds(4 * j + part, SETS, stride=PAIR), :] = even
            modes_ref[pl.ds(4 * j + 2 + part, SETS, stride=PAIR), :] = odd


def spread_modes(modes_ref, sum_ref, out_ref, scale=None):
    low = low_lanes()
    for j in range(CH // 2):
        lanes = slice(2 * HALF * j, 2 * HALF * (j + 1))
        for part in range(2):
            even = modes_ref[pl.ds(4 * j + part, SETS, stride=PAIR), :]
            odd = modes_ref[pl.ds(4 * j + 2 + part, SETS, stride=PAIR), :]
            if scale is not None:
                even = even * scale
                odd = odd * scale
            sum_ref[part * SETS : (part + 1) * SETS, lanes] = jnp.where(
                low, even, pltpu.roll(odd, HALF, 1)
            )
            sum_ref[(2 + part) * SETS : (3 + part) * SETS, lanes] = jnp.where(
                low, pltpu.roll(even, HALF, 1), odd
            )
    modes = sum_ref[...].astype(BF)
    for owner in range(GY):
        out_ref[owner] = modes


def fold_scale(where_ref):
    kz = where_ref[1] * KB + lax.broadcasted_iota(jnp.int32, (SETS, 2 * HALF), 0) % KB
    return jnp.where(kz == 0, 1.0, 2.0).astype(F32) / float(NX * NY * NZ)


def turned(rows):
    even = lax.broadcasted_iota(jnp.int32, rows.shape, 0) % 2 == 0
    up = pltpu.roll(rows, PAIR - 1, 0)
    down = pltpu.roll(rows, 1, 0)
    return jnp.where(even, -up, down)


def hand_out(where_ref, modes_ref, outs):
    for k in range(DP):
        chunk = lax.rem(where_ref[0] + k, DP)
        start = pl.multiple_of(chunk * KB * PAIR, 8)
        outs[k][...] = modes_ref[pl.ds(start, KB * PAIR), :].astype(BF)


def set_row(where_ref, k):
    block = (lax.rem(where_ref[0] + k, DP) ^ (2 * (where_ref[1] & 1))) * KB + pl.program_id(0)
    return pl.multiple_of(block * PAIR, 8)


def mix_kernel(
    where_ref, arrived_ref, w0, w1, w2, w3, out_ref, u0, u1, u2, u3, sum_ref, in_ref, mix_ref
):
    step = pl.program_id(0)

    @pl.when(step == 0)
    def _():
        gather_modes(arrived_ref, sum_ref, in_ref)
        hand_out(where_ref, in_ref, (u0, u1, u2, u3))

    for k, weight_ref in enumerate((w0, w1, w2, w3)):
        base = set_row(where_ref, k)

        def add(i, totals, weight_ref=weight_ref, base=base):
            by_real, by_imag = totals
            for r in range(UNROLL):
                c = i * UNROLL + r
                weight = weight_ref[0, c].astype(F32)
                by_real = by_real + weight * in_ref[pl.ds(base + 2 * c, 1), :]
                by_imag = by_imag + weight * in_ref[pl.ds(base + 2 * c + 1, 1), :]
            return by_real, by_imag

        zero = jnp.zeros((PAIR, 2 * HALF), F32)
        by_real, by_imag = lax.fori_loop(0, CH // UNROLL, add, (zero, zero))
        mix_ref[pl.ds(base, PAIR), :] = (by_real + turned(by_imag)).astype(BF).astype(F32)

    @pl.when(step == KB - 1)
    def _():
        spread_modes(mix_ref, sum_ref, out_ref, fold_scale(where_ref))


def back_kernel(
    where_ref, arrived_ref, w0, w1, w2, w3, out_ref, u0, u1, u2, u3, sum_ref, in_ref, mix_ref
):
    step = pl.program_id(0)

    @pl.when(step == 0)
    def _():
        gather_modes(arrived_ref, sum_ref, in_ref, fold_scale(where_ref))
        hand_out(where_ref, in_ref, (u0, u1, u2, u3))

    for k, weight_ref in enumerate((w0, w1, w2, w3)):
        base = set_row(where_ref, k)
        grad = in_ref[pl.ds(base, PAIR), :]
        other = -turned(grad)

        @pl.loop(0, CH // UNROLL)
        def _(i, weight_ref=weight_ref, base=base, grad=grad, other=other):
            for r in range(UNROLL):
                c = i * UNROLL + r
                weight = weight_ref[0, c].astype(F32)
                mix_ref[pl.ds(base + 2 * c, 1), :] = jnp.sum(weight * grad, axis=0, keepdims=True)
                mix_ref[pl.ds(base + 2 * c + 1, 1), :] = jnp.sum(
                    weight * other, axis=0, keepdims=True
                )

    @pl.when(step == KB - 1)
    def _():
        spread_modes(mix_ref, sum_ref, out_ref)


def mode_call(kernel, name, where, arrived, weights):
    chunk = pl.BlockSpec((KB * PAIR, 2 * HALF), lambda i, w: (0, 0))
    return pl.pallas_call(
        kernel,
        grid_spec=pltpu.PrefetchScalarGridSpec(
            num_scalar_prefetch=1,
            grid=(KB,),
            in_specs=[pl.BlockSpec((GY, 48, WIDE), lambda i, w: (0, 0, 0))]
            + [pl.BlockSpec((1, CH, PAIR, 2 * HALF), lambda i, w: (i, 0, 0, 0))] * 4,
            out_specs=[pl.BlockSpec((GY, 48, WIDE), lambda i, w: (0, 0, 0))] + [chunk] * 4,
            scratch_shapes=[
                pltpu.VMEM((48, WIDE), F32),
                pltpu.VMEM((SETS * PAIR, 2 * HALF), F32),
                pltpu.VMEM((SETS * PAIR, 2 * HALF), F32),
            ],
        ),
        out_shape=[jax.ShapeDtypeStruct((GY, 48, WIDE), BF)]
        + [jax.ShapeDtypeStruct((KB * PAIR, 2 * HALF), BF)] * 4,
        compiler_params=PARAMS,
        cost_estimate=cost(5),
        name=name,
    )(where, arrived, *weights)


def outer_kernel(s0, s1, s2, s3, g0, g1, g2, g3, out_ref, spec_ref):
    for k, ref in enumerate((s0, s1, s2, s3)):
        spec_ref[k] = ref[...].astype(F32)
    for i in range(KB):
        grads = []
        others = []
        for ref in (g0, g1, g2, g3):
            grad = ref[...].astype(F32)[i * PAIR : (i + 1) * PAIR]
            grads.append(grad)
            others.append(-turned(grad))

        @pl.loop(0, CH)
        def _(c):
            row = i * PAIR + 2 * c
            total = jnp.zeros((PAIR, 2 * HALF), F32)
            for k in range(DP):
                total = total + spec_ref[k, pl.ds(row, 1), :] * grads[k]
                total = total + spec_ref[k, pl.ds(row + 1, 1), :] * others[k]
            out_ref[i, c] = total


def outer_sum(spectra, grads):
    return pl.pallas_call(
        outer_kernel,
        out_shape=jax.ShapeDtypeStruct((KB, CH, PAIR, 2 * HALF), F32),
        scratch_shapes=[pltpu.VMEM((DP, KB * PAIR, 2 * HALF), F32)],
        cost_estimate=cost(3),
        name="outer_sum",
    )(*spectra, *grads)


def swap(values, bit):
    return lax.ppermute(values, "gx", [(i, i ^ bit) for i in range(GX)])


def start_slabs(pieces, beside):
    own, far, near, across = pieces
    far_sum = (far.astype(F32) + swap(across, 1).astype(F32)).astype(BF)
    arrived, beside = lax.optimization_barrier((swap(far_sum, 2), beside))
    return (own, swap(near, 1), arrived), beside


def share_slabs(own, *waiting):
    far = swap(own, 2)
    far, *waiting = lax.optimization_barrier((far, *waiting))
    return own, far, swap(own, 1), swap(far, 1), *waiting


def gather_weights(weight):
    held = [weight]
    for k in range(1, DP):
        held.append(lax.ppermute(weight, "dp", [((a + k) % DP, a) for a in range(DP)]))
    return [part.reshape(KB, CH, PAIR, 2 * HALF) for part in held]


def exchange_lines(parts):
    return lax.all_to_all(parts, "gy", split_axis=0, concat_axis=0, tiled=True)


def to_owners(chunks):
    moved = []
    for k, chunk in enumerate(chunks):
        pairs = [
            (a * GX + b, b * GX + (a + k) % DP) for a in range(DP) for b in range(GX)
        ]
        moved.append(lax.ppermute(chunk, ("dp", "gx"), pairs))
    return moved


def per_device(field, spectral_weight, bypass_weight, bias, cotangent):
    where = jnp.stack(
        [lax.axis_index("dp"), lax.axis_index("gx"), lax.axis_index("gy")]
    ).astype(jnp.int32)
    turn = [(a * GX + b, (b ^ (2 * (a % 2))) * GX + a) for a in range(DP) for b in range(GX)]
    weight = lax.ppermute(spectral_weight, ("dp", "gx"), turn)
    spread = jnp.asarray(SPREAD)

    def mixer_of(matrix):
        wide = dot(dot(spread, matrix).astype(BF), spread, 1, 1)
        return wide.astype(BF) * jnp.asarray(SAME)

    values = field[0]
    *pieces, weight = lax.optimization_barrier((*start_columns(where, values), weight))
    parts, bypass = start_slabs(pieces, bypass_columns(values, mixer_of(bypass_weight)))
    weights = gather_weights(weight)
    lines, weights[1], weights[3] = lax.optimization_barrier(
        (to_lines(where, *parts), weights[1], weights[3])
    )
    arrived = exchange_lines(lines)
    modes, *spectra = mode_call(mix_kernel, "mix_modes", where, arrived, weights)
    modes, *spectra = lax.optimization_barrier((exchange_lines(modes), *to_owners(spectra)))
    coeffs = share_slabs(from_lines(where, modes))
    activation, grad, *pieces = middle_columns(where, bias, coeffs, bypass, cotangent[0])
    parts, bypass = start_slabs(pieces, bypass_columns(grad, mixer_of(bypass_weight.T)))
    arrived = exchange_lines(to_lines(where, *parts))
    modes, *grads = mode_call(back_kernel, "back_modes", where, arrived, weights)
    modes, *grads = lax.optimization_barrier((exchange_lines(modes), *to_owners(grads)))
    *coeffs, weight_grad = share_slabs(from_lines(where, modes), outer_sum(spectra, grads))
    field_grad = end_columns(where, coeffs, bypass)
    return (
        activation[None],
        field_grad[None],
        weight_grad.reshape(KB, CH, CH, 2, 2 * HALF),
    )


def solution(mesh):
    placed = (
        P("dp", None, "gx", "gy"),
        P("dp", None, None, None, ("gx", "gy")),
        P(),
        P(),
        P("dp", None, "gx", "gy"),
    )
    return jax.shard_map(
        per_device,
        mesh=mesh,
        in_specs=placed,
        out_specs=(
            P("dp", None, "gx", "gy"),
            P("dp", None, "gx", "gy"),
            P("dp", None, None, None, ("gx", "gy")),
        ),
        check_vma=False,
    )
```

```python
import functools
import math

import jax
import jax.numpy as jnp
import ml_dtypes
import numpy as np
from jax import lax
from jax.experimental import pallas as pl
from jax.experimental.pallas import tpu as pltpu
from jax.sharding import PartitionSpec as P

CH = 20
NX = 256
NY = 256
NZ = 64
KX = 64
KY = 64
KZ = 12
GX = 4
GY = 8
DP = 4
XL = NX // GX
YL = NY // GY
YB = 8
STEPS = YL // YB
LANES = YB * NZ
KB = KZ // GX
ROWS = 2 * KB * YB
GROUP = 4
GROUPS = CH // GROUP
GL = GROUP * KX
WIDE = CH * KX
XB = 8
EB = 16
ORDER = (0, 2, 1, 3)

BF = jnp.bfloat16
F32 = jnp.float32


def wave(freqs, points, length):
    offsets = np.mod(freqs[:, None] * points[None, :], length)
    angle = offsets.astype(np.float32) * np.float32(2.0 * math.pi / length)
    return np.cos(angle), np.sin(angle)


def kept(count):
    index = np.arange(count)
    return np.where(index < count // 2, index, index - count)


def depth_tables():
    out = np.zeros((GX, 2, GX, KB, LANES), np.float32)
    for b in range(GX):
        for pos, delta in enumerate(ORDER):
            freqs = (b ^ delta) * KB + np.arange(KB)
            cosine, sine = wave(freqs, np.arange(NZ), NZ)
            out[b, 0, pos] = np.tile(cosine, (1, YB))
            out[b, 1, pos] = np.tile(-sine, (1, YB))
    return out.reshape(GX, 2 * KZ, LANES).astype(ml_dtypes.bfloat16)


def width_tables():
    out = np.zeros((GX, 2, XL, KX), np.float32)
    for b in range(GX):
        cosine, sine = wave(kept(KX), b * XL + np.arange(XL), NX)
        out[b, 0] = cosine.T
        out[b, 1] = sine.T
    return out.astype(ml_dtypes.bfloat16)


def line_tables():
    out = np.zeros((GY, GY, 2, 2, GX, KB, STEPS, 2, KB, YB), np.float32)
    fy = kept(KY)
    for g in range(GY):
        cosine, sine = wave(fy, g * YL + np.arange(YL), NY)
        cosine = cosine.reshape(GX, GY, 2, STEPS, YB)
        sine = sine.reshape(GX, GY, 2, STEPS, YB)
        for i in range(KB):
            for owner in range(GY):
                for q in range(2):
                    c = cosine[:, owner, q]
                    s = sine[:, owner, q]
                    out[g, owner, q, 0, :, i, :, 0, i] = c
                    out[g, owner, q, 0, :, i, :, 1, i] = s
                    out[g, owner, q, 1, :, i, :, 0, i] = -s
                    out[g, owner, q, 1, :, i, :, 1, i] = c
    return out.reshape(GY, GY * 48, STEPS * ROWS).astype(ml_dtypes.bfloat16)


DEPTH = depth_tables()
WIDTH = width_tables()
LINE = line_tables()
SPREAD = np.kron(np.eye(CH), np.ones((XB, 1))).astype(ml_dtypes.bfloat16)
SAME = np.kron(np.ones((CH, CH)), np.eye(XB)).astype(ml_dtypes.bfloat16)


def dot(left, right, left_dim=1, right_dim=0):
    return lax.dot_general(
        left, right, (((left_dim,), (right_dim,)), ((), ())), preferred_element_type=F32
    )


def fill_tables(strip_ref, wide_ref, depth_ref, tall_ref, long_ref):
    strips = jnp.broadcast_to(strip_ref[0].astype(F32)[:, None, :], (2 * KZ, YB, LANES))
    row = lax.broadcasted_iota(jnp.int32, (2 * KZ, YB, LANES), 1)
    column = lax.broadcasted_iota(jnp.int32, (2 * KZ, YB, LANES), 2) // NZ
    blocks = jnp.where(row == column, strips, 0.0)
    depth_ref[...] = blocks.reshape(2 * KZ * YB, LANES).astype(BF)
    rows = lax.broadcasted_iota(jnp.int32, (GL, GL), 0) // XL
    columns = lax.broadcasted_iota(jnp.int32, (GL, GL), 1) // KX
    for part in range(2):
        strip = wide_ref[0, part].astype(F32)
        full = jnp.concatenate([jnp.concatenate([strip] * GROUP, axis=1)] * GROUP, axis=0)
        block = jnp.where(rows == columns, full, 0.0).astype(BF)
        tall_ref[GL * part : GL * (part + 1), :] = block
        long_ref[:, GL * part : GL * (part + 1)] = block


def forward_group(rows, depth_ref, tall_ref, outs, y):
    half = KZ * YB
    planes = dot(depth_ref[...], rows, 1, 1)
    real = planes[:half]
    imag = planes[half:]
    sides = jnp.concatenate(
        [jnp.concatenate([real, imag], axis=1), jnp.concatenate([imag, -real], axis=1)], axis=0
    ).astype(BF)
    lines = dot(sides, tall_ref[...])
    for pos in range(GX):
        lo = pos * KB * YB
        piece = jnp.concatenate(
            [lines[lo : lo + KB * YB], lines[half + lo : half + lo + KB * YB]], axis=0
        )
        outs[pos][y] = piece.astype(BF)


def inverse_group(ins, depth_ref, long_ref, y):
    part = KB * YB
    pieces = [ref[y].astype(F32) for ref in ins]
    real = jnp.concatenate([piece[:part] for piece in pieces], axis=0)
    imag = jnp.concatenate([piece[part:] for piece in pieces], axis=0)
    sides = jnp.concatenate(
        [jnp.concatenate([real, -imag], axis=1), jnp.concatenate([imag, real], axis=1)], axis=0
    ).astype(BF)
    planes = dot(long_ref[...], sides, 1, 1).astype(BF)
    return dot(planes, depth_ref[...])


def run_rows(ref, y):
    return ref[:, :, LANES * y : LANES * (y + 1)].reshape(GROUP * XL, LANES)


def bypass_kernel(source_ref, mixer_ref, out_ref):
    for i in range(XL // XB):
        span = slice(i * XB, (i + 1) * XB)
        rows = source_ref[:, span, :].reshape(CH * XB, LANES)
        out_ref[:, span, :] = dot(mixer_ref[...], rows).reshape(CH, XB, LANES).astype(BF)


def start_kernel(
    where_ref, field_ref, strip_ref, wide_ref, o0, o1, o2, o3, depth_ref, tall_ref, long_ref
):
    @pl.when(pl.program_id(0) == 0)
    def _():
        fill_tables(strip_ref, wide_ref, depth_ref, tall_ref, long_ref)

    for y in range(STEPS):
        forward_group(run_rows(field_ref, y), depth_ref, tall_ref, (o0, o1, o2, o3), y)


ROOT = math.sqrt(2.0 / math.pi)
CUBE = 0.044715


def activate(bias_ref, upstream_ref, total_ref, act_ref, grad_ref, y):
    lanes = slice(LANES * y, LANES * (y + 1))
    for channel in range(GROUP):
        shift = bias_ref[GROUP * pl.program_id(0) + channel]
        for i in range(XL // EB):
            span = slice(i * EB, (i + 1) * EB)
            x = total_ref[y, channel, span, :] + shift
            square = x * x
            t = jnp.tanh(x * (ROOT + (ROOT * CUBE) * square))
            h = 0.5 * t + 0.5
            act = x * h
            slope = h + act * (1.0 - h) * (2.0 * ROOT + (6.0 * ROOT * CUBE) * square)
            act_ref[channel, span, lanes] = act.astype(BF)
            up = upstream_ref[channel, span, lanes].astype(F32)
            grad_ref[channel, span, lanes] = (up * slope).astype(BF)


def middle_kernel(
    where_ref, bias_ref, i0, i1, i2, i3, bypass_ref, upstream_ref, strip_ref, wide_ref,
    act_ref, grad_ref, o0, o1, o2, o3, depth_ref, tall_ref, long_ref, total_ref,
):
    @pl.when(pl.program_id(0) == 0)
    def _():
        fill_tables(strip_ref, wide_ref, depth_ref, tall_ref, long_ref)

    def inverse(y):
        values = inverse_group((i0, i1, i2, i3), depth_ref, long_ref, y)
        lanes = slice(LANES * y, LANES * (y + 1))
        total_ref[y] = bypass_ref[:, :, lanes].astype(F32) + values.reshape(GROUP, XL, LANES)

    def forward(y):
        forward_group(run_rows(grad_ref, y), depth_ref, tall_ref, (o0, o1, o2, o3), y)

    inverse(0)
    for y in range(STEPS):
        if y + 1 < STEPS:
            inverse(y + 1)
        activate(bias_ref, upstream_ref, total_ref, act_ref, grad_ref, y)
        if y > 0:
            forward(y - 1)
    forward(STEPS - 1)


def end_kernel(
    where_ref, i0, i1, i2, i3, bypass_ref, strip_ref, wide_ref, out_ref,
    depth_ref, tall_ref, long_ref,
):
    @pl.when(pl.program_id(0) == 0)
    def _():
        fill_tables(strip_ref, wide_ref, depth_ref, tall_ref, long_ref)

    for y in range(STEPS):
        values = inverse_group((i0, i1, i2, i3), depth_ref, long_ref, y)
        lanes = slice(LANES * y, LANES * (y + 1))
        out_ref[:, :, lanes] = (
            bypass_ref[:, :, lanes].astype(F32) + values.reshape(GROUP, XL, LANES)
        ).astype(BF)


def cost(micros):
    return pl.CostEstimate(flops=0, bytes_accessed=micros * 3_000_000, transcendentals=0)


def column_specs():
    columns = pl.BlockSpec((GROUP, XL, YL * NZ), lambda j, w: (j, 0, 0))
    coeffs = pl.BlockSpec((STEPS, ROWS, GL), lambda j, w: (0, 0, j))
    depth = pl.BlockSpec((1, 2 * KZ, LANES), lambda j, w: (w[1], 0, 0))
    wide = pl.BlockSpec((1, 2, XL, KX), lambda j, w: (w[1], 0, 0, 0))
    return columns, coeffs, depth, wide


COEFFS = jax.ShapeDtypeStruct((STEPS, ROWS, WIDE), BF)
COLUMNS = jax.ShapeDtypeStruct((CH, XL, YL * NZ), BF)
BLOCKS = [
    pltpu.VMEM((2 * KZ * YB, LANES), BF),
    pltpu.VMEM((2 * GL, GL), BF),
    pltpu.VMEM((GL, 2 * GL), BF),
]
TOTAL = pltpu.VMEM((STEPS, GROUP, XL, LANES), F32)
PARAMS = pltpu.CompilerParams(vmem_limit_bytes=56 * 1024 * 1024)
ALONE = pltpu.CompilerParams(vmem_limit_bytes=63 * 1024 * 1024)


def bypass_columns(source, mixer):
    columns = pl.BlockSpec((CH, XL, LANES), lambda i: (0, 0, i))
    return pl.pallas_call(
        bypass_kernel,
        grid=(STEPS,),
        in_specs=[columns, pl.BlockSpec((CH * XB, CH * XB), lambda i: (0, 0))],
        out_specs=columns,
        out_shape=COLUMNS,
        compiler_params=PARAMS,
        cost_estimate=cost(6),
        name="bypass_columns",
    )(source, mixer)


def start_columns(where, field):
    columns, coeffs, depth, wide = column_specs()
    return pl.pallas_call(
        start_kernel,
        grid_spec=pltpu.PrefetchScalarGridSpec(
            num_scalar_prefetch=1,
            grid=(GROUPS,),
            in_specs=[columns, depth, wide],
            out_specs=[coeffs] * 4,
            scratch_shapes=BLOCKS,
        ),
        out_shape=[COEFFS] * 4,
        compiler_params=PARAMS,
        cost_estimate=cost(8),
        name="start_columns",
    )(where, field, jnp.asarray(DEPTH), jnp.asarray(WIDTH))


def middle_columns(where, bias, coeffs_in, bypass, upstream):
    columns, coeffs, depth, wide = column_specs()
    return pl.pallas_call(
        middle_kernel,
        grid_spec=pltpu.PrefetchScalarGridSpec(
            num_scalar_prefetch=1,
            grid=(GROUPS,),
            in_specs=[pl.BlockSpec(memory_space=pltpu.SMEM)]
            + [coeffs] * 4
            + [columns, columns, depth, wide],
            out_specs=[columns, columns] + [coeffs] * 4,
            scratch_shapes=BLOCKS + [TOTAL],
        ),
        out_shape=[COLUMNS, COLUMNS] + [COEFFS] * 4,
        compiler_params=PARAMS,
        cost_estimate=cost(19),
        name="middle_columns",
    )(where, bias, *coeffs_in, bypass, upstream, jnp.asarray(DEPTH), jnp.asarray(WIDTH))


def end_columns(where, coeffs_in, bypass):
    columns, coeffs, depth, wide = column_specs()
    return pl.pallas_call(
        end_kernel,
        grid_spec=pltpu.PrefetchScalarGridSpec(
            num_scalar_prefetch=1,
            grid=(GROUPS,),
            in_specs=[coeffs] * 4 + [columns, depth, wide],
            out_specs=columns,
            scratch_shapes=BLOCKS,
        ),
        out_shape=COLUMNS,
        compiler_params=PARAMS,
        cost_estimate=cost(10),
        name="end_columns",
    )(where, *coeffs_in, bypass, jnp.asarray(DEPTH), jnp.asarray(WIDTH))


def line_kernel(where_ref, a_ref, b_ref, c_ref, table_ref, out_ref):
    for j in range(GROUPS):
        lanes = slice(GL * j, GL * (j + 1))
        parts = [ref[:, :, lanes].astype(F32) for ref in (a_ref, b_ref, c_ref)]
        rows = (parts[0] + parts[1] + parts[2]).astype(BF).reshape(STEPS * ROWS, GL)
        out_ref[:, :, lanes] = dot(table_ref[0], rows).astype(BF).reshape(GY, 48, GL)


def unline_kernel(where_ref, *refs):
    *modes_refs, table_ref, out_ref, order_ref = refs
    for k in range(GY):
        owner = ((where_ref[2] + (k & 6)) & 7) ^ (k & 1)
        start = pl.multiple_of(owner * 48, 16)
        order_ref[48 * k : 48 * (k + 1)] = table_ref[0, pl.ds(start, 48), :]
    for j in range(GROUPS):
        lanes = slice(GL * j, GL * (j + 1))
        rows = jnp.concatenate([ref[:, lanes] for ref in modes_refs], axis=0)
        out_ref[:, :, lanes] = dot(order_ref[...], rows, 0, 0).astype(BF).reshape(STEPS, ROWS, GL)


def line_call(kernel, name, where, ins, out_shape, scratch=()):
    whole = pl.BlockSpec(ins[0].shape, lambda i, w: (0,) * ins[0].ndim)
    table = pl.BlockSpec((1, GY * 48, STEPS * ROWS), lambda i, w: (w[2], 0, 0))
    return pl.pallas_call(
        kernel,
        grid_spec=pltpu.PrefetchScalarGridSpec(
            num_scalar_prefetch=1,
            grid=(1,),
            in_specs=[whole] * len(ins) + [table],
            out_specs=pl.BlockSpec(out_shape.shape, lambda i, w: (0, 0, 0)),
            scratch_shapes=list(scratch),
        ),
        out_shape=out_shape,
        compiler_params=ALONE,
        cost_estimate=cost(3),
        name=name,
    )(where, *ins, jnp.asarray(LINE))


def to_lines(where, *parts):
    out = jax.ShapeDtypeStruct((GY, 48, WIDE), BF)
    return line_call(line_kernel, "to_lines", where, parts, out)


def from_lines(where, modes):
    order = pltpu.VMEM((GY * 48, STEPS * ROWS), BF)
    return line_call(unline_kernel, "from_lines", where, modes, COEFFS, [order])


UNROLL = 4
SETS = GX * KB
PAIR = 2 * CH
HALF = KX


def low_lanes():
    return lax.broadcasted_iota(jnp.int32, (SETS, 2 * HALF), 1) < HALF


def gather_modes(arrived_ref, sum_ref, modes_ref, scale=None):
    total = arrived_ref[0].astype(F32)
    for i in range(1, GY):
        total = total + arrived_ref[i].astype(F32)
    sum_ref[...] = total.astype(BF).astype(F32)
    low = low_lanes()
    for j in range(CH // 2):
        lanes = slice(2 * HALF * j, 2 * HALF * (j + 1))
        for part in range(2):
            first = sum_ref[part * SETS : (part + 1) * SETS, lanes]
            second = sum_ref[(2 + part) * SETS : (3 + part) * SETS, lanes]
            if scale is not None:
                first = first * scale
                second = second * scale
            even = jnp.where(low, first, pltpu.roll(second, HALF, 1))
            odd = jnp.where(low, pltpu.roll(first, HALF, 1), second)
            modes_ref[pl.ds(4 * j + part, SETS, stride=PAIR), :] = even
            modes_ref[pl.ds(4 * j + 2 + part, SETS, stride=PAIR), :] = odd


def spread_modes(modes_ref, sum_ref, out_ref, scale=None):
    low = low_lanes()
    for j in range(CH // 2):
        lanes = slice(2 * HALF * j, 2 * HALF * (j + 1))
        for part in range(2):
            even = modes_ref[pl.ds(4 * j + part, SETS, stride=PAIR), :]
            odd = modes_ref[pl.ds(4 * j + 2 + part, SETS, stride=PAIR), :]
            if scale is not None:
                even = even * scale
                odd = odd * scale
            sum_ref[part * SETS : (part + 1) * SETS, lanes] = jnp.where(
                low, even, pltpu.roll(odd, HALF, 1)
            )
            sum_ref[(2 + part) * SETS : (3 + part) * SETS, lanes] = jnp.where(
                low, pltpu.roll(even, HALF, 1), odd
            )
    out_ref[...] = sum_ref[...].astype(BF)


def fold_scale(where_ref):
    kz = where_ref[1] * KB + lax.broadcasted_iota(jnp.int32, (SETS, 2 * HALF), 0) % KB
    return jnp.where(kz == 0, 1.0, 2.0).astype(F32) / float(NX * NY * NZ)


def turned(rows):
    even = lax.broadcasted_iota(jnp.int32, rows.shape, 0) % 2 == 0
    up = pltpu.roll(rows, PAIR - 1, 0)
    down = pltpu.roll(rows, 1, 0)
    return jnp.where(even, -up, down)


def hand_out(where_ref, modes_ref, outs):
    for k in range(DP):
        chunk = lax.rem(where_ref[0] + k, DP)
        start = pl.multiple_of(chunk * KB * PAIR, 8)
        outs[k][...] = modes_ref[pl.ds(start, KB * PAIR), :].astype(BF)


def set_row(where_ref, k):
    block = (lax.rem(where_ref[0] + k, DP) ^ (2 * (where_ref[1] & 1))) * KB + pl.program_id(0)
    return pl.multiple_of(block * PAIR, 8)


def mix_kernel(
    where_ref, arrived_ref, w0, w1, w2, w3, out_ref, u0, u1, u2, u3, sum_ref, in_ref, mix_ref
):
    step = pl.program_id(0)

    @pl.when(step == 0)
    def _():
        gather_modes(arrived_ref, sum_ref, in_ref)
        hand_out(where_ref, in_ref, (u0, u1, u2, u3))

    for k, weight_ref in enumerate((w0, w1, w2, w3)):
        base = set_row(where_ref, k)

        def add(i, totals, weight_ref=weight_ref, base=base):
            by_real, by_imag = totals
            for r in range(UNROLL):
                c = i * UNROLL + r
                weight = weight_ref[0, c].astype(F32)
                by_real = by_real + weight * in_ref[pl.ds(base + 2 * c, 1), :]
                by_imag = by_imag + weight * in_ref[pl.ds(base + 2 * c + 1, 1), :]
            return by_real, by_imag

        zero = jnp.zeros((PAIR, 2 * HALF), F32)
        by_real, by_imag = lax.fori_loop(0, CH // UNROLL, add, (zero, zero))
        mix_ref[pl.ds(base, PAIR), :] = (by_real + turned(by_imag)).astype(BF).astype(F32)

    @pl.when(step == KB - 1)
    def _():
        spread_modes(mix_ref, sum_ref, out_ref, fold_scale(where_ref))


def back_kernel(
    where_ref, arrived_ref, w0, w1, w2, w3, out_ref, u0, u1, u2, u3, sum_ref, in_ref, mix_ref
):
    step = pl.program_id(0)

    @pl.when(step == 0)
    def _():
        gather_modes(arrived_ref, sum_ref, in_ref, fold_scale(where_ref))
        hand_out(where_ref, in_ref, (u0, u1, u2, u3))

    for k, weight_ref in enumerate((w0, w1, w2, w3)):
        base = set_row(where_ref, k)
        grad = in_ref[pl.ds(base, PAIR), :]
        other = -turned(grad)

        @pl.loop(0, CH // UNROLL)
        def _(i, weight_ref=weight_ref, base=base, grad=grad, other=other):
            for r in range(UNROLL):
                c = i * UNROLL + r
                weight = weight_ref[0, c].astype(F32)
                mix_ref[pl.ds(base + 2 * c, 1), :] = jnp.sum(weight * grad, axis=0, keepdims=True)
                mix_ref[pl.ds(base + 2 * c + 1, 1), :] = jnp.sum(
                    weight * other, axis=0, keepdims=True
                )

    @pl.when(step == KB - 1)
    def _():
        spread_modes(mix_ref, sum_ref, out_ref)


def mode_call(kernel, name, where, arrived, weights):
    chunk = pl.BlockSpec((KB * PAIR, 2 * HALF), lambda i, w: (0, 0))
    return pl.pallas_call(
        kernel,
        grid_spec=pltpu.PrefetchScalarGridSpec(
            num_scalar_prefetch=1,
            grid=(KB,),
            in_specs=[pl.BlockSpec((GY, 48, WIDE), lambda i, w: (0, 0, 0))]
            + [pl.BlockSpec((1, CH, PAIR, 2 * HALF), lambda i, w: (i, 0, 0, 0))] * 4,
            out_specs=[pl.BlockSpec((48, WIDE), lambda i, w: (0, 0))] + [chunk] * 4,
            scratch_shapes=[
                pltpu.VMEM((48, WIDE), F32),
                pltpu.VMEM((SETS * PAIR, 2 * HALF), F32),
                pltpu.VMEM((SETS * PAIR, 2 * HALF), F32),
            ],
        ),
        out_shape=[jax.ShapeDtypeStruct((48, WIDE), BF)]
        + [jax.ShapeDtypeStruct((KB * PAIR, 2 * HALF), BF)] * 4,
        compiler_params=ALONE,
        cost_estimate=cost(5),
        name=name,
    )(where, arrived, *weights)


def outer_kernel(s0, s1, s2, s3, g0, g1, g2, g3, out_ref, spec_ref):
    for k, ref in enumerate((s0, s1, s2, s3)):
        spec_ref[k] = ref[...].astype(F32)
    for i in range(KB):
        grads = []
        others = []
        for ref in (g0, g1, g2, g3):
            grad = ref[...].astype(F32)[i * PAIR : (i + 1) * PAIR]
            grads.append(grad)
            others.append(-turned(grad))

        @pl.loop(0, CH)
        def _(c):
            row = i * PAIR + 2 * c
            total = jnp.zeros((PAIR, 2 * HALF), F32)
            for k in range(DP):
                total = total + spec_ref[k, pl.ds(row, 1), :] * grads[k]
                total = total + spec_ref[k, pl.ds(row + 1, 1), :] * others[k]
            out_ref[i, c] = total


def outer_sum(spectra, grads):
    return pl.pallas_call(
        outer_kernel,
        out_shape=jax.ShapeDtypeStruct((KB, CH, PAIR, 2 * HALF), F32),
        scratch_shapes=[pltpu.VMEM((DP, KB * PAIR, 2 * HALF), F32)],
        cost_estimate=cost(3),
        name="outer_sum",
    )(*spectra, *grads)


def swap(values, bit):
    return lax.ppermute(values, "gx", [(i, i ^ bit) for i in range(GX)])


def start_slabs(pieces, beside):
    own, far, near, across = pieces
    far_sum = (far.astype(F32) + swap(across, 1).astype(F32)).astype(BF)
    arrived, beside = lax.optimization_barrier((swap(far_sum, 2), beside))
    return (own, swap(near, 1), arrived), beside


def share_slabs(own, *waiting):
    far = swap(own, 2)
    far, *waiting = lax.optimization_barrier((far, *waiting))
    return own, far, swap(own, 1), swap(far, 1), *waiting


def gather_weights(weight):
    held = [weight]
    for k in range(1, DP):
        held.append(lax.ppermute(weight, "dp", [((a + k) % DP, a) for a in range(DP)]))
    return [part.reshape(KB, CH, PAIR, 2 * HALF) for part in held]


def gather_lines(modes):
    held = [modes, lax.ppermute(modes, "gy", [(g ^ 1, g) for g in range(GY)])]
    for step in range(2, GY, 2):
        pairs = [((g + step) % GY, g) for g in range(GY)]
        held += [lax.ppermute(part, "gy", pairs) for part in held[:2]]
    return held


def exchange_lines(parts):
    return lax.all_to_all(parts, "gy", split_axis=0, concat_axis=0, tiled=True)


def to_owners(chunks):
    moved = []
    for k, chunk in enumerate(chunks):
        pairs = [
            (a * GX + b, b * GX + (a + k) % DP) for a in range(DP) for b in range(GX)
        ]
        moved.append(lax.ppermute(chunk, ("dp", "gx"), pairs))
    return moved


def per_device(field, spectral_weight, bypass_weight, bias, cotangent):
    where = jnp.stack(
        [lax.axis_index("dp"), lax.axis_index("gx"), lax.axis_index("gy")]
    ).astype(jnp.int32)
    turn = [(a * GX + b, (b ^ (2 * (a % 2))) * GX + a) for a in range(DP) for b in range(GX)]
    weight = lax.ppermute(spectral_weight, ("dp", "gx"), turn)
    spread = jnp.asarray(SPREAD)

    def mixer_of(matrix):
        wide = dot(dot(spread, matrix).astype(BF), spread, 1, 1)
        return wide.astype(BF) * jnp.asarray(SAME)

    values = field[0]
    *pieces, weight = lax.optimization_barrier((*start_columns(where, values), weight))
    parts, bypass = start_slabs(pieces, bypass_columns(values, mixer_of(bypass_weight)))
    weights = gather_weights(weight)
    lines, weights[1], weights[3] = lax.optimization_barrier(
        (to_lines(where, *parts), weights[1], weights[3])
    )
    arrived = exchange_lines(lines)
    modes, *spectra = mode_call(mix_kernel, "mix_modes", where, arrived, weights)
    own = from_lines(where, gather_lines(modes))
    *coeffs, s0, s1, s2, s3 = share_slabs(own, *to_owners(spectra))
    activation, grad, *pieces = middle_columns(where, bias, coeffs, bypass, cotangent[0])
    parts, bypass = start_slabs(pieces, bypass_columns(grad, mixer_of(bypass_weight.T)))
    arrived = exchange_lines(to_lines(where, *parts))
    modes, *grads = mode_call(back_kernel, "back_modes", where, arrived, weights)
    own = from_lines(where, gather_lines(modes))
    *coeffs, weight_grad = share_slabs(own, outer_sum((s0, s1, s2, s3), to_owners(grads)))
    field_grad = end_columns(where, coeffs, bypass)
    return (
        activation[None],
        field_grad[None],
        weight_grad.reshape(KB, CH, CH, 2, 2 * HALF),
    )


def solution(mesh):
    placed = (
        P("dp", None, "gx", "gy"),
        P("dp", None, None, None, ("gx", "gy")),
        P(),
        P(),
        P("dp", None, "gx", "gy"),
    )
    return jax.shard_map(
        per_device,
        mesh=mesh,
        in_specs=placed,
        out_specs=(
            P("dp", None, "gx", "gy"),
            P("dp", None, "gx", "gy"),
            P("dp", None, None, None, ("gx", "gy")),
        ),
        check_vma=False,
    )
```

```python
import functools
import math

import jax
import jax.numpy as jnp
import ml_dtypes
import numpy as np
from jax import lax
from jax.experimental import pallas as pl
from jax.experimental.pallas import tpu as pltpu
from jax.sharding import PartitionSpec as P

CH = 20
NX = 256
NY = 256
NZ = 64
KX = 64
KY = 64
KZ = 12
GX = 4
GY = 8
DP = 4
XL = NX // GX
YL = NY // GY
YB = 8
STEPS = YL // YB
LANES = YB * NZ
KB = KZ // GX
ROWS = 2 * KB * YB
GROUP = 4
GROUPS = CH // GROUP
GL = GROUP * KX
WIDE = CH * KX
XB = 8
EB = 16
ORDER = (0, 2, 1, 3)

BF = jnp.bfloat16
F32 = jnp.float32


def wave(freqs, points, length):
    offsets = np.mod(freqs[:, None] * points[None, :], length)
    angle = offsets.astype(np.float32) * np.float32(2.0 * math.pi / length)
    return np.cos(angle), np.sin(angle)


def kept(count):
    index = np.arange(count)
    return np.where(index < count // 2, index, index - count)


def depth_tables():
    out = np.zeros((GX, 2, GX, KB, LANES), np.float32)
    for b in range(GX):
        for pos, delta in enumerate(ORDER):
            freqs = (b ^ delta) * KB + np.arange(KB)
            cosine, sine = wave(freqs, np.arange(NZ), NZ)
            out[b, 0, pos] = np.tile(cosine, (1, YB))
            out[b, 1, pos] = np.tile(-sine, (1, YB))
    return out.reshape(GX, 2 * KZ, LANES).astype(ml_dtypes.bfloat16)


def width_tables():
    out = np.zeros((GX, 2, XL, KX), np.float32)
    for b in range(GX):
        cosine, sine = wave(kept(KX), b * XL + np.arange(XL), NX)
        out[b, 0] = cosine.T
        out[b, 1] = sine.T
    return out.astype(ml_dtypes.bfloat16)


def line_tables():
    out = np.zeros((GY, GY, 2, 2, GX, KB, STEPS, 2, KB, YB), np.float32)
    fy = kept(KY)
    for g in range(GY):
        cosine, sine = wave(fy, g * YL + np.arange(YL), NY)
        cosine = cosine.reshape(GX, GY, 2, STEPS, YB)
        sine = sine.reshape(GX, GY, 2, STEPS, YB)
        for i in range(KB):
            for owner in range(GY):
                for q in range(2):
                    c = cosine[:, owner, q]
                    s = sine[:, owner, q]
                    out[g, owner, q, 0, :, i, :, 0, i] = c
                    out[g, owner, q, 0, :, i, :, 1, i] = s
                    out[g, owner, q, 1, :, i, :, 0, i] = -s
                    out[g, owner, q, 1, :, i, :, 1, i] = c
    return out.reshape(GY, GY * 48, STEPS * ROWS).astype(ml_dtypes.bfloat16)


DEPTH = depth_tables()
WIDTH = width_tables()
LINE = line_tables()
SPREAD = np.kron(np.eye(CH), np.ones((XB, 1))).astype(ml_dtypes.bfloat16)
SAME = np.kron(np.ones((CH, CH)), np.eye(XB)).astype(ml_dtypes.bfloat16)


def dot(left, right, left_dim=1, right_dim=0):
    return lax.dot_general(
        left, right, (((left_dim,), (right_dim,)), ((), ())), preferred_element_type=F32
    )


def fill_tables(strip_ref, wide_ref, depth_ref, tall_ref, long_ref):
    strips = jnp.broadcast_to(strip_ref[0].astype(F32)[:, None, :], (2 * KZ, YB, LANES))
    row = lax.broadcasted_iota(jnp.int32, (2 * KZ, YB, LANES), 1)
    column = lax.broadcasted_iota(jnp.int32, (2 * KZ, YB, LANES), 2) // NZ
    blocks = jnp.where(row == column, strips, 0.0)
    depth_ref[...] = blocks.reshape(2 * KZ * YB, LANES).astype(BF)
    rows = lax.broadcasted_iota(jnp.int32, (GL, GL), 0) // XL
    columns = lax.broadcasted_iota(jnp.int32, (GL, GL), 1) // KX
    for part in range(2):
        strip = wide_ref[0, part].astype(F32)
        full = jnp.concatenate([jnp.concatenate([strip] * GROUP, axis=1)] * GROUP, axis=0)
        block = jnp.where(rows == columns, full, 0.0).astype(BF)
        tall_ref[GL * part : GL * (part + 1), :] = block
        long_ref[:, GL * part : GL * (part + 1)] = block


def forward_group(rows, depth_ref, tall_ref, outs, y):
    half = KZ * YB
    planes = dot(depth_ref[...], rows, 1, 1)
    real = planes[:half]
    imag = planes[half:]
    sides = jnp.concatenate(
        [jnp.concatenate([real, imag], axis=1), jnp.concatenate([imag, -real], axis=1)], axis=0
    ).astype(BF)
    lines = dot(sides, tall_ref[...])
    for pos in range(GX):
        lo = pos * KB * YB
        piece = jnp.concatenate(
            [lines[lo : lo + KB * YB], lines[half + lo : half + lo + KB * YB]], axis=0
        )
        outs[pos][y] = piece.astype(BF)


def inverse_group(ins, depth_ref, long_ref, y):
    part = KB * YB
    pieces = [ref[y].astype(F32) for ref in ins]
    real = jnp.concatenate([piece[:part] for piece in pieces], axis=0)
    imag = jnp.concatenate([piece[part:] for piece in pieces], axis=0)
    sides = jnp.concatenate(
        [jnp.concatenate([real, -imag], axis=1), jnp.concatenate([imag, real], axis=1)], axis=0
    ).astype(BF)
    planes = dot(long_ref[...], sides, 1, 1).astype(BF)
    return dot(planes, depth_ref[...])


def run_rows(ref, y):
    return ref[:, :, LANES * y : LANES * (y + 1)].reshape(GROUP * XL, LANES)


def bypass_kernel(source_ref, mixer_ref, out_ref):
    for i in range(XL // XB):
        span = slice(i * XB, (i + 1) * XB)
        rows = source_ref[:, span, :].reshape(CH * XB, LANES)
        out_ref[:, span, :] = dot(mixer_ref[...], rows).reshape(CH, XB, LANES).astype(BF)


def start_kernel(
    where_ref, field_ref, strip_ref, wide_ref, o0, o1, o2, o3, depth_ref, tall_ref, long_ref
):
    @pl.when(pl.program_id(0) == 0)
    def _():
        fill_tables(strip_ref, wide_ref, depth_ref, tall_ref, long_ref)

    for y in range(STEPS):
        forward_group(run_rows(field_ref, y), depth_ref, tall_ref, (o0, o1, o2, o3), y)


ROOT = math.sqrt(2.0 / math.pi)
CUBE = 0.044715


def activate(bias_ref, upstream_ref, total_ref, act_ref, grad_ref, y):
    lanes = slice(LANES * y, LANES * (y + 1))
    for channel in range(GROUP):
        shift = bias_ref[GROUP * pl.program_id(0) + channel]
        for i in range(XL // EB):
            span = slice(i * EB, (i + 1) * EB)
            x = total_ref[y, channel, span, :] + shift
            square = x * x
            t = jnp.tanh(x * (ROOT + (ROOT * CUBE) * square))
            h = 0.5 * t + 0.5
            act = x * h
            slope = h + act * (1.0 - h) * (2.0 * ROOT + (6.0 * ROOT * CUBE) * square)
            act_ref[channel, span, lanes] = act.astype(BF)
            up = upstream_ref[channel, span, lanes].astype(F32)
            grad_ref[channel, span, lanes] = (up * slope).astype(BF)


def middle_kernel(
    where_ref, bias_ref, i0, i1, i2, i3, bypass_ref, upstream_ref, strip_ref, wide_ref,
    act_ref, grad_ref, o0, o1, o2, o3, depth_ref, tall_ref, long_ref, total_ref,
):
    @pl.when(pl.program_id(0) == 0)
    def _():
        fill_tables(strip_ref, wide_ref, depth_ref, tall_ref, long_ref)

    def inverse(y):
        values = inverse_group((i0, i1, i2, i3), depth_ref, long_ref, y)
        lanes = slice(LANES * y, LANES * (y + 1))
        total_ref[y] = bypass_ref[:, :, lanes].astype(F32) + values.reshape(GROUP, XL, LANES)

    def forward(y):
        forward_group(run_rows(grad_ref, y), depth_ref, tall_ref, (o0, o1, o2, o3), y)

    inverse(0)
    for y in range(STEPS):
        if y + 1 < STEPS:
            inverse(y + 1)
        activate(bias_ref, upstream_ref, total_ref, act_ref, grad_ref, y)
        if y > 0:
            forward(y - 1)
    forward(STEPS - 1)


def end_kernel(
    where_ref, i0, i1, i2, i3, bypass_ref, strip_ref, wide_ref, out_ref,
    depth_ref, tall_ref, long_ref,
):
    @pl.when(pl.program_id(0) == 0)
    def _():
        fill_tables(strip_ref, wide_ref, depth_ref, tall_ref, long_ref)

    for y in range(STEPS):
        values = inverse_group((i0, i1, i2, i3), depth_ref, long_ref, y)
        lanes = slice(LANES * y, LANES * (y + 1))
        out_ref[:, :, lanes] = (
            bypass_ref[:, :, lanes].astype(F32) + values.reshape(GROUP, XL, LANES)
        ).astype(BF)


def cost(micros):
    return pl.CostEstimate(flops=0, bytes_accessed=micros * 3_000_000, transcendentals=0)


def column_specs():
    columns = pl.BlockSpec((GROUP, XL, YL * NZ), lambda j, w: (j, 0, 0))
    coeffs = pl.BlockSpec((STEPS, ROWS, GL), lambda j, w: (0, 0, j))
    depth = pl.BlockSpec((1, 2 * KZ, LANES), lambda j, w: (w[1], 0, 0))
    wide = pl.BlockSpec((1, 2, XL, KX), lambda j, w: (w[1], 0, 0, 0))
    return columns, coeffs, depth, wide


COEFFS = jax.ShapeDtypeStruct((STEPS, ROWS, WIDE), BF)
COLUMNS = jax.ShapeDtypeStruct((CH, XL, YL * NZ), BF)
BLOCKS = [
    pltpu.VMEM((2 * KZ * YB, LANES), BF),
    pltpu.VMEM((2 * GL, GL), BF),
    pltpu.VMEM((GL, 2 * GL), BF),
]
TOTAL = pltpu.VMEM((STEPS, GROUP, XL, LANES), F32)
PARAMS = pltpu.CompilerParams(vmem_limit_bytes=56 * 1024 * 1024)
ALONE = pltpu.CompilerParams(vmem_limit_bytes=63 * 1024 * 1024)


def bypass_columns(source, mixer):
    columns = pl.BlockSpec((CH, XL, LANES), lambda i: (0, 0, i))
    return pl.pallas_call(
        bypass_kernel,
        grid=(STEPS,),
        in_specs=[columns, pl.BlockSpec((CH * XB, CH * XB), lambda i: (0, 0))],
        out_specs=columns,
        out_shape=COLUMNS,
        compiler_params=PARAMS,
        cost_estimate=cost(6),
        name="bypass_columns",
    )(source, mixer)


def start_columns(where, field):
    columns, coeffs, depth, wide = column_specs()
    return pl.pallas_call(
        start_kernel,
        grid_spec=pltpu.PrefetchScalarGridSpec(
            num_scalar_prefetch=1,
            grid=(GROUPS,),
            in_specs=[columns, depth, wide],
            out_specs=[coeffs] * 4,
            scratch_shapes=BLOCKS,
        ),
        out_shape=[COEFFS] * 4,
        compiler_params=PARAMS,
        cost_estimate=cost(8),
        name="start_columns",
    )(where, field, jnp.asarray(DEPTH), jnp.asarray(WIDTH))


def middle_columns(where, bias, coeffs_in, bypass, upstream):
    columns, coeffs, depth, wide = column_specs()
    return pl.pallas_call(
        middle_kernel,
        grid_spec=pltpu.PrefetchScalarGridSpec(
            num_scalar_prefetch=1,
            grid=(GROUPS,),
            in_specs=[pl.BlockSpec(memory_space=pltpu.SMEM)]
            + [coeffs] * 4
            + [columns, columns, depth, wide],
            out_specs=[columns, columns] + [coeffs] * 4,
            scratch_shapes=BLOCKS + [TOTAL],
        ),
        out_shape=[COLUMNS, COLUMNS] + [COEFFS] * 4,
        compiler_params=PARAMS,
        cost_estimate=cost(19),
        name="middle_columns",
    )(where, bias, *coeffs_in, bypass, upstream, jnp.asarray(DEPTH), jnp.asarray(WIDTH))


def end_columns(where, coeffs_in, bypass):
    columns, coeffs, depth, wide = column_specs()
    return pl.pallas_call(
        end_kernel,
        grid_spec=pltpu.PrefetchScalarGridSpec(
            num_scalar_prefetch=1,
            grid=(GROUPS,),
            in_specs=[coeffs] * 4 + [columns, depth, wide],
            out_specs=columns,
            scratch_shapes=BLOCKS,
        ),
        out_shape=COLUMNS,
        compiler_params=PARAMS,
        cost_estimate=cost(10),
        name="end_columns",
    )(where, *coeffs_in, bypass, jnp.asarray(DEPTH), jnp.asarray(WIDTH))


def order_table(where_ref, table_ref, order_ref):
    for k in range(GY):
        owner = ((where_ref[2] + (k & 6)) & 7) ^ (k & 1)
        start = pl.multiple_of(owner * 48, 16)
        order_ref[48 * k : 48 * (k + 1)] = table_ref[0, pl.ds(start, 48), :]


def line_kernel(where_ref, a_ref, b_ref, c_ref, table_ref, o0, o1, o2, o3, order_ref):
    order_table(where_ref, table_ref, order_ref)
    for j in range(GROUPS):
        lanes = slice(GL * j, GL * (j + 1))
        parts = [ref[:, :, lanes].astype(F32) for ref in (a_ref, b_ref, c_ref)]
        rows = (parts[0] + parts[1] + parts[2]).astype(BF).reshape(STEPS * ROWS, GL)
        lines = dot(order_ref[...], rows).astype(BF)
        for k, out_ref in enumerate((o0, o1, o2, o3)):
            out_ref[:, :, lanes] = lines[96 * k : 96 * (k + 1)].reshape(2, 48, GL)


def unline_kernel(where_ref, *refs):
    *modes_refs, table_ref, out_ref, order_ref = refs
    order_table(where_ref, table_ref, order_ref)
    for j in range(GROUPS):
        lanes = slice(GL * j, GL * (j + 1))
        rows = jnp.concatenate([ref[:, lanes] for ref in modes_refs], axis=0)
        out_ref[:, :, lanes] = dot(order_ref[...], rows, 0, 0).astype(BF).reshape(STEPS, ROWS, GL)


def line_call(kernel, name, where, ins, out_shapes):
    whole = pl.BlockSpec(ins[0].shape, lambda i, w: (0,) * ins[0].ndim)
    table = pl.BlockSpec((1, GY * 48, STEPS * ROWS), lambda i, w: (w[2], 0, 0))
    return pl.pallas_call(
        kernel,
        grid_spec=pltpu.PrefetchScalarGridSpec(
            num_scalar_prefetch=1,
            grid=(1,),
            in_specs=[whole] * len(ins) + [table],
            out_specs=[pl.BlockSpec(out.shape, lambda i, w: (0, 0, 0)) for out in out_shapes],
            scratch_shapes=[pltpu.VMEM((GY * 48, STEPS * ROWS), BF)],
        ),
        out_shape=out_shapes,
        compiler_params=ALONE,
        cost_estimate=cost(3),
        name=name,
    )(where, *ins, jnp.asarray(LINE))


def to_lines(where, *parts):
    out = jax.ShapeDtypeStruct((2, 48, WIDE), BF)
    return line_call(line_kernel, "to_lines", where, parts, [out] * 4)


def from_lines(where, modes):
    return line_call(unline_kernel, "from_lines", where, modes, [COEFFS])[0]


UNROLL = 4
SETS = GX * KB
PAIR = 2 * CH
HALF = KX


def low_lanes():
    return lax.broadcasted_iota(jnp.int32, (SETS, 2 * HALF), 1) < HALF


def gather_modes(arrived, sum_ref, modes_ref, scale=None):
    *sets, last_ref = arrived
    total = last_ref[...].astype(F32)
    for ref in sets:
        total = total + ref[0].astype(F32)
    sum_ref[...] = total.astype(BF).astype(F32)
    low = low_lanes()
    for j in range(CH // 2):
        lanes = slice(2 * HALF * j, 2 * HALF * (j + 1))
        for part in range(2):
            first = sum_ref[part * SETS : (part + 1) * SETS, lanes]
            second = sum_ref[(2 + part) * SETS : (3 + part) * SETS, lanes]
            if scale is not None:
                first = first * scale
                second = second * scale
            even = jnp.where(low, first, pltpu.roll(second, HALF, 1))
            odd = jnp.where(low, pltpu.roll(first, HALF, 1), second)
            modes_ref[pl.ds(4 * j + part, SETS, stride=PAIR), :] = even
            modes_ref[pl.ds(4 * j + 2 + part, SETS, stride=PAIR), :] = odd


def spread_modes(modes_ref, sum_ref, out_ref, scale=None):
    low = low_lanes()
    for j in range(CH // 2):
        lanes = slice(2 * HALF * j, 2 * HALF * (j + 1))
        for part in range(2):
            even = modes_ref[pl.ds(4 * j + part, SETS, stride=PAIR), :]
            odd = modes_ref[pl.ds(4 * j + 2 + part, SETS, stride=PAIR), :]
            if scale is not None:
                even = even * scale
                odd = odd * scale
            sum_ref[part * SETS : (part + 1) * SETS, lanes] = jnp.where(
                low, even, pltpu.roll(odd, HALF, 1)
            )
            sum_ref[(2 + part) * SETS : (3 + part) * SETS, lanes] = jnp.where(
                low, pltpu.roll(even, HALF, 1), odd
            )
    out_ref[...] = sum_ref[...].astype(BF)


def fold_scale(where_ref):
    kz = where_ref[1] * KB + lax.broadcasted_iota(jnp.int32, (SETS, 2 * HALF), 0) % KB
    return jnp.where(kz == 0, 1.0, 2.0).astype(F32) / float(NX * NY * NZ)


def turned(rows):
    even = lax.broadcasted_iota(jnp.int32, rows.shape, 0) % 2 == 0
    up = pltpu.roll(rows, PAIR - 1, 0)
    down = pltpu.roll(rows, 1, 0)
    return jnp.where(even, -up, down)


def hand_out(where_ref, modes_ref, outs):
    for k in range(DP):
        chunk = lax.rem(where_ref[0] + k, DP)
        start = pl.multiple_of(chunk * KB * PAIR, 8)
        outs[k][...] = modes_ref[pl.ds(start, KB * PAIR), :].astype(BF)


def set_row(where_ref, k):
    block = (lax.rem(where_ref[0] + k, DP) ^ (2 * (where_ref[1] & 1))) * KB + pl.program_id(0)
    return pl.multiple_of(block * PAIR, 8)


def mix_kernel(
    where_ref, a0, a1, a2, a3, a4, w0, w1, w2, w3, out_ref, u0, u1, u2, u3,
    sum_ref, in_ref, mix_ref,
):
    step = pl.program_id(0)

    @pl.when(step == 0)
    def _():
        gather_modes((a0, a1, a2, a3, a4), sum_ref, in_ref)
        hand_out(where_ref, in_ref, [ref.at[0] for ref in (u0, u1, u2, u3)])

    for k, weight_ref in enumerate((w0, w1, w2, w3)):
        base = set_row(where_ref, k)

        def add(i, totals, weight_ref=weight_ref, base=base):
            by_real, by_imag = totals
            for r in range(UNROLL):
                c = i * UNROLL + r
                weight = weight_ref[0, c].astype(F32)
                by_real = by_real + weight * in_ref[pl.ds(base + 2 * c, 1), :]
                by_imag = by_imag + weight * in_ref[pl.ds(base + 2 * c + 1, 1), :]
            return by_real, by_imag

        zero = jnp.zeros((PAIR, 2 * HALF), F32)
        by_real, by_imag = lax.fori_loop(0, CH // UNROLL, add, (zero, zero))
        mix_ref[pl.ds(base, PAIR), :] = (by_real + turned(by_imag)).astype(BF).astype(F32)

    @pl.when(step == KB - 1)
    def _():
        spread_modes(mix_ref, sum_ref, out_ref, fold_scale(where_ref))


def back_kernel(
    where_ref, a0, a1, a2, a3, a4, w0, w1, w2, w3, s0, s1, s2, s3, out_ref, u0, u1, u2, u3,
    sum_ref, in_ref, mix_ref,
):
    step = pl.program_id(0)

    @pl.when(step == 0)
    def _():
        gather_modes((a0, a1, a2, a3, a4), sum_ref, in_ref, fold_scale(where_ref))
        hand_out(where_ref, in_ref, [ref.at[1] for ref in (u0, u1, u2, u3)])
        for spec_ref, ref in zip((s0, s1, s2, s3), (u0, u1, u2, u3)):
            ref[0] = spec_ref[0]

    for k, weight_ref in enumerate((w0, w1, w2, w3)):
        base = set_row(where_ref, k)
        grad = in_ref[pl.ds(base, PAIR), :]
        other = -turned(grad)

        @pl.loop(0, CH // UNROLL)
        def _(i, weight_ref=weight_ref, base=base, grad=grad, other=other):
            for r in range(UNROLL):
                c = i * UNROLL + r
                weight = weight_ref[0, c].astype(F32)
                mix_ref[pl.ds(base + 2 * c, 1), :] = jnp.sum(weight * grad, axis=0, keepdims=True)
                mix_ref[pl.ds(base + 2 * c + 1, 1), :] = jnp.sum(
                    weight * other, axis=0, keepdims=True
                )

    @pl.when(step == KB - 1)
    def _():
        spread_modes(mix_ref, sum_ref, out_ref)


def mode_call(kernel, name, where, arrived, weights, spectra=()):
    sets = 2 if spectra else 1

    def chunk(n):
        return pl.BlockSpec((n, KB * PAIR, 2 * HALF), lambda i, w: (0, 0, 0))

    return pl.pallas_call(
        kernel,
        grid_spec=pltpu.PrefetchScalarGridSpec(
            num_scalar_prefetch=1,
            grid=(KB,),
            in_specs=[pl.BlockSpec((1, 48, WIDE), lambda i, w: (0, 0, 0))] * 4
            + [pl.BlockSpec((48, WIDE), lambda i, w: (0, 0))]
            + [pl.BlockSpec((1, CH, PAIR, 2 * HALF), lambda i, w: (i, 0, 0, 0))] * 4
            + [chunk(1)] * len(spectra),
            out_specs=[pl.BlockSpec((48, WIDE), lambda i, w: (0, 0))] + [chunk(sets)] * 4,
            scratch_shapes=[
                pltpu.VMEM((48, WIDE), F32),
                pltpu.VMEM((SETS * PAIR, 2 * HALF), F32),
                pltpu.VMEM((SETS * PAIR, 2 * HALF), F32),
            ],
        ),
        out_shape=[jax.ShapeDtypeStruct((48, WIDE), BF)]
        + [jax.ShapeDtypeStruct((sets, KB * PAIR, 2 * HALF), BF)] * 4,
        compiler_params=ALONE,
        cost_estimate=cost(5),
        name=name,
    )(where, *arrived, *weights, *spectra)


def outer_kernel(p0, p1, p2, p3, out_ref, spec_ref):
    pairs = (p0, p1, p2, p3)
    for k, ref in enumerate(pairs):
        spec_ref[k] = ref[0].astype(F32)
    for i in range(KB):
        grads = []
        others = []
        for ref in pairs:
            grad = ref[1].astype(F32)[i * PAIR : (i + 1) * PAIR]
            grads.append(grad)
            others.append(-turned(grad))

        @pl.loop(0, CH)
        def _(c):
            row = i * PAIR + 2 * c
            total = jnp.zeros((PAIR, 2 * HALF), F32)
            for k in range(DP):
                total = total + spec_ref[k, pl.ds(row, 1), :] * grads[k]
                total = total + spec_ref[k, pl.ds(row + 1, 1), :] * others[k]
            out_ref[i, c] = total


def outer_sum(pairs):
    return pl.pallas_call(
        outer_kernel,
        out_shape=jax.ShapeDtypeStruct((KB, CH, PAIR, 2 * HALF), F32),
        scratch_shapes=[pltpu.VMEM((DP, KB * PAIR, 2 * HALF), F32)],
        cost_estimate=cost(3),
        name="outer_sum",
    )(*pairs)


def swap(values, bit):
    return lax.ppermute(values, "gx", [(i, i ^ bit) for i in range(GX)])


def start_slabs(pieces, beside):
    own, far, near, across = pieces
    far_sum = (far.astype(F32) + swap(across, 1).astype(F32)).astype(BF)
    arrived, beside = lax.optimization_barrier((swap(far_sum, 2), beside))
    return (own, swap(near, 1), arrived), beside


def share_slabs(own, *beside):
    far, *beside = lax.optimization_barrier((swap(own, 2), *beside))
    return own, far, swap(own, 1), swap(far, 1), *beside


def gather_weights(weight):
    held = [weight]
    for k in range(1, DP):
        held.append(lax.ppermute(weight, "dp", [((a + k) % DP, a) for a in range(DP)]))
    return [part.reshape(KB, CH, PAIR, 2 * HALF) for part in held]


def gather_lines(modes):
    held = [modes, lax.ppermute(modes, "gy", [(g ^ 1, g) for g in range(GY)])]
    for step in range(2, GY, 2):
        pairs = [((g + step) % GY, g) for g in range(GY)]
        held += [lax.ppermute(part, "gy", pairs) for part in held[:2]]
    return held


def sum_lines(sets, *waiting):
    moved = [sets[0]]
    for k in range(1, 4):
        pairs = [(g, (g + 2 * k) % GY) for g in range(GY)]
        moved.append(lax.ppermute(sets[k], "gy", pairs))
    other = sum(part[1].astype(F32) for part in moved).astype(BF)
    other, *waiting = lax.optimization_barrier((other, *waiting))
    other = lax.ppermute(other, "gy", [(g ^ 1, g) for g in range(GY)])
    return (*moved, other), waiting


def to_owners(chunks):
    moved = []
    for k, chunk in enumerate(chunks):
        pairs = [
            (a * GX + b, b * GX + (a + k) % DP) for a in range(DP) for b in range(GX)
        ]
        moved.append(lax.ppermute(chunk, ("dp", "gx"), pairs))
    return moved


def per_device(field, spectral_weight, bypass_weight, bias, cotangent):
    where = jnp.stack(
        [lax.axis_index("dp"), lax.axis_index("gx"), lax.axis_index("gy")]
    ).astype(jnp.int32)
    turn = [(a * GX + b, (b ^ (2 * (a % 2))) * GX + a) for a in range(DP) for b in range(GX)]
    weight = lax.ppermute(spectral_weight, ("dp", "gx"), turn)
    spread = jnp.asarray(SPREAD)

    def mixer_of(matrix):
        wide = dot(dot(spread, matrix).astype(BF), spread, 1, 1)
        return wide.astype(BF) * jnp.asarray(SAME)

    values = field[0]
    *pieces, weight = lax.optimization_barrier((*start_columns(where, values), weight))
    parts, bypass = start_slabs(pieces, bypass_columns(values, mixer_of(bypass_weight)))
    weights = gather_weights(weight)
    *sets, weights[1], weights[3] = lax.optimization_barrier(
        (*to_lines(where, *parts), weights[1], weights[3])
    )
    arrived, (weights[2],) = sum_lines(sets, weights[2])
    modes, *spectra = mode_call(mix_kernel, "mix_modes", where, arrived, weights)
    coeffs = share_slabs(from_lines(where, gather_lines(modes)))
    activation, grad, *pieces = middle_columns(where, bias, coeffs, bypass, cotangent[0])
    parts, bypass = start_slabs(pieces, bypass_columns(grad, mixer_of(bypass_weight.T)))
    arrived, _ = sum_lines(to_lines(where, *parts))
    modes, *pairs = mode_call(back_kernel, "back_modes", where, arrived, weights, spectra)
    own = from_lines(where, gather_lines(modes))
    own, far, near, across, *pairs = share_slabs(own, *to_owners(pairs))
    across, weight_grad = lax.optimization_barrier((across, outer_sum(pairs)))
    field_grad = end_columns(where, (own, far, near, across), bypass)
    return (
        activation[None],
        field_grad[None],
        weight_grad.reshape(KB, CH, CH, 2, 2 * HALF),
    )


def solution(mesh):
    placed = (
        P("dp", None, "gx", "gy"),
        P("dp", None, None, None, ("gx", "gy")),
        P(),
        P(),
        P("dp", None, "gx", "gy"),
    )
    return jax.shard_map(
        per_device,
        mesh=mesh,
        in_specs=placed,
        out_specs=(
            P("dp", None, "gx", "gy"),
            P("dp", None, "gx", "gy"),
            P("dp", None, None, None, ("gx", "gy")),
        ),
        check_vma=False,
    )
```

```python
import functools
import math

import jax
import jax.numpy as jnp
import ml_dtypes
import numpy as np
from jax import lax
from jax.experimental import pallas as pl
from jax.experimental.pallas import tpu as pltpu
from jax.sharding import PartitionSpec as P

CH = 20
NX = 256
NY = 256
NZ = 64
KX = 64
KY = 64
KZ = 12
GX = 4
GY = 8
DP = 4
XL = NX // GX
YL = NY // GY
YB = 8
STEPS = YL // YB
LANES = YB * NZ
KB = KZ // GX
ROWS = 2 * KB * YB
GROUP = 4
GROUPS = CH // GROUP
GL = GROUP * KX
WIDE = CH * KX
XB = 8
EB = 16
ORDER = (0, 2, 1, 3)

BF = jnp.bfloat16
F32 = jnp.float32


def wave(freqs, points, length):
    offsets = np.mod(freqs[:, None] * points[None, :], length)
    angle = offsets.astype(np.float32) * np.float32(2.0 * math.pi / length)
    return np.cos(angle), np.sin(angle)


def kept(count):
    index = np.arange(count)
    return np.where(index < count // 2, index, index - count)


def depth_tables():
    out = np.zeros((GX, 2, GX, KB, LANES), np.float32)
    for b in range(GX):
        for pos, delta in enumerate(ORDER):
            freqs = (b ^ delta) * KB + np.arange(KB)
            cosine, sine = wave(freqs, np.arange(NZ), NZ)
            out[b, 0, pos] = np.tile(cosine, (1, YB))
            out[b, 1, pos] = np.tile(-sine, (1, YB))
    return out.reshape(GX, 2 * KZ, LANES).astype(ml_dtypes.bfloat16)


def width_tables():
    out = np.zeros((GX, 2, XL, KX), np.float32)
    for b in range(GX):
        cosine, sine = wave(kept(KX), b * XL + np.arange(XL), NX)
        out[b, 0] = cosine.T
        out[b, 1] = sine.T
    return out.astype(ml_dtypes.bfloat16)


def line_tables():
    out = np.zeros((GY, GY, 2, 2, GX, KB, STEPS, 2, KB, YB), np.float32)
    fy = kept(KY)
    for g in range(GY):
        cosine, sine = wave(fy, g * YL + np.arange(YL), NY)
        cosine = cosine.reshape(GX, GY, 2, STEPS, YB)
        sine = sine.reshape(GX, GY, 2, STEPS, YB)
        for i in range(KB):
            for owner in range(GY):
                for q in range(2):
                    c = cosine[:, owner, q]
                    s = sine[:, owner, q]
                    out[g, owner, q, 0, :, i, :, 0, i] = c
                    out[g, owner, q, 0, :, i, :, 1, i] = s
                    out[g, owner, q, 1, :, i, :, 0, i] = -s
                    out[g, owner, q, 1, :, i, :, 1, i] = c
    return out.reshape(GY, GY * 48, STEPS * ROWS).astype(ml_dtypes.bfloat16)


DEPTH = depth_tables()
WIDTH = width_tables()
LINE = line_tables()
SPREAD = np.kron(np.eye(CH), np.ones((XB, 1))).astype(ml_dtypes.bfloat16)
SAME = np.kron(np.ones((CH, CH)), np.eye(XB)).astype(ml_dtypes.bfloat16)


def dot(left, right, left_dim=1, right_dim=0):
    return lax.dot_general(
        left, right, (((left_dim,), (right_dim,)), ((), ())), preferred_element_type=F32
    )


def fill_tables(strip_ref, wide_ref, depth_ref, tall_ref, long_ref):
    strips = jnp.broadcast_to(strip_ref[0].astype(F32)[:, None, :], (2 * KZ, YB, LANES))
    row = lax.broadcasted_iota(jnp.int32, (2 * KZ, YB, LANES), 1)
    column = lax.broadcasted_iota(jnp.int32, (2 * KZ, YB, LANES), 2) // NZ
    blocks = jnp.where(row == column, strips, 0.0)
    depth_ref[...] = blocks.reshape(2 * KZ * YB, LANES).astype(BF)
    rows = lax.broadcasted_iota(jnp.int32, (GL, GL), 0) // XL
    columns = lax.broadcasted_iota(jnp.int32, (GL, GL), 1) // KX
    for part in range(2):
        strip = wide_ref[0, part].astype(F32)
        full = jnp.concatenate([jnp.concatenate([strip] * GROUP, axis=1)] * GROUP, axis=0)
        block = jnp.where(rows == columns, full, 0.0).astype(BF)
        tall_ref[GL * part : GL * (part + 1), :] = block
        long_ref[:, GL * part : GL * (part + 1)] = block


def forward_runs(source_ref, depth_ref, tall_ref, outs, runs):
    half = KZ * YB
    part = KB * YB
    sides = []
    for y in runs:
        planes = dot(depth_ref[...], run_rows(source_ref, y), 1, 1)
        real = planes[:half]
        imag = planes[half:]
        sides.append(jnp.concatenate([real, imag], axis=1).astype(BF))
        sides.append(jnp.concatenate([imag, -real], axis=1).astype(BF))
    lines = dot(jnp.concatenate(sides, axis=0), tall_ref[...])
    for n, y in enumerate(runs):
        for pos in range(GX):
            lo = 2 * half * n + pos * part
            piece = jnp.concatenate(
                [lines[lo : lo + part], lines[half + lo : half + lo + part]], axis=0
            )
            outs[pos][y] = piece.astype(BF)


def inverse_group(ins, depth_ref, long_ref, y):
    part = KB * YB
    pieces = [ref[y].astype(F32) for ref in ins]
    real = jnp.concatenate([piece[:part] for piece in pieces], axis=0)
    imag = jnp.concatenate([piece[part:] for piece in pieces], axis=0)
    sides = jnp.concatenate(
        [jnp.concatenate([real, -imag], axis=1), jnp.concatenate([imag, real], axis=1)], axis=0
    ).astype(BF)
    planes = dot(long_ref[...], sides, 1, 1).astype(BF)
    return dot(planes, depth_ref[...])


def run_rows(ref, y):
    return ref[:, :, LANES * y : LANES * (y + 1)].reshape(GROUP * XL, LANES)


def bypass_kernel(shift_ref, source_ref, mixer_ref, out_ref):
    for i in range(XL // XB):
        span = slice(i * XB, (i + 1) * XB)
        rows = source_ref[:, span, :].reshape(CH * XB, LANES)
        mixed = dot(mixer_ref[...], rows).reshape(CH, XB, LANES)
        for channel in range(CH):
            out_ref[channel, span, :] = (mixed[channel] + shift_ref[channel]).astype(BF)


def start_kernel(
    where_ref, field_ref, strip_ref, wide_ref, o0, o1, o2, o3, depth_ref, tall_ref, long_ref
):
    @pl.when(pl.program_id(0) == 0)
    def _():
        fill_tables(strip_ref, wide_ref, depth_ref, tall_ref, long_ref)

    forward_runs(field_ref, depth_ref, tall_ref, (o0, o1, o2, o3), range(STEPS))


ROOT = math.sqrt(2.0 / math.pi)
CUBE = 0.044715


def activate(upstream_ref, total_ref, act_ref, grad_ref, y):
    lanes = slice(LANES * y, LANES * (y + 1))
    for channel in range(GROUP):
        for i in range(XL // EB):
            span = slice(i * EB, (i + 1) * EB)
            x = total_ref[y, channel, span, :]
            square = x * x
            t = jnp.tanh(x * (ROOT + (ROOT * CUBE) * square))
            h = 0.5 * t + 0.5
            act = x * h
            slope = h + act * (1.0 - h) * (2.0 * ROOT + (6.0 * ROOT * CUBE) * square)
            act_ref[channel, span, lanes] = act.astype(BF)
            grad_ref[channel, span, lanes] = upstream_ref[channel, span, lanes] * slope.astype(BF)


def middle_kernel(
    where_ref, i0, i1, i2, i3, bypass_ref, upstream_ref, strip_ref, wide_ref,
    act_ref, grad_ref, o0, o1, o2, o3, depth_ref, tall_ref, long_ref, total_ref,
):
    @pl.when(pl.program_id(0) == 0)
    def _():
        fill_tables(strip_ref, wide_ref, depth_ref, tall_ref, long_ref)

    def inverse(y):
        values = inverse_group((i0, i1, i2, i3), depth_ref, long_ref, y)
        lanes = slice(LANES * y, LANES * (y + 1))
        total_ref[y] = bypass_ref[:, :, lanes].astype(F32) + values.reshape(GROUP, XL, LANES)

    def forward(*runs):
        forward_runs(grad_ref, depth_ref, tall_ref, (o0, o1, o2, o3), runs)

    inverse(0)
    for y in range(STEPS):
        if y + 1 < STEPS:
            inverse(y + 1)
        activate(upstream_ref, total_ref, act_ref, grad_ref, y)
        if y == 2:
            forward(0, 1)
    forward(2, 3)


def end_kernel(
    where_ref, i0, i1, i2, i3, bypass_ref, strip_ref, wide_ref, out_ref,
    depth_ref, tall_ref, long_ref,
):
    @pl.when(pl.program_id(0) == 0)
    def _():
        fill_tables(strip_ref, wide_ref, depth_ref, tall_ref, long_ref)

    for y in range(STEPS):
        values = inverse_group((i0, i1, i2, i3), depth_ref, long_ref, y)
        lanes = slice(LANES * y, LANES * (y + 1))
        out_ref[:, :, lanes] = (
            bypass_ref[:, :, lanes].astype(F32) + values.reshape(GROUP, XL, LANES)
        ).astype(BF)


def cost(micros):
    return pl.CostEstimate(flops=0, bytes_accessed=micros * 3_000_000, transcendentals=0)


def column_specs():
    columns = pl.BlockSpec((GROUP, XL, YL * NZ), lambda j, w: (j, 0, 0))
    coeffs = pl.BlockSpec((STEPS, ROWS, GL), lambda j, w: (0, 0, j))
    depth = pl.BlockSpec((1, 2 * KZ, LANES), lambda j, w: (w[1], 0, 0))
    wide = pl.BlockSpec((1, 2, XL, KX), lambda j, w: (w[1], 0, 0, 0))
    return columns, coeffs, depth, wide


COEFFS = jax.ShapeDtypeStruct((STEPS, ROWS, WIDE), BF)
COLUMNS = jax.ShapeDtypeStruct((CH, XL, YL * NZ), BF)
BLOCKS = [
    pltpu.VMEM((2 * KZ * YB, LANES), BF),
    pltpu.VMEM((2 * GL, GL), BF),
    pltpu.VMEM((GL, 2 * GL), BF),
]
TOTAL = pltpu.VMEM((STEPS, GROUP, XL, LANES), F32)
PARAMS = pltpu.CompilerParams(vmem_limit_bytes=56 * 1024 * 1024)
ALONE = pltpu.CompilerParams(vmem_limit_bytes=63 * 1024 * 1024)


def bypass_columns(source, mixer, shift):
    columns = pl.BlockSpec((CH, XL, LANES), lambda i: (0, 0, i))
    return pl.pallas_call(
        bypass_kernel,
        grid=(STEPS,),
        in_specs=[
            pl.BlockSpec(memory_space=pltpu.SMEM),
            columns,
            pl.BlockSpec((CH * XB, CH * XB), lambda i: (0, 0)),
        ],
        out_specs=columns,
        out_shape=COLUMNS,
        compiler_params=PARAMS,
        cost_estimate=cost(6),
        name="bypass_columns",
    )(shift, source, mixer)


def start_columns(where, field):
    columns, coeffs, depth, wide = column_specs()
    return pl.pallas_call(
        start_kernel,
        grid_spec=pltpu.PrefetchScalarGridSpec(
            num_scalar_prefetch=1,
            grid=(GROUPS,),
            in_specs=[columns, depth, wide],
            out_specs=[coeffs] * 4,
            scratch_shapes=BLOCKS,
        ),
        out_shape=[COEFFS] * 4,
        compiler_params=PARAMS,
        cost_estimate=cost(8),
        name="start_columns",
    )(where, field, jnp.asarray(DEPTH), jnp.asarray(WIDTH))


def middle_columns(where, coeffs_in, bypass, upstream):
    columns, coeffs, depth, wide = column_specs()
    return pl.pallas_call(
        middle_kernel,
        grid_spec=pltpu.PrefetchScalarGridSpec(
            num_scalar_prefetch=1,
            grid=(GROUPS,),
            in_specs=[coeffs] * 4 + [columns, columns, depth, wide],
            out_specs=[columns, columns] + [coeffs] * 4,
            scratch_shapes=BLOCKS + [TOTAL],
        ),
        out_shape=[COLUMNS, COLUMNS] + [COEFFS] * 4,
        compiler_params=PARAMS,
        cost_estimate=cost(19),
        name="middle_columns",
    )(where, *coeffs_in, bypass, upstream, jnp.asarray(DEPTH), jnp.asarray(WIDTH))


def end_columns(where, coeffs_in, bypass):
    columns, coeffs, depth, wide = column_specs()
    return pl.pallas_call(
        end_kernel,
        grid_spec=pltpu.PrefetchScalarGridSpec(
            num_scalar_prefetch=1,
            grid=(GROUPS,),
            in_specs=[coeffs] * 4 + [columns, depth, wide],
            out_specs=columns,
            scratch_shapes=BLOCKS,
        ),
        out_shape=COLUMNS,
        compiler_params=PARAMS,
        cost_estimate=cost(10),
        name="end_columns",
    )(where, *coeffs_in, bypass, jnp.asarray(DEPTH), jnp.asarray(WIDTH))


def order_table(where_ref, table_ref, order_ref):
    for k in range(GY):
        owner = ((where_ref[2] + (k & 6)) & 7) ^ (k & 1)
        start = pl.multiple_of(owner * 48, 16)
        order_ref[48 * k : 48 * (k + 1)] = table_ref[0, pl.ds(start, 48), :]


def line_kernel(where_ref, a_ref, b_ref, c_ref, table_ref, out_ref):
    for j in range(GROUPS):
        lanes = slice(GL * j, GL * (j + 1))
        parts = [ref[:, :, lanes].astype(F32) for ref in (a_ref, b_ref, c_ref)]
        rows = (parts[0] + parts[1] + parts[2]).astype(BF).reshape(STEPS * ROWS, GL)
        out_ref[:, :, lanes] = dot(table_ref[0], rows).astype(BF).reshape(GY, 48, GL)


def unline_kernel(where_ref, modes_ref, table_ref, out_ref):
    for j in range(GROUPS):
        lanes = slice(GL * j, GL * (j + 1))
        rows = modes_ref[:, :, lanes].reshape(GY * 48, GL)
        out_ref[:, :, lanes] = dot(table_ref[0], rows, 0, 0).astype(BF).reshape(STEPS, ROWS, GL)


def unline_set_kernel(where_ref, *refs):
    *modes_refs, table_ref, out_ref, order_ref = refs
    for k in range(GY):
        owner = ((where_ref[2] + (k & 6)) & 7) ^ (k & 1)
        start = pl.multiple_of(owner * 48, 16)
        order_ref[48 * k : 48 * (k + 1)] = table_ref[0, pl.ds(start, 48), :]
    for j in range(GROUPS):
        lanes = slice(GL * j, GL * (j + 1))
        rows = jnp.concatenate([ref[:, lanes] for ref in modes_refs], axis=0)
        out_ref[:, :, lanes] = dot(order_ref[...], rows, 0, 0).astype(BF).reshape(STEPS, ROWS, GL)


def line_call(kernel, name, where, ins, out, scratch=()):
    whole = pl.BlockSpec(ins[0].shape, lambda i, w: (0,) * ins[0].ndim)
    table = pl.BlockSpec((1, GY * 48, STEPS * ROWS), lambda i, w: (w[2], 0, 0))
    return pl.pallas_call(
        kernel,
        grid_spec=pltpu.PrefetchScalarGridSpec(
            num_scalar_prefetch=1,
            grid=(1,),
            in_specs=[whole] * len(ins) + [table],
            out_specs=pl.BlockSpec(out.shape, lambda i, w: (0, 0, 0)),
            scratch_shapes=list(scratch),
        ),
        out_shape=out,
        compiler_params=ALONE,
        cost_estimate=cost(3),
        name=name,
    )(where, *ins, jnp.asarray(LINE))


def to_lines(where, *parts):
    out = jax.ShapeDtypeStruct((GY, 48, WIDE), BF)
    return line_call(line_kernel, "to_lines", where, parts, out)


def from_lines(where, modes):
    return line_call(unline_kernel, "from_lines", where, (modes,), COEFFS)


def from_line_set(where, modes):
    order = pltpu.VMEM((GY * 48, STEPS * ROWS), BF)
    return line_call(unline_set_kernel, "from_line_set", where, modes, COEFFS, [order])


UNROLL = 4
SETS = GX * KB
PAIR = 2 * CH
HALF = KX


def low_lanes():
    return lax.broadcasted_iota(jnp.int32, (SETS, 2 * HALF), 1) < HALF


def gather_modes(arrived, sum_ref, modes_ref, scale=None):
    total = arrived[0].astype(F32)
    for i in range(1, GY):
        total = total + arrived[i].astype(F32)
    sum_ref[...] = total.astype(BF).astype(F32)
    low = low_lanes()
    for j in range(CH // 2):
        lanes = slice(2 * HALF * j, 2 * HALF * (j + 1))
        for part in range(2):
            first = sum_ref[part * SETS : (part + 1) * SETS, lanes]
            second = sum_ref[(2 + part) * SETS : (3 + part) * SETS, lanes]
            if scale is not None:
                first = first * scale
                second = second * scale
            even = jnp.where(low, first, pltpu.roll(second, HALF, 1))
            odd = jnp.where(low, pltpu.roll(first, HALF, 1), second)
            modes_ref[pl.ds(4 * j + part, SETS, stride=PAIR), :] = even
            modes_ref[pl.ds(4 * j + 2 + part, SETS, stride=PAIR), :] = odd


def spread_modes(modes_ref, sum_ref, out_ref, scale=None):
    low = low_lanes()
    for j in range(CH // 2):
        lanes = slice(2 * HALF * j, 2 * HALF * (j + 1))
        for part in range(2):
            even = modes_ref[pl.ds(4 * j + part, SETS, stride=PAIR), :]
            odd = modes_ref[pl.ds(4 * j + 2 + part, SETS, stride=PAIR), :]
            if scale is not None:
                even = even * scale
                odd = odd * scale
            sum_ref[part * SETS : (part + 1) * SETS, lanes] = jnp.where(
                low, even, pltpu.roll(odd, HALF, 1)
            )
            sum_ref[(2 + part) * SETS : (3 + part) * SETS, lanes] = jnp.where(
                low, pltpu.roll(even, HALF, 1), odd
            )
    modes = sum_ref[...].astype(BF)
    for copy in range(out_ref.shape[0]):
        out_ref[copy] = modes


def fold_scale(where_ref):
    kz = where_ref[1] * KB + lax.broadcasted_iota(jnp.int32, (SETS, 2 * HALF), 0) % KB
    return jnp.where(kz == 0, 1.0, 2.0).astype(F32) / float(NX * NY * NZ)


def turned(rows):
    even = lax.broadcasted_iota(jnp.int32, rows.shape, 0) % 2 == 0
    up = pltpu.roll(rows, PAIR - 1, 0)
    down = pltpu.roll(rows, 1, 0)
    return jnp.where(even, -up, down)


def hand_out(where_ref, modes_ref, outs):
    for k in range(DP):
        chunk = lax.rem(where_ref[0] + k, DP)
        start = pl.multiple_of(chunk * KB * PAIR, 8)
        outs[k][...] = modes_ref[pl.ds(start, KB * PAIR), :].astype(BF)


def set_row(where_ref, k):
    block = (lax.rem(where_ref[0] + k, DP) ^ (2 * (where_ref[1] & 1))) * KB + pl.program_id(0)
    return pl.multiple_of(block * PAIR, 8)


def mix_kernel(
    where_ref, arrived_ref, w0, w1, w2, w3, out_ref, u0, u1, u2, u3,
    sum_ref, in_ref, mix_ref,
):
    step = pl.program_id(0)

    @pl.when(step == 0)
    def _():
        gather_modes(arrived_ref, sum_ref, in_ref)
        hand_out(where_ref, in_ref, [ref.at[0] for ref in (u0, u1, u2, u3)])

    for k, weight_ref in enumerate((w0, w1, w2, w3)):
        base = set_row(where_ref, k)

        def add(i, totals, weight_ref=weight_ref, base=base):
            by_real, by_imag = totals
            for r in range(UNROLL):
                c = i * UNROLL + r
                weight = weight_ref[0, c].astype(F32)
                by_real = by_real + weight * in_ref[pl.ds(base + 2 * c, 1), :]
                by_imag = by_imag + weight * in_ref[pl.ds(base + 2 * c + 1, 1), :]
            return by_real, by_imag

        zero = jnp.zeros((PAIR, 2 * HALF), F32)
        by_real, by_imag = lax.fori_loop(0, CH // UNROLL, add, (zero, zero))
        mix_ref[pl.ds(base, PAIR), :] = (by_real + turned(by_imag)).astype(BF).astype(F32)

    @pl.when(step == KB - 1)
    def _():
        spread_modes(mix_ref, sum_ref, out_ref, fold_scale(where_ref))


def back_kernel(
    where_ref, arrived_ref, w0, w1, w2, w3, s0, s1, s2, s3, out_ref, u0, u1, u2, u3,
    sum_ref, in_ref, mix_ref,
):
    step = pl.program_id(0)

    @pl.when(step == 0)
    def _():
        gather_modes(arrived_ref, sum_ref, in_ref, fold_scale(where_ref))
        hand_out(where_ref, in_ref, [ref.at[1] for ref in (u0, u1, u2, u3)])
        for spec_ref, ref in zip((s0, s1, s2, s3), (u0, u1, u2, u3)):
            ref[0] = spec_ref[0]

    for k, weight_ref in enumerate((w0, w1, w2, w3)):
        base = set_row(where_ref, k)
        grad = in_ref[pl.ds(base, PAIR), :]
        other = -turned(grad)

        @pl.loop(0, CH // UNROLL)
        def _(i, weight_ref=weight_ref, base=base, grad=grad, other=other):
            for r in range(UNROLL):
                c = i * UNROLL + r
                weight = weight_ref[0, c].astype(F32)
                mix_ref[pl.ds(base + 2 * c, 1), :] = jnp.sum(weight * grad, axis=0, keepdims=True)
                mix_ref[pl.ds(base + 2 * c + 1, 1), :] = jnp.sum(
                    weight * other, axis=0, keepdims=True
                )

    @pl.when(step == KB - 1)
    def _():
        spread_modes(mix_ref, sum_ref, out_ref)


def mode_call(kernel, name, where, arrived, weights, spectra=()):
    sets, copies = (2, GY) if spectra else (1, 1)

    def chunk(n):
        return pl.BlockSpec((n, KB * PAIR, 2 * HALF), lambda i, w: (0, 0, 0))

    return pl.pallas_call(
        kernel,
        grid_spec=pltpu.PrefetchScalarGridSpec(
            num_scalar_prefetch=1,
            grid=(KB,),
            in_specs=[pl.BlockSpec((GY, 48, WIDE), lambda i, w: (0, 0, 0))]
            + [pl.BlockSpec((1, CH, PAIR, 2 * HALF), lambda i, w: (i, 0, 0, 0))] * 4
            + [chunk(1)] * len(spectra),
            out_specs=[pl.BlockSpec((copies, 48, WIDE), lambda i, w: (0, 0, 0))]
            + [chunk(sets)] * 4,
            scratch_shapes=[
                pltpu.VMEM((48, WIDE), F32),
                pltpu.VMEM((SETS * PAIR, 2 * HALF), F32),
                pltpu.VMEM((SETS * PAIR, 2 * HALF), F32),
            ],
        ),
        out_shape=[jax.ShapeDtypeStruct((copies, 48, WIDE), BF)]
        + [jax.ShapeDtypeStruct((sets, KB * PAIR, 2 * HALF), BF)] * 4,
        compiler_params=ALONE,
        cost_estimate=cost(5),
        name=name,
    )(where, arrived, *weights, *spectra)


def outer_kernel(p0, p1, p2, p3, out_ref, spec_ref):
    pairs = (p0, p1, p2, p3)
    for k, ref in enumerate(pairs):
        spec_ref[k] = ref[0].astype(F32)
    for i in range(KB):
        grads = []
        others = []
        for ref in pairs:
            grad = ref[1].astype(F32)[i * PAIR : (i + 1) * PAIR]
            grads.append(grad)
            others.append(-turned(grad))

        @pl.loop(0, CH)
        def _(c):
            row = i * PAIR + 2 * c
            total = jnp.zeros((PAIR, 2 * HALF), F32)
            for k in range(DP):
                total = total + spec_ref[k, pl.ds(row, 1), :] * grads[k]
                total = total + spec_ref[k, pl.ds(row + 1, 1), :] * others[k]
            out_ref[i, c] = total


def outer_sum(pairs):
    return pl.pallas_call(
        outer_kernel,
        out_shape=jax.ShapeDtypeStruct((KB, CH, PAIR, 2 * HALF), F32),
        scratch_shapes=[pltpu.VMEM((DP, KB * PAIR, 2 * HALF), F32)],
        cost_estimate=cost(3),
        name="outer_sum",
    )(*pairs)


def swap(values, bit):
    return lax.ppermute(values, "gx", [(i, i ^ bit) for i in range(GX)])


def start_slabs(pieces, beside):
    own, far, near, across = pieces
    far_sum = (far.astype(F32) + swap(across, 1).astype(F32)).astype(BF)
    arrived, beside = lax.optimization_barrier((swap(far_sum, 2), beside))
    return (own, swap(near, 1), arrived), beside


def share_slabs(own, *beside):
    far, *beside = lax.optimization_barrier((swap(own, 2), *beside))
    return own, far, swap(own, 1), swap(far, 1), *beside


def gather_weights(weight):
    held = [weight]
    for k in range(1, DP):
        held.append(lax.ppermute(weight, "dp", [((a + k) % DP, a) for a in range(DP)]))
    return [part.reshape(KB, CH, PAIR, 2 * HALF) for part in held]


def gather_lines(modes):
    held = [modes, lax.ppermute(modes, "gy", [(g ^ 1, g) for g in range(GY)])]
    for step in range(2, GY, 2):
        pairs = [((g + step) % GY, g) for g in range(GY)]
        held += [lax.ppermute(part, "gy", pairs) for part in held[:2]]
    return held


def exchange_lines(parts):
    return lax.all_to_all(parts, "gy", split_axis=0, concat_axis=0, tiled=True)


def to_owners(chunks):
    moved = []
    for k, chunk in enumerate(chunks):
        pairs = [
            (a * GX + b, b * GX + (a + k) % DP) for a in range(DP) for b in range(GX)
        ]
        moved.append(lax.ppermute(chunk, ("dp", "gx"), pairs))
    return moved


def per_device(field, spectral_weight, bypass_weight, bias, cotangent):
    where = jnp.stack(
        [lax.axis_index("dp"), lax.axis_index("gx"), lax.axis_index("gy")]
    ).astype(jnp.int32)
    turn = [(a * GX + b, (b ^ (2 * (a % 2))) * GX + a) for a in range(DP) for b in range(GX)]
    weight = lax.ppermute(spectral_weight, ("dp", "gx"), turn)
    spread = jnp.asarray(SPREAD)

    def mixer_of(matrix):
        wide = dot(dot(spread, matrix).astype(BF), spread, 1, 1)
        return wide.astype(BF) * jnp.asarray(SAME)

    values = field[0]
    *pieces, weight = lax.optimization_barrier((*start_columns(where, values), weight))
    parts, bypass = start_slabs(pieces, bypass_columns(values, mixer_of(bypass_weight), bias))
    weights = gather_weights(weight)
    lines, weights[1], weights[3] = lax.optimization_barrier(
        (to_lines(where, *parts), weights[1], weights[3])
    )
    arrived = exchange_lines(lines)
    modes, *spectra = mode_call(mix_kernel, "mix_modes", where, arrived, weights)
    coeffs = share_slabs(from_line_set(where, gather_lines(modes[0])))
    activation, grad, *pieces = middle_columns(where, coeffs, bypass, cotangent[0])
    mixer = mixer_of(bypass_weight.T)
    parts, bypass = start_slabs(pieces, bypass_columns(grad, mixer, jnp.zeros_like(bias)))
    arrived = exchange_lines(to_lines(where, *parts))
    modes, *pairs = mode_call(back_kernel, "back_modes", where, arrived, weights, spectra)
    modes, *pairs = lax.optimization_barrier((exchange_lines(modes), *to_owners(pairs)))
    *coeffs, weight_grad = share_slabs(from_lines(where, modes), outer_sum(pairs))
    field_grad = end_columns(where, coeffs, bypass)
    return (
        activation[None],
        field_grad[None],
        weight_grad.reshape(KB, CH, CH, 2, 2 * HALF),
    )


def solution(mesh):
    placed = (
        P("dp", None, "gx", "gy"),
        P("dp", None, None, None, ("gx", "gy")),
        P(),
        P(),
        P("dp", None, "gx", "gy"),
    )
    return jax.shard_map(
        per_device,
        mesh=mesh,
        in_specs=placed,
        out_specs=(
            P("dp", None, "gx", "gy"),
            P("dp", None, "gx", "gy"),
            P("dp", None, None, None, ("gx", "gy")),
        ),
        check_vma=False,
    )
```

```python
import functools
import math

import jax
import jax.numpy as jnp
import ml_dtypes
import numpy as np
from jax import lax
from jax.experimental import pallas as pl
from jax.experimental.pallas import tpu as pltpu
from jax.sharding import PartitionSpec as P

CH = 20
NX = 256
NY = 256
NZ = 64
KX = 64
KY = 64
KZ = 12
GX = 4
GY = 8
DP = 4
XL = NX // GX
YL = NY // GY
YB = 8
STEPS = YL // YB
LANES = YB * NZ
KB = KZ // GX
ROWS = 2 * KB * YB
GROUP = 4
GROUPS = CH // GROUP
GL = GROUP * KX
WIDE = CH * KX
XB = 8
EB = 16
ORDER = (0, 2, 1, 3)

BF = jnp.bfloat16
F32 = jnp.float32


def wave(freqs, points, length):
    offsets = np.mod(freqs[:, None] * points[None, :], length)
    angle = offsets.astype(np.float32) * np.float32(2.0 * math.pi / length)
    return np.cos(angle), np.sin(angle)


def kept(count):
    index = np.arange(count)
    return np.where(index < count // 2, index, index - count)


def depth_tables():
    out = np.zeros((GX, 2, GX, KB, LANES), np.float32)
    for b in range(GX):
        for pos, delta in enumerate(ORDER):
            freqs = (b ^ delta) * KB + np.arange(KB)
            cosine, sine = wave(freqs, np.arange(NZ), NZ)
            out[b, 0, pos] = np.tile(cosine, (1, YB))
            out[b, 1, pos] = np.tile(-sine, (1, YB))
    return out.reshape(GX, 2 * KZ, LANES).astype(ml_dtypes.bfloat16)


def width_tables():
    out = np.zeros((GX, 2, XL, KX), np.float32)
    for b in range(GX):
        cosine, sine = wave(kept(KX), b * XL + np.arange(XL), NX)
        out[b, 0] = cosine.T
        out[b, 1] = sine.T
    return out.astype(ml_dtypes.bfloat16)


def line_tables():
    out = np.zeros((GY, GY, 2, 2, GX, KB, STEPS, 2, KB, YB), np.float32)
    fy = kept(KY)
    for g in range(GY):
        cosine, sine = wave(fy, g * YL + np.arange(YL), NY)
        cosine = cosine.reshape(GX, GY, 2, STEPS, YB)
        sine = sine.reshape(GX, GY, 2, STEPS, YB)
        for i in range(KB):
            for owner in range(GY):
                for q in range(2):
                    c = cosine[:, owner, q]
                    s = sine[:, owner, q]
                    out[g, owner, q, 0, :, i, :, 0, i] = c
                    out[g, owner, q, 0, :, i, :, 1, i] = s
                    out[g, owner, q, 1, :, i, :, 0, i] = -s
                    out[g, owner, q, 1, :, i, :, 1, i] = c
    return out.reshape(GY, GY * 48, STEPS * ROWS).astype(ml_dtypes.bfloat16)


DEPTH = depth_tables()
WIDTH = width_tables()
LINE = line_tables()
SPREAD = np.kron(np.eye(CH), np.ones((XB, 1))).astype(ml_dtypes.bfloat16)
SAME = np.kron(np.ones((CH, CH)), np.eye(XB)).astype(ml_dtypes.bfloat16)


def dot(left, right, left_dim=1, right_dim=0):
    return lax.dot_general(
        left, right, (((left_dim,), (right_dim,)), ((), ())), preferred_element_type=F32
    )


def fill_tables(strip_ref, wide_ref, depth_ref, tall_ref, long_ref):
    strips = jnp.broadcast_to(strip_ref[0].astype(F32)[:, None, :], (2 * KZ, YB, LANES))
    row = lax.broadcasted_iota(jnp.int32, (2 * KZ, YB, LANES), 1)
    column = lax.broadcasted_iota(jnp.int32, (2 * KZ, YB, LANES), 2) // NZ
    blocks = jnp.where(row == column, strips, 0.0)
    depth_ref[...] = blocks.reshape(2 * KZ * YB, LANES).astype(BF)
    rows = lax.broadcasted_iota(jnp.int32, (GL, GL), 0) // XL
    columns = lax.broadcasted_iota(jnp.int32, (GL, GL), 1) // KX
    for part in range(2):
        strip = wide_ref[0, part].astype(F32)
        full = jnp.concatenate([jnp.concatenate([strip] * GROUP, axis=1)] * GROUP, axis=0)
        block = jnp.where(rows == columns, full, 0.0).astype(BF)
        tall_ref[GL * part : GL * (part + 1), :] = block
        long_ref[:, GL * part : GL * (part + 1)] = block


def forward_runs(source_ref, depth_ref, tall_ref, outs, runs):
    half = KZ * YB
    part = KB * YB
    sides = []
    for y in runs:
        planes = dot(depth_ref[...], run_rows(source_ref, y), 1, 1)
        real = planes[:half]
        imag = planes[half:]
        sides.append(jnp.concatenate([real, imag], axis=1).astype(BF))
        sides.append(jnp.concatenate([imag, -real], axis=1).astype(BF))
    lines = dot(jnp.concatenate(sides, axis=0), tall_ref[...])
    for n, y in enumerate(runs):
        for pos in range(GX):
            lo = 2 * half * n + pos * part
            piece = jnp.concatenate(
                [lines[lo : lo + part], lines[half + lo : half + lo + part]], axis=0
            )
            outs[pos][y] = piece.astype(BF)


def inverse_runs(ins, depth_ref, long_ref, runs):
    part = KB * YB
    planes = []
    for y in runs:
        pieces = [ref[y].astype(F32) for ref in ins]
        real = jnp.concatenate([piece[:part] for piece in pieces], axis=0)
        imag = jnp.concatenate([piece[part:] for piece in pieces], axis=0)
        sides = jnp.concatenate(
            [jnp.concatenate([real, -imag], axis=1), jnp.concatenate([imag, real], axis=1)],
            axis=0,
        ).astype(BF)
        planes.append(dot(long_ref[...], sides, 1, 1).astype(BF))
    return dot(jnp.concatenate(planes, axis=0), depth_ref[...])


def run_rows(ref, y):
    return ref[:, :, LANES * y : LANES * (y + 1)].reshape(GROUP * XL, LANES)


def bypass_kernel(shift_ref, source_ref, mixer_ref, out_ref):
    for i in range(XL // XB):
        span = slice(i * XB, (i + 1) * XB)
        rows = source_ref[:, span, :].reshape(CH * XB, LANES)
        mixed = dot(mixer_ref[...], rows).reshape(CH, XB, LANES)
        for channel in range(CH):
            out_ref[channel, span, :] = (mixed[channel] + shift_ref[channel]).astype(BF)


def start_kernel(
    where_ref, field_ref, strip_ref, wide_ref, o0, o1, o2, o3, depth_ref, tall_ref, long_ref
):
    @pl.when(pl.program_id(0) == 0)
    def _():
        fill_tables(strip_ref, wide_ref, depth_ref, tall_ref, long_ref)

    forward_runs(field_ref, depth_ref, tall_ref, (o0, o1, o2, o3), range(STEPS))


ROOT = math.sqrt(2.0 / math.pi)
CUBE = 0.044715


def activate(upstream_ref, total_ref, act_ref, grad_ref, y):
    lanes = slice(LANES * y, LANES * (y + 1))
    for channel in range(GROUP):
        for i in range(XL // EB):
            span = slice(i * EB, (i + 1) * EB)
            x = total_ref[y, channel, span, :]
            square = x * x
            t = jnp.tanh(x * (ROOT + (ROOT * CUBE) * square))
            h = 0.5 * t + 0.5
            act = x * h
            slope = h + act * (1.0 - h) * (2.0 * ROOT + (6.0 * ROOT * CUBE) * square)
            act_ref[channel, span, lanes] = act.astype(BF)
            grad_ref[channel, span, lanes] = upstream_ref[channel, span, lanes] * slope.astype(BF)


def middle_kernel(
    where_ref, i0, i1, i2, i3, bypass_ref, upstream_ref, strip_ref, wide_ref,
    act_ref, grad_ref, o0, o1, o2, o3, depth_ref, tall_ref, long_ref, total_ref,
):
    @pl.when(pl.program_id(0) == 0)
    def _():
        fill_tables(strip_ref, wide_ref, depth_ref, tall_ref, long_ref)

    def inverse(*runs):
        values = inverse_runs((i0, i1, i2, i3), depth_ref, long_ref, runs)
        for n, y in enumerate(runs):
            lanes = slice(LANES * y, LANES * (y + 1))
            own = values[GL * n : GL * (n + 1)].reshape(GROUP, XL, LANES)
            total_ref[y] = bypass_ref[:, :, lanes].astype(F32) + own

    def forward(*runs):
        forward_runs(grad_ref, depth_ref, tall_ref, (o0, o1, o2, o3), runs)

    def activation(y):
        activate(upstream_ref, total_ref, act_ref, grad_ref, y)

    inverse(0, 1)
    activation(0)
    inverse(2, 3)
    activation(1)
    activation(2)
    forward(0, 1)
    activation(3)
    forward(2, 3)


def end_kernel(
    where_ref, i0, i1, i2, i3, bypass_ref, strip_ref, wide_ref, out_ref,
    depth_ref, tall_ref, long_ref,
):
    @pl.when(pl.program_id(0) == 0)
    def _():
        fill_tables(strip_ref, wide_ref, depth_ref, tall_ref, long_ref)

    for first in range(0, STEPS, 2):
        runs = (first, first + 1)
        values = inverse_runs((i0, i1, i2, i3), depth_ref, long_ref, runs)
        for n, y in enumerate(runs):
            lanes = slice(LANES * y, LANES * (y + 1))
            own = values[GL * n : GL * (n + 1)].reshape(GROUP, XL, LANES)
            out_ref[:, :, lanes] = (bypass_ref[:, :, lanes].astype(F32) + own).astype(BF)


def cost(micros):
    return pl.CostEstimate(flops=0, bytes_accessed=micros * 3_000_000, transcendentals=0)


def column_specs():
    columns = pl.BlockSpec((GROUP, XL, YL * NZ), lambda j, w: (j, 0, 0))
    coeffs = pl.BlockSpec((STEPS, ROWS, GL), lambda j, w: (0, 0, j))
    depth = pl.BlockSpec((1, 2 * KZ, LANES), lambda j, w: (w[1], 0, 0))
    wide = pl.BlockSpec((1, 2, XL, KX), lambda j, w: (w[1], 0, 0, 0))
    return columns, coeffs, depth, wide


COEFFS = jax.ShapeDtypeStruct((STEPS, ROWS, WIDE), BF)
COLUMNS = jax.ShapeDtypeStruct((CH, XL, YL * NZ), BF)
BLOCKS = [
    pltpu.VMEM((2 * KZ * YB, LANES), BF),
    pltpu.VMEM((2 * GL, GL), BF),
    pltpu.VMEM((GL, 2 * GL), BF),
]
TOTAL = pltpu.VMEM((STEPS, GROUP, XL, LANES), F32)
PARAMS = pltpu.CompilerParams(vmem_limit_bytes=56 * 1024 * 1024)
ALONE = pltpu.CompilerParams(vmem_limit_bytes=67_043_328)


def bypass_columns(source, mixer, shift):
    columns = pl.BlockSpec((CH, XL, LANES), lambda i: (0, 0, i))
    return pl.pallas_call(
        bypass_kernel,
        grid=(STEPS,),
        in_specs=[
            pl.BlockSpec(memory_space=pltpu.SMEM),
            columns,
            pl.BlockSpec((CH * XB, CH * XB), lambda i: (0, 0)),
        ],
        out_specs=columns,
        out_shape=COLUMNS,
        compiler_params=PARAMS,
        cost_estimate=cost(6),
        name="bypass_columns",
    )(shift, source, mixer)


def start_columns(where, field):
    columns, coeffs, depth, wide = column_specs()
    return pl.pallas_call(
        start_kernel,
        grid_spec=pltpu.PrefetchScalarGridSpec(
            num_scalar_prefetch=1,
            grid=(GROUPS,),
            in_specs=[columns, depth, wide],
            out_specs=[coeffs] * 4,
            scratch_shapes=BLOCKS,
        ),
        out_shape=[COEFFS] * 4,
        compiler_params=PARAMS,
        cost_estimate=cost(8),
        name="start_columns",
    )(where, field, jnp.asarray(DEPTH), jnp.asarray(WIDTH))


def middle_columns(where, coeffs_in, bypass, upstream):
    columns, coeffs, depth, wide = column_specs()
    return pl.pallas_call(
        middle_kernel,
        grid_spec=pltpu.PrefetchScalarGridSpec(
            num_scalar_prefetch=1,
            grid=(GROUPS,),
            in_specs=[coeffs] * 4 + [columns, columns, depth, wide],
            out_specs=[columns, columns] + [coeffs] * 4,
            scratch_shapes=BLOCKS + [TOTAL],
        ),
        out_shape=[COLUMNS, COLUMNS] + [COEFFS] * 4,
        compiler_params=PARAMS,
        cost_estimate=cost(19),
        name="middle_columns",
    )(where, *coeffs_in, bypass, upstream, jnp.asarray(DEPTH), jnp.asarray(WIDTH))


def end_columns(where, coeffs_in, bypass):
    columns, coeffs, depth, wide = column_specs()
    return pl.pallas_call(
        end_kernel,
        grid_spec=pltpu.PrefetchScalarGridSpec(
            num_scalar_prefetch=1,
            grid=(GROUPS,),
            in_specs=[coeffs] * 4 + [columns, depth, wide],
            out_specs=columns,
            scratch_shapes=BLOCKS,
        ),
        out_shape=COLUMNS,
        compiler_params=ALONE,
        cost_estimate=cost(10),
        name="end_columns",
    )(where, *coeffs_in, bypass, jnp.asarray(DEPTH), jnp.asarray(WIDTH))


def order_table(where_ref, table_ref, order_ref):
    for k in range(GY):
        owner = ((where_ref[2] + (k & 6)) & 7) ^ (k & 1)
        start = pl.multiple_of(owner * 48, 16)
        order_ref[48 * k : 48 * (k + 1)] = table_ref[0, pl.ds(start, 48), :]


def line_kernel(where_ref, a_ref, b_ref, c_ref, table_ref, out_ref):
    for j in range(GROUPS):
        lanes = slice(GL * j, GL * (j + 1))
        parts = [ref[:, :, lanes].astype(F32) for ref in (a_ref, b_ref, c_ref)]
        rows = (parts[0] + parts[1] + parts[2]).astype(BF).reshape(STEPS * ROWS, GL)
        out_ref[:, :, lanes] = dot(table_ref[0], rows).astype(BF).reshape(GY, 48, GL)


def unline_kernel(where_ref, modes_ref, table_ref, out_ref):
    for j in range(GROUPS):
        lanes = slice(GL * j, GL * (j + 1))
        rows = modes_ref[:, :, lanes].reshape(GY * 48, GL)
        out_ref[:, :, lanes] = dot(table_ref[0], rows, 0, 0).astype(BF).reshape(STEPS, ROWS, GL)


def unline_set_kernel(where_ref, *refs):
    *modes_refs, table_ref, out_ref, order_ref = refs
    for k in range(GY):
        owner = ((where_ref[2] + (k & 6)) & 7) ^ (k & 1)
        start = pl.multiple_of(owner * 48, 16)
        order_ref[48 * k : 48 * (k + 1)] = table_ref[0, pl.ds(start, 48), :]
    for j in range(GROUPS):
        lanes = slice(GL * j, GL * (j + 1))
        rows = jnp.concatenate([ref[:, lanes] for ref in modes_refs], axis=0)
        out_ref[:, :, lanes] = dot(order_ref[...], rows, 0, 0).astype(BF).reshape(STEPS, ROWS, GL)


def line_call(kernel, name, where, ins, out, scratch=()):
    whole = pl.BlockSpec(ins[0].shape, lambda i, w: (0,) * ins[0].ndim)
    table = pl.BlockSpec((1, GY * 48, STEPS * ROWS), lambda i, w: (w[2], 0, 0))
    return pl.pallas_call(
        kernel,
        grid_spec=pltpu.PrefetchScalarGridSpec(
            num_scalar_prefetch=1,
            grid=(1,),
            in_specs=[whole] * len(ins) + [table],
            out_specs=pl.BlockSpec(out.shape, lambda i, w: (0, 0, 0)),
            scratch_shapes=list(scratch),
        ),
        out_shape=out,
        compiler_params=ALONE,
        cost_estimate=cost(3),
        name=name,
    )(where, *ins, jnp.asarray(LINE))


def to_lines(where, *parts):
    out = jax.ShapeDtypeStruct((GY, 48, WIDE), BF)
    return line_call(line_kernel, "to_lines", where, parts, out)


def from_lines(where, modes):
    return line_call(unline_kernel, "from_lines", where, (modes,), COEFFS)


def from_line_set(where, modes):
    order = pltpu.VMEM((GY * 48, STEPS * ROWS), BF)
    return line_call(unline_set_kernel, "from_line_set", where, modes, COEFFS, [order])


UNROLL = 4
SETS = GX * KB
PAIR = 2 * CH
HALF = KX


def low_lanes():
    return lax.broadcasted_iota(jnp.int32, (SETS, 2 * HALF), 1) < HALF


def gather_modes(arrived, sum_ref, modes_ref, scale=None):
    total = arrived[0].astype(F32)
    for i in range(1, GY):
        total = total + arrived[i].astype(F32)
    sum_ref[...] = total.astype(BF).astype(F32)
    low = low_lanes()
    for j in range(CH // 2):
        lanes = slice(2 * HALF * j, 2 * HALF * (j + 1))
        for part in range(2):
            first = sum_ref[part * SETS : (part + 1) * SETS, lanes]
            second = sum_ref[(2 + part) * SETS : (3 + part) * SETS, lanes]
            if scale is not None:
                first = first * scale
                second = second * scale
            even = jnp.where(low, first, pltpu.roll(second, HALF, 1))
            odd = jnp.where(low, pltpu.roll(first, HALF, 1), second)
            modes_ref[pl.ds(4 * j + part, SETS, stride=PAIR), :] = even
            modes_ref[pl.ds(4 * j + 2 + part, SETS, stride=PAIR), :] = odd


def spread_modes(modes_ref, sum_ref, out_ref, scale=None):
    low = low_lanes()
    for j in range(CH // 2):
        lanes = slice(2 * HALF * j, 2 * HALF * (j + 1))
        for part in range(2):
            even = modes_ref[pl.ds(4 * j + part, SETS, stride=PAIR), :]
            odd = modes_ref[pl.ds(4 * j + 2 + part, SETS, stride=PAIR), :]
            if scale is not None:
                even = even * scale
                odd = odd * scale
            sum_ref[part * SETS : (part + 1) * SETS, lanes] = jnp.where(
                low, even, pltpu.roll(odd, HALF, 1)
            )
            sum_ref[(2 + part) * SETS : (3 + part) * SETS, lanes] = jnp.where(
                low, pltpu.roll(even, HALF, 1), odd
            )
    modes = sum_ref[...].astype(BF)
    for copy in range(out_ref.shape[0]):
        out_ref[copy] = modes


def fold_scale(where_ref):
    kz = where_ref[1] * KB + lax.broadcasted_iota(jnp.int32, (SETS, 2 * HALF), 0) % KB
    return jnp.where(kz == 0, 1.0, 2.0).astype(F32) / float(NX * NY * NZ)


def turned(rows):
    even = lax.broadcasted_iota(jnp.int32, rows.shape, 0) % 2 == 0
    up = pltpu.roll(rows, PAIR - 1, 0)
    down = pltpu.roll(rows, 1, 0)
    return jnp.where(even, -up, down)


def hand_out(where_ref, modes_ref, outs):
    for k in range(DP):
        chunk = lax.rem(where_ref[0] + k, DP)
        start = pl.multiple_of(chunk * KB * PAIR, 8)
        outs[k][...] = modes_ref[pl.ds(start, KB * PAIR), :].astype(BF)


def set_row(where_ref, k):
    block = (lax.rem(where_ref[0] + k, DP) ^ (2 * (where_ref[1] & 1))) * KB + pl.program_id(0)
    return pl.multiple_of(block * PAIR, 8)


def mix_kernel(
    where_ref, arrived_ref, w0, w1, w2, w3, out_ref, u0, u1, u2, u3,
    sum_ref, in_ref, mix_ref,
):
    step = pl.program_id(0)

    @pl.when(step == 0)
    def _():
        gather_modes(arrived_ref, sum_ref, in_ref)
        hand_out(where_ref, in_ref, [ref.at[0] for ref in (u0, u1, u2, u3)])

    for k, weight_ref in enumerate((w0, w1, w2, w3)):
        base = set_row(where_ref, k)

        def add(i, totals, weight_ref=weight_ref, base=base):
            by_real, by_imag = totals
            for r in range(UNROLL):
                c = i * UNROLL + r
                weight = weight_ref[0, c].astype(F32)
                by_real = by_real + weight * in_ref[pl.ds(base + 2 * c, 1), :]
                by_imag = by_imag + weight * in_ref[pl.ds(base + 2 * c + 1, 1), :]
            return by_real, by_imag

        zero = jnp.zeros((PAIR, 2 * HALF), F32)
        by_real, by_imag = lax.fori_loop(0, CH // UNROLL, add, (zero, zero))
        mix_ref[pl.ds(base, PAIR), :] = (by_real + turned(by_imag)).astype(BF).astype(F32)

    @pl.when(step == KB - 1)
    def _():
        spread_modes(mix_ref, sum_ref, out_ref, fold_scale(where_ref))


def back_kernel(
    where_ref, arrived_ref, w0, w1, w2, w3, s0, s1, s2, s3, out_ref, u0, u1, u2, u3,
    sum_ref, in_ref, mix_ref,
):
    step = pl.program_id(0)

    @pl.when(step == 0)
    def _():
        gather_modes(arrived_ref, sum_ref, in_ref, fold_scale(where_ref))
        hand_out(where_ref, in_ref, [ref.at[1] for ref in (u0, u1, u2, u3)])
        for spec_ref, ref in zip((s0, s1, s2, s3), (u0, u1, u2, u3)):
            ref[0] = spec_ref[0]

    for k, weight_ref in enumerate((w0, w1, w2, w3)):
        base = set_row(where_ref, k)
        grad = in_ref[pl.ds(base, PAIR), :]
        other = -turned(grad)

        @pl.loop(0, CH // UNROLL)
        def _(i, weight_ref=weight_ref, base=base, grad=grad, other=other):
            for r in range(UNROLL):
                c = i * UNROLL + r
                weight = weight_ref[0, c].astype(F32)
                mix_ref[pl.ds(base + 2 * c, 1), :] = jnp.sum(weight * grad, axis=0, keepdims=True)
                mix_ref[pl.ds(base + 2 * c + 1, 1), :] = jnp.sum(
                    weight * other, axis=0, keepdims=True
                )

    @pl.when(step == KB - 1)
    def _():
        spread_modes(mix_ref, sum_ref, out_ref)


def mode_call(kernel, name, where, arrived, weights, spectra=()):
    sets, copies = (2, GY) if spectra else (1, 1)

    def chunk(n):
        return pl.BlockSpec((n, KB * PAIR, 2 * HALF), lambda i, w: (0, 0, 0))

    return pl.pallas_call(
        kernel,
        grid_spec=pltpu.PrefetchScalarGridSpec(
            num_scalar_prefetch=1,
            grid=(KB,),
            in_specs=[pl.BlockSpec((GY, 48, WIDE), lambda i, w: (0, 0, 0))]
            + [pl.BlockSpec((1, CH, PAIR, 2 * HALF), lambda i, w: (i, 0, 0, 0))] * 4
            + [chunk(1)] * len(spectra),
            out_specs=[pl.BlockSpec((copies, 48, WIDE), lambda i, w: (0, 0, 0))]
            + [chunk(sets)] * 4,
            scratch_shapes=[
                pltpu.VMEM((48, WIDE), F32),
                pltpu.VMEM((SETS * PAIR, 2 * HALF), F32),
                pltpu.VMEM((SETS * PAIR, 2 * HALF), F32),
            ],
        ),
        out_shape=[jax.ShapeDtypeStruct((copies, 48, WIDE), BF)]
        + [jax.ShapeDtypeStruct((sets, KB * PAIR, 2 * HALF), BF)] * 4,
        compiler_params=ALONE,
        cost_estimate=cost(5),
        name=name,
    )(where, arrived, *weights, *spectra)


def outer_kernel(p0, p1, p2, p3, out_ref, spec_ref):
    pairs = (p0, p1, p2, p3)
    for k, ref in enumerate(pairs):
        spec_ref[k] = ref[0].astype(F32)
    for i in range(KB):
        grads = []
        others = []
        for ref in pairs:
            grad = ref[1].astype(F32)[i * PAIR : (i + 1) * PAIR]
            grads.append(grad)
            others.append(-turned(grad))

        @pl.loop(0, CH)
        def _(c):
            row = i * PAIR + 2 * c
            total = jnp.zeros((PAIR, 2 * HALF), F32)
            for k in range(DP):
                total = total + spec_ref[k, pl.ds(row, 1), :] * grads[k]
                total = total + spec_ref[k, pl.ds(row + 1, 1), :] * others[k]
            out_ref[i, c] = total


def outer_sum(pairs):
    return pl.pallas_call(
        outer_kernel,
        out_shape=jax.ShapeDtypeStruct((KB, CH, PAIR, 2 * HALF), F32),
        scratch_shapes=[pltpu.VMEM((DP, KB * PAIR, 2 * HALF), F32)],
        cost_estimate=cost(3),
        name="outer_sum",
    )(*pairs)


def swap(values, bit):
    return lax.ppermute(values, "gx", [(i, i ^ bit) for i in range(GX)])


def start_slabs(pieces, beside):
    own, far, near, across = pieces
    far_sum = (far.astype(F32) + swap(across, 1).astype(F32)).astype(BF)
    arrived, beside = lax.optimization_barrier((swap(far_sum, 2), beside))
    return (own, swap(near, 1), arrived), beside


def share_slabs(own, *beside):
    far, *beside = lax.optimization_barrier((swap(own, 2), *beside))
    return own, far, swap(own, 1), swap(far, 1), *beside


def gather_weights(weight):
    held = [weight]
    for k in range(1, DP):
        held.append(lax.ppermute(weight, "dp", [((a + k) % DP, a) for a in range(DP)]))
    return [part.reshape(KB, CH, PAIR, 2 * HALF) for part in held]


def gather_lines(modes):
    held = [modes, lax.ppermute(modes, "gy", [(g ^ 1, g) for g in range(GY)])]
    for step in range(2, GY, 2):
        pairs = [((g + step) % GY, g) for g in range(GY)]
        held += [lax.ppermute(part, "gy", pairs) for part in held[:2]]
    return held


def exchange_lines(parts):
    return lax.all_to_all(parts, "gy", split_axis=0, concat_axis=0, tiled=True)


def to_owners(chunks):
    moved = []
    for k, chunk in enumerate(chunks):
        pairs = [
            (a * GX + b, b * GX + (a + k) % DP) for a in range(DP) for b in range(GX)
        ]
        moved.append(lax.ppermute(chunk, ("dp", "gx"), pairs))
    return moved


def per_device(field, spectral_weight, bypass_weight, bias, cotangent):
    where = jnp.stack(
        [lax.axis_index("dp"), lax.axis_index("gx"), lax.axis_index("gy")]
    ).astype(jnp.int32)
    turn = [(a * GX + b, (b ^ (2 * (a % 2))) * GX + a) for a in range(DP) for b in range(GX)]
    weight = lax.ppermute(spectral_weight, ("dp", "gx"), turn)
    spread = jnp.asarray(SPREAD)

    def mixer_of(matrix):
        wide = dot(dot(spread, matrix).astype(BF), spread, 1, 1)
        return wide.astype(BF) * jnp.asarray(SAME)

    values = field[0]
    *pieces, weight = lax.optimization_barrier((*start_columns(where, values), weight))
    parts, bypass = start_slabs(pieces, bypass_columns(values, mixer_of(bypass_weight), bias))
    weights = gather_weights(weight)
    lines, weights[1], weights[3] = lax.optimization_barrier(
        (to_lines(where, *parts), weights[1], weights[3])
    )
    arrived = exchange_lines(lines)
    modes, *spectra = mode_call(mix_kernel, "mix_modes", where, arrived, weights)
    coeffs = share_slabs(from_line_set(where, gather_lines(modes[0])))
    activation, grad, *pieces = middle_columns(where, coeffs, bypass, cotangent[0])
    mixer = mixer_of(bypass_weight.T)
    parts, bypass = start_slabs(pieces, bypass_columns(grad, mixer, jnp.zeros_like(bias)))
    arrived = exchange_lines(to_lines(where, *parts))
    modes, *pairs = mode_call(back_kernel, "back_modes", where, arrived, weights, spectra)
    modes, *pairs = lax.optimization_barrier((exchange_lines(modes), *to_owners(pairs)))
    *coeffs, weight_grad = share_slabs(from_lines(where, modes), outer_sum(pairs))
    field_grad = end_columns(where, coeffs, bypass)
    return (
        activation[None],
        field_grad[None],
        weight_grad.reshape(KB, CH, CH, 2, 2 * HALF),
    )


def solution(mesh):
    placed = (
        P("dp", None, "gx", "gy"),
        P("dp", None, None, None, ("gx", "gy")),
        P(),
        P(),
        P("dp", None, "gx", "gy"),
    )
    return jax.shard_map(
        per_device,
        mesh=mesh,
        in_specs=placed,
        out_specs=(
            P("dp", None, "gx", "gy"),
            P("dp", None, "gx", "gy"),
            P("dp", None, None, None, ("gx", "gy")),
        ),
        check_vma=False,
    )
```

```python
import functools
import math

import jax
import jax.numpy as jnp
import ml_dtypes
import numpy as np
from jax import lax
from jax.experimental import pallas as pl
from jax.experimental.pallas import tpu as pltpu
from jax.sharding import PartitionSpec as P

CH = 20
NX = 256
NY = 256
NZ = 64
KX = 64
KY = 64
KZ = 12
GX = 4
GY = 8
DP = 4
XL = NX // GX
YL = NY // GY
YB = 8
STEPS = YL // YB
LANES = YB * NZ
KB = KZ // GX
ROWS = 2 * KB * YB
GROUP = 4
GROUPS = CH // GROUP
GL = GROUP * KX
WIDE = CH * KX
XB = 8
EB = 16
ORDER = (0, 2, 1, 3)

BF = jnp.bfloat16
F32 = jnp.float32


def wave(freqs, points, length):
    offsets = np.mod(freqs[:, None] * points[None, :], length)
    angle = offsets.astype(np.float32) * np.float32(2.0 * math.pi / length)
    return np.cos(angle), np.sin(angle)


def kept(count):
    index = np.arange(count)
    return np.where(index < count // 2, index, index - count)


def depth_tables():
    out = np.zeros((GX, 2, GX, KB, LANES), np.float32)
    for b in range(GX):
        for pos, delta in enumerate(ORDER):
            freqs = (b ^ delta) * KB + np.arange(KB)
            cosine, sine = wave(freqs, np.arange(NZ), NZ)
            out[b, 0, pos] = np.tile(cosine, (1, YB))
            out[b, 1, pos] = np.tile(-sine, (1, YB))
    return out.reshape(GX, 2 * KZ, LANES).astype(ml_dtypes.bfloat16)


def width_tables():
    out = np.zeros((GX, 2, XL, KX), np.float32)
    for b in range(GX):
        cosine, sine = wave(kept(KX), b * XL + np.arange(XL), NX)
        out[b, 0] = cosine.T
        out[b, 1] = sine.T
    return out.astype(ml_dtypes.bfloat16)


def line_tables():
    out = np.zeros((GY, GY, 2, 2, GX, KB, STEPS, 2, KB, YB), np.float32)
    fy = kept(KY)
    for g in range(GY):
        cosine, sine = wave(fy, g * YL + np.arange(YL), NY)
        cosine = cosine.reshape(GX, GY, 2, STEPS, YB)
        sine = sine.reshape(GX, GY, 2, STEPS, YB)
        for i in range(KB):
            for owner in range(GY):
                for q in range(2):
                    c = cosine[:, owner, q]
                    s = sine[:, owner, q]
                    out[g, owner, q, 0, :, i, :, 0, i] = c
                    out[g, owner, q, 0, :, i, :, 1, i] = s
                    out[g, owner, q, 1, :, i, :, 0, i] = -s
                    out[g, owner, q, 1, :, i, :, 1, i] = c
    return out.reshape(GY, GY * 48, STEPS * ROWS).astype(ml_dtypes.bfloat16)


DEPTH = depth_tables()
WIDTH = width_tables()
LINE = line_tables()
SPREAD = np.kron(np.eye(CH), np.ones((XB, 1))).astype(ml_dtypes.bfloat16)
SAME = np.kron(np.ones((CH, CH)), np.eye(XB)).astype(ml_dtypes.bfloat16)


def dot(left, right, left_dim=1, right_dim=0):
    return lax.dot_general(
        left, right, (((left_dim,), (right_dim,)), ((), ())), preferred_element_type=F32
    )


def fill_tables(strip_ref, wide_ref, depth_ref, tall_ref, long_ref):
    strips = jnp.broadcast_to(strip_ref[0].astype(F32)[:, None, :], (2 * KZ, YB, LANES))
    row = lax.broadcasted_iota(jnp.int32, (2 * KZ, YB, LANES), 1)
    column = lax.broadcasted_iota(jnp.int32, (2 * KZ, YB, LANES), 2) // NZ
    blocks = jnp.where(row == column, strips, 0.0)
    depth_ref[...] = blocks.reshape(2 * KZ * YB, LANES).astype(BF)
    rows = lax.broadcasted_iota(jnp.int32, (GL, GL), 0) // XL
    columns = lax.broadcasted_iota(jnp.int32, (GL, GL), 1) // KX
    for part in range(2):
        strip = wide_ref[0, part].astype(F32)
        full = jnp.concatenate([jnp.concatenate([strip] * GROUP, axis=1)] * GROUP, axis=0)
        block = jnp.where(rows == columns, full, 0.0).astype(BF)
        tall_ref[GL * part : GL * (part + 1), :] = block
        long_ref[:, GL * part : GL * (part + 1)] = block


def forward_runs(source_ref, depth_ref, tall_ref, outs, runs):
    half = KZ * YB
    part = KB * YB
    sides = []
    for y in runs:
        planes = dot(depth_ref[...], run_rows(source_ref, y), 1, 1)
        real = planes[:half]
        imag = planes[half:]
        sides.append(jnp.concatenate([real, imag], axis=1).astype(BF))
        sides.append(jnp.concatenate([imag, -real], axis=1).astype(BF))
    lines = dot(jnp.concatenate(sides, axis=0), tall_ref[...])
    for n, y in enumerate(runs):
        for pos in range(GX):
            lo = 2 * half * n + pos * part
            piece = jnp.concatenate(
                [lines[lo : lo + part], lines[half + lo : half + lo + part]], axis=0
            )
            outs[pos][y] = piece.astype(BF)


def inverse_runs(ins, depth_ref, long_ref, runs):
    part = KB * YB
    planes = []
    for y in runs:
        pieces = [ref[y].astype(F32) for ref in ins]
        real = jnp.concatenate([piece[:part] for piece in pieces], axis=0)
        imag = jnp.concatenate([piece[part:] for piece in pieces], axis=0)
        sides = jnp.concatenate(
            [jnp.concatenate([real, -imag], axis=1), jnp.concatenate([imag, real], axis=1)],
            axis=0,
        ).astype(BF)
        planes.append(dot(long_ref[...], sides, 1, 1).astype(BF))
    return dot(jnp.concatenate(planes, axis=0), depth_ref[...])


def run_rows(ref, y):
    return ref[:, :, LANES * y : LANES * (y + 1)].reshape(GROUP * XL, LANES)


def bypass_kernel(shift_ref, source_ref, mixer_ref, out_ref):
    for i in range(XL // XB):
        span = slice(i * XB, (i + 1) * XB)
        rows = source_ref[:, span, :].reshape(CH * XB, LANES)
        mixed = dot(mixer_ref[...], rows).reshape(CH, XB, LANES)
        for channel in range(CH):
            out_ref[channel, span, :] = (mixed[channel] + shift_ref[channel]).astype(BF)


def start_kernel(
    where_ref, field_ref, strip_ref, wide_ref, o0, o1, o2, o3, depth_ref, tall_ref, long_ref
):
    @pl.when(pl.program_id(0) == 0)
    def _():
        fill_tables(strip_ref, wide_ref, depth_ref, tall_ref, long_ref)

    forward_runs(field_ref, depth_ref, tall_ref, (o0, o1, o2, o3), range(STEPS))


ROOT = math.sqrt(2.0 / math.pi)
CUBE = 0.044715


def activate(upstream_ref, total_ref, act_ref, grad_ref, y):
    lanes = slice(LANES * y, LANES * (y + 1))
    for channel in range(GROUP):
        for i in range(XL // EB):
            span = slice(i * EB, (i + 1) * EB)
            x = total_ref[y, channel, span, :]
            square = x * x
            t = jnp.tanh(x * (ROOT + (ROOT * CUBE) * square))
            h = 0.5 * t + 0.5
            act = x * h
            slope = h + act * (1.0 - h) * (2.0 * ROOT + (6.0 * ROOT * CUBE) * square)
            act_ref[channel, span, lanes] = act.astype(BF)
            grad_ref[channel, span, lanes] = upstream_ref[channel, span, lanes] * slope.astype(BF)


def middle_kernel(
    where_ref, i0, i1, i2, i3, bypass_ref, upstream_ref, strip_ref, wide_ref,
    act_ref, grad_ref, o0, o1, o2, o3, depth_ref, tall_ref, long_ref, total_ref,
):
    @pl.when(pl.program_id(0) == 0)
    def _():
        fill_tables(strip_ref, wide_ref, depth_ref, tall_ref, long_ref)

    def inverse(*runs):
        values = inverse_runs((i0, i1, i2, i3), depth_ref, long_ref, runs)
        for n, y in enumerate(runs):
            lanes = slice(LANES * y, LANES * (y + 1))
            own = values[GL * n : GL * (n + 1)].reshape(GROUP, XL, LANES)
            total_ref[y] = bypass_ref[:, :, lanes].astype(F32) + own

    def forward(*runs):
        forward_runs(grad_ref, depth_ref, tall_ref, (o0, o1, o2, o3), runs)

    def activation(y):
        activate(upstream_ref, total_ref, act_ref, grad_ref, y)

    inverse(0, 1)
    activation(0)
    inverse(2, 3)
    activation(1)
    activation(2)
    forward(0, 1)
    activation(3)
    forward(2, 3)


def end_kernel(
    where_ref, i0, i1, i2, i3, bypass_ref, strip_ref, wide_ref, out_ref,
    depth_ref, tall_ref, long_ref,
):
    @pl.when(pl.program_id(0) == 0)
    def _():
        fill_tables(strip_ref, wide_ref, depth_ref, tall_ref, long_ref)

    for first in range(0, STEPS, 2):
        runs = (first, first + 1)
        values = inverse_runs((i0, i1, i2, i3), depth_ref, long_ref, runs)
        for n, y in enumerate(runs):
            lanes = slice(LANES * y, LANES * (y + 1))
            own = values[GL * n : GL * (n + 1)].reshape(GROUP, XL, LANES)
            out_ref[:, :, lanes] = (bypass_ref[:, :, lanes].astype(F32) + own).astype(BF)


def cost(micros):
    return pl.CostEstimate(flops=0, bytes_accessed=micros * 3_000_000, transcendentals=0)


def column_specs():
    columns = pl.BlockSpec((GROUP, XL, YL * NZ), lambda j, w: (j, 0, 0))
    coeffs = pl.BlockSpec((STEPS, ROWS, GL), lambda j, w: (0, 0, j))
    depth = pl.BlockSpec((1, 2 * KZ, LANES), lambda j, w: (w[1], 0, 0))
    wide = pl.BlockSpec((1, 2, XL, KX), lambda j, w: (w[1], 0, 0, 0))
    return columns, coeffs, depth, wide


COEFFS = jax.ShapeDtypeStruct((STEPS, ROWS, WIDE), BF)
COLUMNS = jax.ShapeDtypeStruct((CH, XL, YL * NZ), BF)
BLOCKS = [
    pltpu.VMEM((2 * KZ * YB, LANES), BF),
    pltpu.VMEM((2 * GL, GL), BF),
    pltpu.VMEM((GL, 2 * GL), BF),
]
TOTAL = pltpu.VMEM((STEPS, GROUP, XL, LANES), F32)
PARAMS = pltpu.CompilerParams(vmem_limit_bytes=56 * 1024 * 1024)
ALONE = pltpu.CompilerParams(vmem_limit_bytes=67_043_328)


def bypass_columns(source, mixer, shift):
    columns = pl.BlockSpec((CH, XL, LANES), lambda i: (0, 0, i))
    return pl.pallas_call(
        bypass_kernel,
        grid=(STEPS,),
        in_specs=[
            pl.BlockSpec(memory_space=pltpu.SMEM),
            columns,
            pl.BlockSpec((CH * XB, CH * XB), lambda i: (0, 0)),
        ],
        out_specs=columns,
        out_shape=COLUMNS,
        compiler_params=PARAMS,
        cost_estimate=cost(6),
        name="bypass_columns",
    )(shift, source, mixer)


def start_columns(where, field):
    columns, coeffs, depth, wide = column_specs()
    return pl.pallas_call(
        start_kernel,
        grid_spec=pltpu.PrefetchScalarGridSpec(
            num_scalar_prefetch=1,
            grid=(GROUPS,),
            in_specs=[columns, depth, wide],
            out_specs=[coeffs] * 4,
            scratch_shapes=BLOCKS,
        ),
        out_shape=[COEFFS] * 4,
        compiler_params=PARAMS,
        cost_estimate=cost(8),
        name="start_columns",
    )(where, field, jnp.asarray(DEPTH), jnp.asarray(WIDTH))


def middle_columns(where, coeffs_in, bypass, upstream):
    columns, coeffs, depth, wide = column_specs()
    return pl.pallas_call(
        middle_kernel,
        grid_spec=pltpu.PrefetchScalarGridSpec(
            num_scalar_prefetch=1,
            grid=(GROUPS,),
            in_specs=[coeffs] * 4 + [columns, columns, depth, wide],
            out_specs=[columns, columns] + [coeffs] * 4,
            scratch_shapes=BLOCKS + [TOTAL],
        ),
        out_shape=[COLUMNS, COLUMNS] + [COEFFS] * 4,
        compiler_params=PARAMS,
        cost_estimate=cost(19),
        name="middle_columns",
    )(where, *coeffs_in, bypass, upstream, jnp.asarray(DEPTH), jnp.asarray(WIDTH))


def end_columns(where, coeffs_in, bypass):
    columns, coeffs, depth, wide = column_specs()
    return pl.pallas_call(
        end_kernel,
        grid_spec=pltpu.PrefetchScalarGridSpec(
            num_scalar_prefetch=1,
            grid=(GROUPS,),
            in_specs=[coeffs] * 4 + [columns, depth, wide],
            out_specs=columns,
            scratch_shapes=BLOCKS,
        ),
        out_shape=COLUMNS,
        compiler_params=ALONE,
        cost_estimate=cost(10),
        name="end_columns",
    )(where, *coeffs_in, bypass, jnp.asarray(DEPTH), jnp.asarray(WIDTH))


def order_table(where_ref, table_ref, order_ref):
    for k in range(GY):
        owner = ((where_ref[2] + (k & 6)) & 7) ^ (k & 1)
        start = pl.multiple_of(owner * 48, 16)
        order_ref[48 * k : 48 * (k + 1)] = table_ref[0, pl.ds(start, 48), :]


def line_kernel(where_ref, a_ref, b_ref, c_ref, table_ref, out_ref):
    for j in range(GROUPS):
        lanes = slice(GL * j, GL * (j + 1))
        parts = [ref[:, :, lanes].astype(F32) for ref in (a_ref, b_ref, c_ref)]
        rows = (parts[0] + parts[1] + parts[2]).astype(BF).reshape(STEPS * ROWS, GL)
        out_ref[:, :, lanes] = dot(table_ref[0], rows).astype(BF).reshape(GY, 48, GL)


def unline_set_kernel(where_ref, *refs):
    *modes_refs, table_ref, out_ref, order_ref = refs
    for k in range(GY):
        owner = ((where_ref[2] + (k & 6)) & 7) ^ (k & 1)
        start = pl.multiple_of(owner * 48, 16)
        order_ref[48 * k : 48 * (k + 1)] = table_ref[0, pl.ds(start, 48), :]
    for j in range(GROUPS):
        lanes = slice(GL * j, GL * (j + 1))
        rows = jnp.concatenate([ref[:, lanes] for ref in modes_refs], axis=0)
        out_ref[:, :, lanes] = dot(order_ref[...], rows, 0, 0).astype(BF).reshape(STEPS, ROWS, GL)


def line_call(kernel, name, where, ins, out, scratch=()):
    whole = pl.BlockSpec(ins[0].shape, lambda i, w: (0,) * ins[0].ndim)
    table = pl.BlockSpec((1, GY * 48, STEPS * ROWS), lambda i, w: (w[2], 0, 0))
    return pl.pallas_call(
        kernel,
        grid_spec=pltpu.PrefetchScalarGridSpec(
            num_scalar_prefetch=1,
            grid=(1,),
            in_specs=[whole] * len(ins) + [table],
            out_specs=pl.BlockSpec(out.shape, lambda i, w: (0, 0, 0)),
            scratch_shapes=list(scratch),
        ),
        out_shape=out,
        compiler_params=ALONE,
        cost_estimate=cost(3),
        name=name,
    )(where, *ins, jnp.asarray(LINE))


def to_lines(where, *parts):
    out = jax.ShapeDtypeStruct((GY, 48, WIDE), BF)
    return line_call(line_kernel, "to_lines", where, parts, out)


def from_line_set(where, modes):
    order = pltpu.VMEM((GY * 48, STEPS * ROWS), BF)
    return line_call(unline_set_kernel, "from_line_set", where, modes, COEFFS, [order])


UNROLL = 4
SETS = GX * KB
PAIR = 2 * CH
HALF = KX


def low_lanes():
    return lax.broadcasted_iota(jnp.int32, (SETS, 2 * HALF), 1) < HALF


def gather_modes(arrived, sum_ref, modes_ref, scale=None):
    total = arrived[0].astype(F32)
    for i in range(1, GY):
        total = total + arrived[i].astype(F32)
    sum_ref[...] = total.astype(BF).astype(F32)
    low = low_lanes()
    for j in range(CH // 2):
        lanes = slice(2 * HALF * j, 2 * HALF * (j + 1))
        for part in range(2):
            first = sum_ref[part * SETS : (part + 1) * SETS, lanes]
            second = sum_ref[(2 + part) * SETS : (3 + part) * SETS, lanes]
            if scale is not None:
                first = first * scale
                second = second * scale
            even = jnp.where(low, first, pltpu.roll(second, HALF, 1))
            odd = jnp.where(low, pltpu.roll(first, HALF, 1), second)
            modes_ref[pl.ds(4 * j + part, SETS, stride=PAIR), :] = even
            modes_ref[pl.ds(4 * j + 2 + part, SETS, stride=PAIR), :] = odd


def spread_modes(modes_ref, sum_ref, out_ref, scale=None):
    low = low_lanes()
    for j in range(CH // 2):
        lanes = slice(2 * HALF * j, 2 * HALF * (j + 1))
        for part in range(2):
            even = modes_ref[pl.ds(4 * j + part, SETS, stride=PAIR), :]
            odd = modes_ref[pl.ds(4 * j + 2 + part, SETS, stride=PAIR), :]
            if scale is not None:
                even = even * scale
                odd = odd * scale
            sum_ref[part * SETS : (part + 1) * SETS, lanes] = jnp.where(
                low, even, pltpu.roll(odd, HALF, 1)
            )
            sum_ref[(2 + part) * SETS : (3 + part) * SETS, lanes] = jnp.where(
                low, pltpu.roll(even, HALF, 1), odd
            )
    modes = sum_ref[...].astype(BF)
    for copy in range(out_ref.shape[0]):
        out_ref[copy] = modes


def fold_scale(where_ref):
    kz = where_ref[1] * KB + lax.broadcasted_iota(jnp.int32, (SETS, 2 * HALF), 0) % KB
    return jnp.where(kz == 0, 1.0, 2.0).astype(F32) / float(NX * NY * NZ)


def turned(rows):
    even = lax.broadcasted_iota(jnp.int32, rows.shape, 0) % 2 == 0
    up = pltpu.roll(rows, PAIR - 1, 0)
    down = pltpu.roll(rows, 1, 0)
    return jnp.where(even, -up, down)


def hand_out(where_ref, modes_ref, outs):
    for k in range(DP):
        chunk = lax.rem(where_ref[0] + k, DP)
        start = pl.multiple_of(chunk * KB * PAIR, 8)
        outs[k][...] = modes_ref[pl.ds(start, KB * PAIR), :].astype(BF)


def set_row(where_ref, k):
    block = (lax.rem(where_ref[0] + k, DP) ^ (2 * (where_ref[1] & 1))) * KB + pl.program_id(0)
    return pl.multiple_of(block * PAIR, 8)


def take_weights(first_ref, rest_ref, held_ref):
    @pl.when(pl.program_id(0) == 0)
    def _():
        held_ref[...] = first_ref[...]

    @pl.when(pl.program_id(0) > 0)
    def _():
        held_ref[...] = rest_ref[...]


def mix_kernel(
    where_ref, arrived_ref, w0, w1, w3, first_ref, rest_ref, out_ref, u0, u1, u2, u3,
    sum_ref, in_ref, mix_ref, w2,
):
    step = pl.program_id(0)

    @pl.when(step == 0)
    def _():
        gather_modes(arrived_ref, sum_ref, in_ref)
        hand_out(where_ref, in_ref, [ref.at[0] for ref in (u0, u1, u2, u3)])

    take_weights(first_ref, rest_ref, w2)
    for k, weight_ref in enumerate((w0, w1, w2, w3)):
        base = set_row(where_ref, k)

        def add(i, totals, weight_ref=weight_ref, base=base):
            by_real, by_imag = totals
            for r in range(UNROLL):
                c = i * UNROLL + r
                weight = weight_ref[0, c].astype(F32)
                by_real = by_real + weight * in_ref[pl.ds(base + 2 * c, 1), :]
                by_imag = by_imag + weight * in_ref[pl.ds(base + 2 * c + 1, 1), :]
            return by_real, by_imag

        zero = jnp.zeros((PAIR, 2 * HALF), F32)
        by_real, by_imag = lax.fori_loop(0, CH // UNROLL, add, (zero, zero))
        mix_ref[pl.ds(base, PAIR), :] = (by_real + turned(by_imag)).astype(BF).astype(F32)

    @pl.when(step == KB - 1)
    def _():
        spread_modes(mix_ref, sum_ref, out_ref, fold_scale(where_ref))


def back_kernel(
    where_ref, arrived_ref, w0, w1, w3, first_ref, rest_ref, s0, s1, s2, s3,
    out_ref, u0, u1, u2, u3, sum_ref, in_ref, mix_ref, w2,
):
    step = pl.program_id(0)

    @pl.when(step == 0)
    def _():
        gather_modes(arrived_ref, sum_ref, in_ref, fold_scale(where_ref))
        hand_out(where_ref, in_ref, [ref.at[1] for ref in (u0, u1, u2, u3)])
        for spec_ref, ref in zip((s0, s1, s2, s3), (u0, u1, u2, u3)):
            ref[0] = spec_ref[0]

    take_weights(first_ref, rest_ref, w2)
    for k, weight_ref in enumerate((w0, w1, w2, w3)):
        base = set_row(where_ref, k)
        grad = in_ref[pl.ds(base, PAIR), :]
        other = -turned(grad)

        @pl.loop(0, CH // UNROLL)
        def _(i, weight_ref=weight_ref, base=base, grad=grad, other=other):
            for r in range(UNROLL):
                c = i * UNROLL + r
                weight = weight_ref[0, c].astype(F32)
                mix_ref[pl.ds(base + 2 * c, 1), :] = jnp.sum(weight * grad, axis=0, keepdims=True)
                mix_ref[pl.ds(base + 2 * c + 1, 1), :] = jnp.sum(
                    weight * other, axis=0, keepdims=True
                )

    @pl.when(step == KB - 1)
    def _():
        spread_modes(mix_ref, sum_ref, out_ref)


def mode_call(kernel, name, where, arrived, weights, spectra=()):
    sets = 2 if spectra else 1
    weight = (1, CH, PAIR, 2 * HALF)

    def chunk(n):
        return pl.BlockSpec((n, KB * PAIR, 2 * HALF), lambda i, w: (0, 0, 0))

    return pl.pallas_call(
        kernel,
        grid_spec=pltpu.PrefetchScalarGridSpec(
            num_scalar_prefetch=1,
            grid=(KB,),
            in_specs=[pl.BlockSpec((GY, 48, WIDE), lambda i, w: (0, 0, 0))]
            + [pl.BlockSpec(weight, lambda i, w: (i, 0, 0, 0))] * 3
            + [pl.BlockSpec(weight, lambda i, w: (0, 0, 0, 0))]
            + [pl.BlockSpec(weight, lambda i, w: (lax.max(i, 1) - 1, 0, 0, 0))]
            + [chunk(1)] * len(spectra),
            out_specs=[pl.BlockSpec((1, 48, WIDE), lambda i, w: (0, 0, 0))]
            + [chunk(sets)] * 4,
            scratch_shapes=[
                pltpu.VMEM((48, WIDE), F32),
                pltpu.VMEM((SETS * PAIR, 2 * HALF), F32),
                pltpu.VMEM((SETS * PAIR, 2 * HALF), F32),
                pltpu.VMEM(weight, BF),
            ],
        ),
        out_shape=[jax.ShapeDtypeStruct((1, 48, WIDE), BF)]
        + [jax.ShapeDtypeStruct((sets, KB * PAIR, 2 * HALF), BF)] * 4,
        compiler_params=ALONE,
        cost_estimate=cost(5),
        name=name,
    )(where, arrived, *weights, *spectra)


def outer_kernel(p0, p1, p2, p3, out_ref, spec_ref):
    pairs = (p0, p1, p2, p3)
    for k, ref in enumerate(pairs):
        spec_ref[k] = ref[0].astype(F32)
    for i in range(KB):
        grads = []
        others = []
        for ref in pairs:
            grad = ref[1].astype(F32)[i * PAIR : (i + 1) * PAIR]
            grads.append(grad)
            others.append(-turned(grad))

        @pl.loop(0, CH)
        def _(c):
            row = i * PAIR + 2 * c
            total = jnp.zeros((PAIR, 2 * HALF), F32)
            for k in range(DP):
                total = total + spec_ref[k, pl.ds(row, 1), :] * grads[k]
                total = total + spec_ref[k, pl.ds(row + 1, 1), :] * others[k]
            out_ref[i, c] = total


def outer_sum(pairs):
    return pl.pallas_call(
        outer_kernel,
        out_shape=jax.ShapeDtypeStruct((KB, CH, PAIR, 2 * HALF), F32),
        scratch_shapes=[pltpu.VMEM((DP, KB * PAIR, 2 * HALF), F32)],
        cost_estimate=cost(3),
        name="outer_sum",
    )(*pairs)


def swap(values, bit):
    return lax.ppermute(values, "gx", [(i, i ^ bit) for i in range(GX)])


def start_slabs(pieces, beside):
    own, far, near, across = pieces
    far_sum = (far.astype(F32) + swap(across, 1).astype(F32)).astype(BF)
    arrived, beside = lax.optimization_barrier((swap(far_sum, 2), beside))
    return (own, swap(near, 1), arrived), beside


def share_slabs(own, *beside):
    far, *beside = lax.optimization_barrier((swap(own, 2), *beside))
    return own, far, swap(own, 1), swap(far, 1), *beside


def gather_weights(weight):
    def fetch(part, k):
        moved = lax.ppermute(part, "dp", [((a + k) % DP, a) for a in range(DP)])
        return moved.reshape(-1, CH, PAIR, 2 * HALF)

    own = weight.reshape(KB, CH, PAIR, 2 * HALF)
    return [own, fetch(weight, 1), fetch(weight, 3), fetch(weight[:1], 2), fetch(weight[1:], 2)]


def gather_lines(modes):
    held = [modes, lax.ppermute(modes, "gy", [(g ^ 1, g) for g in range(GY)])]
    for step in range(2, GY, 2):
        pairs = [((g + step) % GY, g) for g in range(GY)]
        held += [lax.ppermute(part, "gy", pairs) for part in held[:2]]
    return held


def exchange_lines(parts):
    return lax.all_to_all(parts, "gy", split_axis=0, concat_axis=0, tiled=True)


def to_owners(chunks):
    moved = []
    for k, chunk in enumerate(chunks):
        pairs = [
            (a * GX + b, b * GX + (a + k) % DP) for a in range(DP) for b in range(GX)
        ]
        moved.append(lax.ppermute(chunk, ("dp", "gx"), pairs))
    return moved


def per_device(field, spectral_weight, bypass_weight, bias, cotangent):
    where = jnp.stack(
        [lax.axis_index("dp"), lax.axis_index("gx"), lax.axis_index("gy")]
    ).astype(jnp.int32)
    turn = [(a * GX + b, (b ^ (2 * (a % 2))) * GX + a) for a in range(DP) for b in range(GX)]
    weight = lax.ppermute(spectral_weight, ("dp", "gx"), turn)
    spread = jnp.asarray(SPREAD)

    def mixer_of(matrix):
        wide = dot(dot(spread, matrix).astype(BF), spread, 1, 1)
        return wide.astype(BF) * jnp.asarray(SAME)

    values = field[0]
    *pieces, weight = lax.optimization_barrier((*start_columns(where, values), weight))
    parts, bypass = start_slabs(pieces, bypass_columns(values, mixer_of(bypass_weight), bias))
    weights = gather_weights(weight)
    lines, *weights[1:4] = lax.optimization_barrier((to_lines(where, *parts), *weights[1:4]))
    arrived = exchange_lines(lines)
    modes, *spectra = mode_call(mix_kernel, "mix_modes", where, arrived, weights)
    coeffs = share_slabs(from_line_set(where, gather_lines(modes[0])))
    activation, grad, *pieces = middle_columns(where, coeffs, bypass, cotangent[0])
    mixer = mixer_of(bypass_weight.T)
    parts, bypass = start_slabs(pieces, bypass_columns(grad, mixer, jnp.zeros_like(bias)))
    arrived = exchange_lines(to_lines(where, *parts))
    modes, *pairs = mode_call(back_kernel, "back_modes", where, arrived, weights, spectra)
    coeffs = share_slabs(from_line_set(where, gather_lines(modes[0])))
    field_grad = end_columns(where, coeffs, bypass)
    field_grad, *pairs = lax.optimization_barrier((field_grad, *to_owners(pairs)))
    weight_grad = outer_sum(pairs)
    return (
        activation[None],
        field_grad[None],
        weight_grad.reshape(KB, CH, CH, 2, 2 * HALF),
    )


def solution(mesh):
    placed = (
        P("dp", None, "gx", "gy"),
        P("dp", None, None, None, ("gx", "gy")),
        P(),
        P(),
        P("dp", None, "gx", "gy"),
    )
    return jax.shard_map(
        per_device,
        mesh=mesh,
        in_specs=placed,
        out_specs=(
            P("dp", None, "gx", "gy"),
            P("dp", None, "gx", "gy"),
            P("dp", None, None, None, ("gx", "gy")),
        ),
        check_vma=False,
    )
```

```python
import functools
import math

import jax
import jax.numpy as jnp
import ml_dtypes
import numpy as np
from jax import lax
from jax.experimental import pallas as pl
from jax.experimental.pallas import tpu as pltpu
from jax.sharding import PartitionSpec as P

CH = 20
NX = 256
NY = 256
NZ = 64
KX = 64
KY = 64
KZ = 12
GX = 4
GY = 8
DP = 4
XL = NX // GX
YL = NY // GY
YB = 8
STEPS = YL // YB
LANES = YB * NZ
KB = KZ // GX
ROWS = 2 * KB * YB
GROUP = 4
GROUPS = CH // GROUP
GL = GROUP * KX
WIDE = CH * KX
XB = 8
EB = 16
ORDER = (0, 2, 1, 3)

BF = jnp.bfloat16
F32 = jnp.float32


def wave(freqs, points, length):
    offsets = np.mod(freqs[:, None] * points[None, :], length)
    angle = offsets.astype(np.float32) * np.float32(2.0 * math.pi / length)
    return np.cos(angle), np.sin(angle)


def kept(count):
    index = np.arange(count)
    return np.where(index < count // 2, index, index - count)


def depth_tables():
    out = np.zeros((GX, 2, GX, KB, LANES), np.float32)
    for b in range(GX):
        for pos, delta in enumerate(ORDER):
            freqs = (b ^ delta) * KB + np.arange(KB)
            cosine, sine = wave(freqs, np.arange(NZ), NZ)
            out[b, 0, pos] = np.tile(cosine, (1, YB))
            out[b, 1, pos] = np.tile(-sine, (1, YB))
    return out.reshape(GX, 2 * KZ, LANES).astype(ml_dtypes.bfloat16)


def width_tables():
    out = np.zeros((GX, 2, XL, KX), np.float32)
    for b in range(GX):
        cosine, sine = wave(kept(KX), b * XL + np.arange(XL), NX)
        out[b, 0] = cosine.T
        out[b, 1] = sine.T
    return out.astype(ml_dtypes.bfloat16)


def line_tables():
    out = np.zeros((GY, GY, 2, 2, GX, KB, STEPS, 2, KB, YB), np.float32)
    fy = kept(KY)
    for g in range(GY):
        cosine, sine = wave(fy, g * YL + np.arange(YL), NY)
        cosine = cosine.reshape(GX, GY, 2, STEPS, YB)
        sine = sine.reshape(GX, GY, 2, STEPS, YB)
        for i in range(KB):
            for owner in range(GY):
                for q in range(2):
                    c = cosine[:, owner, q]
                    s = sine[:, owner, q]
                    out[g, owner, q, 0, :, i, :, 0, i] = c
                    out[g, owner, q, 0, :, i, :, 1, i] = s
                    out[g, owner, q, 1, :, i, :, 0, i] = -s
                    out[g, owner, q, 1, :, i, :, 1, i] = c
    return out.reshape(GY, GY * 48, STEPS * ROWS).astype(ml_dtypes.bfloat16)


DEPTH = depth_tables()
WIDTH = width_tables()
LINE = line_tables()
SPREAD = np.kron(np.eye(CH), np.ones((XB, 1))).astype(ml_dtypes.bfloat16)
SAME = np.kron(np.ones((CH, CH)), np.eye(XB)).astype(ml_dtypes.bfloat16)


def dot(left, right, left_dim=1, right_dim=0):
    return lax.dot_general(
        left, right, (((left_dim,), (right_dim,)), ((), ())), preferred_element_type=F32
    )


def fill_tables(strip_ref, wide_ref, depth_ref, tall_ref, long_ref):
    strips = jnp.broadcast_to(strip_ref[0].astype(F32)[:, None, :], (2 * KZ, YB, LANES))
    row = lax.broadcasted_iota(jnp.int32, (2 * KZ, YB, LANES), 1)
    column = lax.broadcasted_iota(jnp.int32, (2 * KZ, YB, LANES), 2) // NZ
    blocks = jnp.where(row == column, strips, 0.0)
    depth_ref[...] = blocks.reshape(2 * KZ * YB, LANES).astype(BF)
    rows = lax.broadcasted_iota(jnp.int32, (GL, GL), 0) // XL
    columns = lax.broadcasted_iota(jnp.int32, (GL, GL), 1) // KX
    for part in range(2):
        strip = wide_ref[0, part].astype(F32)
        full = jnp.concatenate([jnp.concatenate([strip] * GROUP, axis=1)] * GROUP, axis=0)
        block = jnp.where(rows == columns, full, 0.0).astype(BF)
        tall_ref[GL * part : GL * (part + 1), :] = block
        long_ref[:, GL * part : GL * (part + 1)] = block


def forward_runs(source_ref, depth_ref, tall_ref, outs, runs):
    half = KZ * YB
    part = KB * YB
    sides = []
    for y in runs:
        planes = dot(depth_ref[...], run_rows(source_ref, y), 1, 1)
        real = planes[:half]
        imag = planes[half:]
        sides.append(jnp.concatenate([real, imag], axis=1).astype(BF))
        sides.append(jnp.concatenate([imag, -real], axis=1).astype(BF))
    lines = dot(jnp.concatenate(sides, axis=0), tall_ref[...])
    for n, y in enumerate(runs):
        for pos in range(GX):
            lo = 2 * half * n + pos * part
            piece = jnp.concatenate(
                [lines[lo : lo + part], lines[half + lo : half + lo + part]], axis=0
            )
            outs[pos][y] = piece.astype(BF)


def inverse_runs(ins, depth_ref, long_ref, runs):
    part = KB * YB
    planes = []
    for y in runs:
        pieces = [ref[y].astype(F32) for ref in ins]
        real = jnp.concatenate([piece[:part] for piece in pieces], axis=0)
        imag = jnp.concatenate([piece[part:] for piece in pieces], axis=0)
        sides = jnp.concatenate(
            [jnp.concatenate([real, -imag], axis=1), jnp.concatenate([imag, real], axis=1)],
            axis=0,
        ).astype(BF)
        planes.append(dot(long_ref[...], sides, 1, 1).astype(BF))
    return dot(jnp.concatenate(planes, axis=0), depth_ref[...])


def run_rows(ref, y):
    return ref[:, :, LANES * y : LANES * (y + 1)].reshape(GROUP * XL, LANES)


def bypass_kernel(shift_ref, source_ref, mixer_ref, out_ref):
    for i in range(XL // XB):
        span = slice(i * XB, (i + 1) * XB)
        rows = source_ref[:, span, :].reshape(CH * XB, LANES)
        mixed = dot(mixer_ref[...], rows).reshape(CH, XB, LANES)
        for channel in range(CH):
            out_ref[channel, span, :] = (mixed[channel] + shift_ref[channel]).astype(BF)


def start_kernel(
    where_ref, field_ref, strip_ref, wide_ref, o0, o1, o2, o3, depth_ref, tall_ref, long_ref
):
    @pl.when(pl.program_id(0) == 0)
    def _():
        fill_tables(strip_ref, wide_ref, depth_ref, tall_ref, long_ref)

    forward_runs(field_ref, depth_ref, tall_ref, (o0, o1, o2, o3), range(STEPS))


ROOT = math.sqrt(2.0 / math.pi)
CUBE = 0.044715


def activate(upstream_ref, total_ref, act_ref, grad_ref, y):
    lanes = slice(LANES * y, LANES * (y + 1))
    for channel in range(GROUP):
        for i in range(XL // EB):
            span = slice(i * EB, (i + 1) * EB)
            x = total_ref[y, channel, span, :]
            square = x * x
            t = jnp.tanh(x * (ROOT + (ROOT * CUBE) * square))
            h = 0.5 * t + 0.5
            act = x * h
            slope = h + act * (1.0 - h) * (2.0 * ROOT + (6.0 * ROOT * CUBE) * square)
            act_ref[channel, span, lanes] = act.astype(BF)
            grad_ref[channel, span, lanes] = upstream_ref[channel, span, lanes] * slope.astype(BF)


def middle_kernel(
    where_ref, i0, i1, i2, i3, bypass_ref, upstream_ref, strip_ref, wide_ref,
    act_ref, grad_ref, o0, o1, o2, o3, depth_ref, tall_ref, long_ref, total_ref,
):
    @pl.when(pl.program_id(0) == 0)
    def _():
        fill_tables(strip_ref, wide_ref, depth_ref, tall_ref, long_ref)

    def inverse(*runs):
        values = inverse_runs((i0, i1, i2, i3), depth_ref, long_ref, runs)
        for n, y in enumerate(runs):
            lanes = slice(LANES * y, LANES * (y + 1))
            own = values[GL * n : GL * (n + 1)].reshape(GROUP, XL, LANES)
            total_ref[y] = bypass_ref[:, :, lanes].astype(F32) + own

    def forward(*runs):
        forward_runs(grad_ref, depth_ref, tall_ref, (o0, o1, o2, o3), runs)

    def activation(y):
        activate(upstream_ref, total_ref, act_ref, grad_ref, y)

    inverse(0, 1)
    activation(0)
    inverse(2, 3)
    activation(1)
    activation(2)
    forward(0, 1)
    activation(3)
    forward(2, 3)


def end_kernel(
    where_ref, i0, i1, i2, i3, bypass_ref, strip_ref, wide_ref, out_ref,
    depth_ref, tall_ref, long_ref,
):
    @pl.when(pl.program_id(0) == 0)
    def _():
        fill_tables(strip_ref, wide_ref, depth_ref, tall_ref, long_ref)

    for first in range(0, STEPS, 2):
        runs = (first, first + 1)
        values = inverse_runs((i0, i1, i2, i3), depth_ref, long_ref, runs)
        for n, y in enumerate(runs):
            lanes = slice(LANES * y, LANES * (y + 1))
            own = values[GL * n : GL * (n + 1)].reshape(GROUP, XL, LANES)
            out_ref[:, :, lanes] = (bypass_ref[:, :, lanes].astype(F32) + own).astype(BF)


def cost(micros):
    return pl.CostEstimate(flops=0, bytes_accessed=micros * 3_000_000, transcendentals=0)


def column_specs():
    columns = pl.BlockSpec((GROUP, XL, YL * NZ), lambda j, w: (j, 0, 0))
    coeffs = pl.BlockSpec((STEPS, ROWS, GL), lambda j, w: (0, 0, j))
    depth = pl.BlockSpec((1, 2 * KZ, LANES), lambda j, w: (w[1], 0, 0))
    wide = pl.BlockSpec((1, 2, XL, KX), lambda j, w: (w[1], 0, 0, 0))
    return columns, coeffs, depth, wide


COEFFS = jax.ShapeDtypeStruct((STEPS, ROWS, WIDE), BF)
COLUMNS = jax.ShapeDtypeStruct((CH, XL, YL * NZ), BF)
BLOCKS = [
    pltpu.VMEM((2 * KZ * YB, LANES), BF),
    pltpu.VMEM((2 * GL, GL), BF),
    pltpu.VMEM((GL, 2 * GL), BF),
]
TOTAL = pltpu.VMEM((STEPS, GROUP, XL, LANES), F32)
PARAMS = pltpu.CompilerParams(vmem_limit_bytes=56 * 1024 * 1024)
ALONE = pltpu.CompilerParams(vmem_limit_bytes=67_043_328)


def bypass_columns(source, mixer, shift):
    columns = pl.BlockSpec((CH, XL, LANES), lambda i: (0, 0, i))
    return pl.pallas_call(
        bypass_kernel,
        grid=(STEPS,),
        in_specs=[
            pl.BlockSpec(memory_space=pltpu.SMEM),
            columns,
            pl.BlockSpec((CH * XB, CH * XB), lambda i: (0, 0)),
        ],
        out_specs=columns,
        out_shape=COLUMNS,
        compiler_params=PARAMS,
        cost_estimate=cost(6),
        name="bypass_columns",
    )(shift, source, mixer)


def start_columns(where, field):
    columns, coeffs, depth, wide = column_specs()
    return pl.pallas_call(
        start_kernel,
        grid_spec=pltpu.PrefetchScalarGridSpec(
            num_scalar_prefetch=1,
            grid=(GROUPS,),
            in_specs=[columns, depth, wide],
            out_specs=[coeffs] * 4,
            scratch_shapes=BLOCKS,
        ),
        out_shape=[COEFFS] * 4,
        compiler_params=PARAMS,
        cost_estimate=cost(8),
        name="start_columns",
    )(where, field, jnp.asarray(DEPTH), jnp.asarray(WIDTH))


def middle_columns(where, coeffs_in, bypass, upstream):
    columns, coeffs, depth, wide = column_specs()
    return pl.pallas_call(
        middle_kernel,
        grid_spec=pltpu.PrefetchScalarGridSpec(
            num_scalar_prefetch=1,
            grid=(GROUPS,),
            in_specs=[coeffs] * 4 + [columns, columns, depth, wide],
            out_specs=[columns, columns] + [coeffs] * 4,
            scratch_shapes=BLOCKS + [TOTAL],
        ),
        out_shape=[COLUMNS, COLUMNS] + [COEFFS] * 4,
        compiler_params=PARAMS,
        cost_estimate=cost(19),
        name="middle_columns",
    )(where, *coeffs_in, bypass, upstream, jnp.asarray(DEPTH), jnp.asarray(WIDTH))


def end_columns(where, coeffs_in, bypass):
    columns, coeffs, depth, wide = column_specs()
    return pl.pallas_call(
        end_kernel,
        grid_spec=pltpu.PrefetchScalarGridSpec(
            num_scalar_prefetch=1,
            grid=(GROUPS,),
            in_specs=[coeffs] * 4 + [columns, depth, wide],
            out_specs=columns,
            scratch_shapes=BLOCKS,
        ),
        out_shape=COLUMNS,
        compiler_params=ALONE,
        cost_estimate=cost(10),
        name="end_columns",
    )(where, *coeffs_in, bypass, jnp.asarray(DEPTH), jnp.asarray(WIDTH))


def order_table(where_ref, table_ref, order_ref):
    for k in range(GY):
        owner = ((where_ref[2] + (k & 6)) & 7) ^ (k & 1)
        start = pl.multiple_of(owner * 48, 16)
        order_ref[48 * k : 48 * (k + 1)] = table_ref[0, pl.ds(start, 48), :]


def line_kernel(where_ref, a_ref, b_ref, c_ref, table_ref, out_ref):
    for j in range(GROUPS):
        lanes = slice(GL * j, GL * (j + 1))
        parts = [ref[:, :, lanes].astype(F32) for ref in (a_ref, b_ref, c_ref)]
        rows = (parts[0] + parts[1] + parts[2]).astype(BF).reshape(STEPS * ROWS, GL)
        out_ref[:, :, lanes] = dot(table_ref[0], rows).astype(BF).reshape(GY, 48, GL)


def unline_kernel(where_ref, modes_ref, table_ref, out_ref):
    for j in range(GROUPS):
        lanes = slice(GL * j, GL * (j + 1))
        rows = modes_ref[:, :, lanes].reshape(GY * 48, GL)
        out_ref[:, :, lanes] = dot(table_ref[0], rows, 0, 0).astype(BF).reshape(STEPS, ROWS, GL)


def unline_set_kernel(where_ref, *refs):
    *modes_refs, table_ref, out_ref, order_ref = refs
    for k in range(GY):
        owner = ((where_ref[2] + (k & 6)) & 7) ^ (k & 1)
        start = pl.multiple_of(owner * 48, 16)
        order_ref[48 * k : 48 * (k + 1)] = table_ref[0, pl.ds(start, 48), :]
    for j in range(GROUPS):
        lanes = slice(GL * j, GL * (j + 1))
        rows = jnp.concatenate([ref[:, lanes] for ref in modes_refs], axis=0)
        out_ref[:, :, lanes] = dot(order_ref[...], rows, 0, 0).astype(BF).reshape(STEPS, ROWS, GL)


def line_call(kernel, name, where, ins, out, scratch=()):
    whole = pl.BlockSpec(ins[0].shape, lambda i, w: (0,) * ins[0].ndim)
    table = pl.BlockSpec((1, GY * 48, STEPS * ROWS), lambda i, w: (w[2], 0, 0))
    return pl.pallas_call(
        kernel,
        grid_spec=pltpu.PrefetchScalarGridSpec(
            num_scalar_prefetch=1,
            grid=(1,),
            in_specs=[whole] * len(ins) + [table],
            out_specs=pl.BlockSpec(out.shape, lambda i, w: (0, 0, 0)),
            scratch_shapes=list(scratch),
        ),
        out_shape=out,
        compiler_params=ALONE,
        cost_estimate=cost(3),
        name=name,
    )(where, *ins, jnp.asarray(LINE))


def to_lines(where, *parts):
    out = jax.ShapeDtypeStruct((GY, 48, WIDE), BF)
    return line_call(line_kernel, "to_lines", where, parts, out)


def from_lines(where, modes):
    return line_call(unline_kernel, "from_lines", where, (modes,), COEFFS)


def from_line_set(where, modes):
    order = pltpu.VMEM((GY * 48, STEPS * ROWS), BF)
    return line_call(unline_set_kernel, "from_line_set", where, modes, COEFFS, [order])


UNROLL = 10
SETS = GX * KB
PAIR = 2 * CH
HALF = KX


def low_lanes():
    return lax.broadcasted_iota(jnp.int32, (SETS, 2 * HALF), 1) < HALF


def gather_modes(arrived, sum_ref, modes_ref, scale=None):
    total = arrived[0].astype(F32)
    for i in range(1, GY):
        total = total + arrived[i].astype(F32)
    sum_ref[...] = total.astype(BF).astype(F32)
    low = low_lanes()
    for j in range(CH // 2):
        lanes = slice(2 * HALF * j, 2 * HALF * (j + 1))
        for part in range(2):
            first = sum_ref[part * SETS : (part + 1) * SETS, lanes]
            second = sum_ref[(2 + part) * SETS : (3 + part) * SETS, lanes]
            if scale is not None:
                first = first * scale
                second = second * scale
            even = jnp.where(low, first, pltpu.roll(second, HALF, 1))
            odd = jnp.where(low, pltpu.roll(first, HALF, 1), second)
            modes_ref[pl.ds(4 * j + part, SETS, stride=PAIR), :] = even
            modes_ref[pl.ds(4 * j + 2 + part, SETS, stride=PAIR), :] = odd


def spread_modes(modes_ref, sum_ref, out_ref, scale=None):
    low = low_lanes()
    for j in range(CH // 2):
        lanes = slice(2 * HALF * j, 2 * HALF * (j + 1))
        for part in range(2):
            even = modes_ref[pl.ds(4 * j + part, SETS, stride=PAIR), :]
            odd = modes_ref[pl.ds(4 * j + 2 + part, SETS, stride=PAIR), :]
            if scale is not None:
                even = even * scale
                odd = odd * scale
            sum_ref[part * SETS : (part + 1) * SETS, lanes] = jnp.where(
                low, even, pltpu.roll(odd, HALF, 1)
            )
            sum_ref[(2 + part) * SETS : (3 + part) * SETS, lanes] = jnp.where(
                low, pltpu.roll(even, HALF, 1), odd
            )
    modes = sum_ref[...].astype(BF)
    for copy in range(out_ref.shape[0]):
        out_ref[copy] = modes


def fold_scale(where_ref):
    kz = where_ref[1] * KB + lax.broadcasted_iota(jnp.int32, (SETS, 2 * HALF), 0) % KB
    return jnp.where(kz == 0, 1.0, 2.0).astype(F32) / float(NX * NY * NZ)


def turned(rows):
    even = lax.broadcasted_iota(jnp.int32, rows.shape, 0) % 2 == 0
    up = pltpu.roll(rows, PAIR - 1, 0)
    down = pltpu.roll(rows, 1, 0)
    return jnp.where(even, -up, down)


def hand_out(where_ref, modes_ref, outs):
    for k in range(DP):
        chunk = lax.rem(where_ref[0] + k, DP)
        start = pl.multiple_of(chunk * KB * PAIR, 8)
        outs[k][...] = modes_ref[pl.ds(start, KB * PAIR), :].astype(BF)


def set_row(where_ref, k):
    block = (lax.rem(where_ref[0] + k, DP) ^ (2 * (where_ref[1] & 1))) * KB + pl.program_id(0)
    return pl.multiple_of(block * PAIR, 8)


def mix_kernel(
    where_ref, arrived_ref, w0, w1, w2, w3, out_ref, u0, u1, u2, u3,
    sum_ref, in_ref, mix_ref,
):
    step = pl.program_id(0)

    @pl.when(step == 0)
    def _():
        gather_modes(arrived_ref, sum_ref, in_ref)
        hand_out(where_ref, in_ref, [ref.at[0] for ref in (u0, u1, u2, u3)])

    for k, weight_ref in enumerate((w0, w1, w2, w3)):
        base = set_row(where_ref, k)

        def add(i, totals, weight_ref=weight_ref, base=base):
            by_real, by_imag = totals
            for r in range(UNROLL):
                c = i * UNROLL + r
                weight = weight_ref[0, c].astype(F32)
                by_real = by_real + weight * in_ref[pl.ds(base + 2 * c, 1), :]
                by_imag = by_imag + weight * in_ref[pl.ds(base + 2 * c + 1, 1), :]
            return by_real, by_imag

        zero = jnp.zeros((PAIR, 2 * HALF), F32)
        by_real, by_imag = lax.fori_loop(0, CH // UNROLL, add, (zero, zero))
        mix_ref[pl.ds(base, PAIR), :] = (by_real + turned(by_imag)).astype(BF).astype(F32)

    @pl.when(step == KB - 1)
    def _():
        spread_modes(mix_ref, sum_ref, out_ref, fold_scale(where_ref))


def back_kernel(
    where_ref, arrived_ref, w0, w1, w2, w3, s0, s1, s2, s3, out_ref, u0, u1, u2, u3,
    sum_ref, in_ref, mix_ref,
):
    step = pl.program_id(0)

    @pl.when(step == 0)
    def _():
        gather_modes(arrived_ref, sum_ref, in_ref, fold_scale(where_ref))
        hand_out(where_ref, in_ref, [ref.at[1] for ref in (u0, u1, u2, u3)])
        for spec_ref, ref in zip((s0, s1, s2, s3), (u0, u1, u2, u3)):
            ref[0] = spec_ref[0]

    for k, weight_ref in enumerate((w0, w1, w2, w3)):
        base = set_row(where_ref, k)
        grad = in_ref[pl.ds(base, PAIR), :]
        other = -turned(grad)

        @pl.loop(0, CH // UNROLL)
        def _(i, weight_ref=weight_ref, base=base, grad=grad, other=other):
            for r in range(UNROLL):
                c = i * UNROLL + r
                weight = weight_ref[0, c].astype(F32)
                mix_ref[pl.ds(base + 2 * c, 1), :] = jnp.sum(weight * grad, axis=0, keepdims=True)
                mix_ref[pl.ds(base + 2 * c + 1, 1), :] = jnp.sum(
                    weight * other, axis=0, keepdims=True
                )

    @pl.when(step == KB - 1)
    def _():
        spread_modes(mix_ref, sum_ref, out_ref)


def mode_call(kernel, name, where, arrived, weights, spectra=()):
    sets, copies = (2, GY) if spectra else (1, 1)

    def chunk(n):
        return pl.BlockSpec((n, KB * PAIR, 2 * HALF), lambda i, w: (0, 0, 0))

    return pl.pallas_call(
        kernel,
        grid_spec=pltpu.PrefetchScalarGridSpec(
            num_scalar_prefetch=1,
            grid=(KB,),
            in_specs=[pl.BlockSpec((GY, 48, WIDE), lambda i, w: (0, 0, 0))]
            + [pl.BlockSpec((1, CH, PAIR, 2 * HALF), lambda i, w: (i, 0, 0, 0))] * 4
            + [chunk(1)] * len(spectra),
            out_specs=[pl.BlockSpec((copies, 48, WIDE), lambda i, w: (0, 0, 0))]
            + [chunk(sets)] * 4,
            scratch_shapes=[
                pltpu.VMEM((48, WIDE), F32),
                pltpu.VMEM((SETS * PAIR, 2 * HALF), F32),
                pltpu.VMEM((SETS * PAIR, 2 * HALF), F32),
            ],
        ),
        out_shape=[jax.ShapeDtypeStruct((copies, 48, WIDE), BF)]
        + [jax.ShapeDtypeStruct((sets, KB * PAIR, 2 * HALF), BF)] * 4,
        compiler_params=ALONE,
        cost_estimate=cost(5),
        name=name,
    )(where, arrived, *weights, *spectra)


def outer_kernel(p0, p1, p2, p3, out_ref, spec_ref):
    pairs = (p0, p1, p2, p3)
    for k, ref in enumerate(pairs):
        spec_ref[k] = ref[0].astype(F32)
    for i in range(KB):
        grads = []
        others = []
        for ref in pairs:
            grad = ref[1].astype(F32)[i * PAIR : (i + 1) * PAIR]
            grads.append(grad)
            others.append(-turned(grad))

        @pl.loop(0, CH)
        def _(c):
            row = i * PAIR + 2 * c
            total = jnp.zeros((PAIR, 2 * HALF), F32)
            for k in range(DP):
                total = total + spec_ref[k, pl.ds(row, 1), :] * grads[k]
                total = total + spec_ref[k, pl.ds(row + 1, 1), :] * others[k]
            out_ref[i, c] = total


def outer_sum(pairs):
    return pl.pallas_call(
        outer_kernel,
        out_shape=jax.ShapeDtypeStruct((KB, CH, PAIR, 2 * HALF), F32),
        scratch_shapes=[pltpu.VMEM((DP, KB * PAIR, 2 * HALF), F32)],
        cost_estimate=cost(3),
        name="outer_sum",
    )(*pairs)


def swap(values, bit):
    return lax.ppermute(values, "gx", [(i, i ^ bit) for i in range(GX)])


def start_slabs(pieces, beside):
    own, far, near, across = pieces
    far_sum = (far.astype(F32) + swap(across, 1).astype(F32)).astype(BF)
    arrived, beside = lax.optimization_barrier((swap(far_sum, 2), beside))
    return (own, swap(near, 1), arrived), beside


def share_slabs(own, *beside):
    far, *beside = lax.optimization_barrier((swap(own, 2), *beside))
    return own, far, swap(own, 1), swap(far, 1), *beside


def gather_weights(weight):
    held = [weight]
    for k in range(1, DP):
        held.append(lax.ppermute(weight, "dp", [((a + k) % DP, a) for a in range(DP)]))
    return [part.reshape(KB, CH, PAIR, 2 * HALF) for part in held]


def gather_lines(modes):
    held = [modes, lax.ppermute(modes, "gy", [(g ^ 1, g) for g in range(GY)])]
    for step in range(2, GY, 2):
        pairs = [((g + step) % GY, g) for g in range(GY)]
        held += [lax.ppermute(part, "gy", pairs) for part in held[:2]]
    return held


def exchange_lines(parts):
    return lax.all_to_all(parts, "gy", split_axis=0, concat_axis=0, tiled=True)


def to_owners(chunks):
    moved = []
    for k, chunk in enumerate(chunks):
        pairs = [
            (a * GX + b, b * GX + (a + k) % DP) for a in range(DP) for b in range(GX)
        ]
        moved.append(lax.ppermute(chunk, ("dp", "gx"), pairs))
    return moved


def per_device(field, spectral_weight, bypass_weight, bias, cotangent):
    where = jnp.stack(
        [lax.axis_index("dp"), lax.axis_index("gx"), lax.axis_index("gy")]
    ).astype(jnp.int32)
    turn = [(a * GX + b, (b ^ (2 * (a % 2))) * GX + a) for a in range(DP) for b in range(GX)]
    weight = lax.ppermute(spectral_weight, ("dp", "gx"), turn)
    spread = jnp.asarray(SPREAD)

    def mixer_of(matrix):
        wide = dot(dot(spread, matrix).astype(BF), spread, 1, 1)
        return wide.astype(BF) * jnp.asarray(SAME)

    values = field[0]
    *pieces, weight = lax.optimization_barrier((*start_columns(where, values), weight))
    parts, bypass = start_slabs(pieces, bypass_columns(values, mixer_of(bypass_weight), bias))
    weights = gather_weights(weight)
    lines, weights[1], weights[3] = lax.optimization_barrier(
        (to_lines(where, *parts), weights[1], weights[3])
    )
    arrived = exchange_lines(lines)
    modes, *spectra = mode_call(mix_kernel, "mix_modes", where, arrived, weights)
    coeffs = share_slabs(from_line_set(where, gather_lines(modes[0])))
    activation, grad, *pieces = middle_columns(where, coeffs, bypass, cotangent[0])
    mixer = mixer_of(bypass_weight.T)
    parts, bypass = start_slabs(pieces, bypass_columns(grad, mixer, jnp.zeros_like(bias)))
    arrived = exchange_lines(to_lines(where, *parts))
    modes, *pairs = mode_call(back_kernel, "back_modes", where, arrived, weights, spectra)
    modes, *pairs = lax.optimization_barrier((exchange_lines(modes), *to_owners(pairs)))
    *coeffs, weight_grad = share_slabs(from_lines(where, modes), outer_sum(pairs))
    field_grad = end_columns(where, coeffs, bypass)
    return (
        activation[None],
        field_grad[None],
        weight_grad.reshape(KB, CH, CH, 2, 2 * HALF),
    )


def solution(mesh):
    placed = (
        P("dp", None, "gx", "gy"),
        P("dp", None, None, None, ("gx", "gy")),
        P(),
        P(),
        P("dp", None, "gx", "gy"),
    )
    return jax.shard_map(
        per_device,
        mesh=mesh,
        in_specs=placed,
        out_specs=(
            P("dp", None, "gx", "gy"),
            P("dp", None, "gx", "gy"),
            P("dp", None, None, None, ("gx", "gy")),
        ),
        check_vma=False,
    )
```

```python
import functools
import math

import jax
import jax.numpy as jnp
import ml_dtypes
import numpy as np
from jax import lax
from jax.experimental import pallas as pl
from jax.experimental.pallas import tpu as pltpu
from jax.sharding import PartitionSpec as P

CH = 20
NX = 256
NY = 256
NZ = 64
KX = 64
KY = 64
KZ = 12
GX = 4
GY = 8
DP = 4
XL = NX // GX
YL = NY // GY
YB = 8
STEPS = YL // YB
LANES = YB * NZ
KB = KZ // GX
ROWS = 2 * KB * YB
GROUP = 4
GROUPS = CH // GROUP
GL = GROUP * KX
WIDE = CH * KX
XB = 8
EB = 16
ORDER = (0, 2, 1, 3)

BF = jnp.bfloat16
F32 = jnp.float32


def wave(freqs, points, length):
    offsets = np.mod(freqs[:, None] * points[None, :], length)
    angle = offsets.astype(np.float32) * np.float32(2.0 * math.pi / length)
    return np.cos(angle), np.sin(angle)


def kept(count):
    index = np.arange(count)
    return np.where(index < count // 2, index, index - count)


def depth_tables():
    out = np.zeros((GX, 2, GX, KB, LANES), np.float32)
    for b in range(GX):
        for pos, delta in enumerate(ORDER):
            freqs = (b ^ delta) * KB + np.arange(KB)
            cosine, sine = wave(freqs, np.arange(NZ), NZ)
            out[b, 0, pos] = np.tile(cosine, (1, YB))
            out[b, 1, pos] = np.tile(-sine, (1, YB))
    return out.reshape(GX, 2 * KZ, LANES).astype(ml_dtypes.bfloat16)


def width_tables():
    out = np.zeros((GX, 2, XL, KX), np.float32)
    for b in range(GX):
        cosine, sine = wave(kept(KX), b * XL + np.arange(XL), NX)
        out[b, 0] = cosine.T
        out[b, 1] = sine.T
    return out.astype(ml_dtypes.bfloat16)


def line_tables():
    out = np.zeros((GY, GY, 2, 2, GX, KB, STEPS, 2, KB, YB), np.float32)
    fy = kept(KY)
    for g in range(GY):
        cosine, sine = wave(fy, g * YL + np.arange(YL), NY)
        cosine = cosine.reshape(GX, GY, 2, STEPS, YB)
        sine = sine.reshape(GX, GY, 2, STEPS, YB)
        for i in range(KB):
            for owner in range(GY):
                for q in range(2):
                    c = cosine[:, owner, q]
                    s = sine[:, owner, q]
                    out[g, owner, q, 0, :, i, :, 0, i] = c
                    out[g, owner, q, 0, :, i, :, 1, i] = s
                    out[g, owner, q, 1, :, i, :, 0, i] = -s
                    out[g, owner, q, 1, :, i, :, 1, i] = c
    return out.reshape(GY, GY * 48, STEPS * ROWS).astype(ml_dtypes.bfloat16)


DEPTH = depth_tables()
WIDTH = width_tables()
LINE = line_tables()
SPREAD = np.kron(np.eye(CH), np.ones((XB, 1))).astype(ml_dtypes.bfloat16)
SAME = np.kron(np.ones((CH, CH)), np.eye(XB)).astype(ml_dtypes.bfloat16)


def dot(left, right, left_dim=1, right_dim=0):
    return lax.dot_general(
        left, right, (((left_dim,), (right_dim,)), ((), ())), preferred_element_type=F32
    )


def fill_tables(strip_ref, wide_ref, depth_ref, tall_ref, long_ref):
    strips = jnp.broadcast_to(strip_ref[0].astype(F32)[:, None, :], (2 * KZ, YB, LANES))
    row = lax.broadcasted_iota(jnp.int32, (2 * KZ, YB, LANES), 1)
    column = lax.broadcasted_iota(jnp.int32, (2 * KZ, YB, LANES), 2) // NZ
    blocks = jnp.where(row == column, strips, 0.0)
    depth_ref[...] = blocks.reshape(2 * KZ * YB, LANES).astype(BF)
    rows = lax.broadcasted_iota(jnp.int32, (GL, GL), 0) // XL
    columns = lax.broadcasted_iota(jnp.int32, (GL, GL), 1) // KX
    for part in range(2):
        strip = wide_ref[0, part].astype(F32)
        full = jnp.concatenate([jnp.concatenate([strip] * GROUP, axis=1)] * GROUP, axis=0)
        block = jnp.where(rows == columns, full, 0.0).astype(BF)
        tall_ref[GL * part : GL * (part + 1), :] = block
        long_ref[:, GL * part : GL * (part + 1)] = block


def forward_runs(source_ref, depth_ref, tall_ref, outs, runs):
    half = KZ * YB
    part = KB * YB
    sides = []
    for y in runs:
        planes = dot(depth_ref[...], run_rows(source_ref, y), 1, 1)
        real = planes[:half]
        imag = planes[half:]
        sides.append(jnp.concatenate([real, imag], axis=1).astype(BF))
        sides.append(jnp.concatenate([imag, -real], axis=1).astype(BF))
    lines = dot(jnp.concatenate(sides, axis=0), tall_ref[...])
    for n, y in enumerate(runs):
        for pos in range(GX):
            lo = 2 * half * n + pos * part
            piece = jnp.concatenate(
                [lines[lo : lo + part], lines[half + lo : half + lo + part]], axis=0
            )
            outs[pos][y] = piece.astype(BF)


def inverse_runs(ins, depth_ref, long_ref, runs):
    part = KB * YB
    planes = []
    for y in runs:
        pieces = [ref[y].astype(F32) for ref in ins]
        real = jnp.concatenate([piece[:part] for piece in pieces], axis=0)
        imag = jnp.concatenate([piece[part:] for piece in pieces], axis=0)
        sides = jnp.concatenate(
            [jnp.concatenate([real, -imag], axis=1), jnp.concatenate([imag, real], axis=1)],
            axis=0,
        ).astype(BF)
        planes.append(dot(long_ref[...], sides, 1, 1).astype(BF))
    return dot(jnp.concatenate(planes, axis=0), depth_ref[...])


def run_rows(ref, y):
    return ref[:, :, LANES * y : LANES * (y + 1)].reshape(GROUP * XL, LANES)


def bypass_kernel(shift_ref, source_ref, mixer_ref, out_ref):
    for i in range(XL // XB):
        span = slice(i * XB, (i + 1) * XB)
        rows = source_ref[:, span, :].reshape(CH * XB, LANES)
        mixed = dot(mixer_ref[...], rows).reshape(CH, XB, LANES)
        for channel in range(CH):
            out_ref[channel, span, :] = (mixed[channel] + shift_ref[channel]).astype(BF)


def start_kernel(
    where_ref, field_ref, strip_ref, wide_ref, o0, o1, o2, o3, depth_ref, tall_ref, long_ref
):
    @pl.when(pl.program_id(0) == 0)
    def _():
        fill_tables(strip_ref, wide_ref, depth_ref, tall_ref, long_ref)

    forward_runs(field_ref, depth_ref, tall_ref, (o0, o1, o2, o3), range(STEPS))


ROOT = math.sqrt(2.0 / math.pi)
CUBE = 0.044715


def activate(upstream_ref, total_ref, act_ref, grad_ref, y):
    lanes = slice(LANES * y, LANES * (y + 1))
    for channel in range(GROUP):
        for i in range(XL // EB):
            span = slice(i * EB, (i + 1) * EB)
            x = total_ref[y, channel, span, :]
            square = x * x
            t = jnp.tanh(x * (ROOT + (ROOT * CUBE) * square))
            h = 0.5 * t + 0.5
            act = x * h
            slope = h + act * (1.0 - h) * (2.0 * ROOT + (6.0 * ROOT * CUBE) * square)
            act_ref[channel, span, lanes] = act.astype(BF)
            grad_ref[channel, span, lanes] = upstream_ref[channel, span, lanes] * slope.astype(BF)


def middle_kernel(
    where_ref, i0, i1, i2, i3, bypass_ref, upstream_ref, strip_ref, wide_ref,
    act_ref, grad_ref, o0, o1, o2, o3, depth_ref, tall_ref, long_ref, total_ref,
):
    @pl.when(pl.program_id(0) == 0)
    def _():
        fill_tables(strip_ref, wide_ref, depth_ref, tall_ref, long_ref)

    def inverse(*runs):
        values = inverse_runs((i0, i1, i2, i3), depth_ref, long_ref, runs)
        for n, y in enumerate(runs):
            lanes = slice(LANES * y, LANES * (y + 1))
            own = values[GL * n : GL * (n + 1)].reshape(GROUP, XL, LANES)
            total_ref[y] = bypass_ref[:, :, lanes].astype(F32) + own

    def forward(*runs):
        forward_runs(grad_ref, depth_ref, tall_ref, (o0, o1, o2, o3), runs)

    def activation(y):
        activate(upstream_ref, total_ref, act_ref, grad_ref, y)

    inverse(0, 1)
    activation(0)
    inverse(2, 3)
    activation(1)
    activation(2)
    forward(0, 1)
    activation(3)
    forward(2, 3)


def end_kernel(
    where_ref, i0, i1, i2, i3, bypass_ref, strip_ref, wide_ref, out_ref,
    depth_ref, tall_ref, long_ref,
):
    @pl.when(pl.program_id(0) == 0)
    def _():
        fill_tables(strip_ref, wide_ref, depth_ref, tall_ref, long_ref)

    for first in range(0, STEPS, 2):
        runs = (first, first + 1)
        values = inverse_runs((i0, i1, i2, i3), depth_ref, long_ref, runs)
        for n, y in enumerate(runs):
            lanes = slice(LANES * y, LANES * (y + 1))
            own = values[GL * n : GL * (n + 1)].reshape(GROUP, XL, LANES)
            out_ref[:, :, lanes] = (bypass_ref[:, :, lanes].astype(F32) + own).astype(BF)


def cost(micros):
    return pl.CostEstimate(flops=0, bytes_accessed=micros * 3_000_000, transcendentals=0)


def column_specs():
    columns = pl.BlockSpec((GROUP, XL, YL * NZ), lambda j, w: (j, 0, 0))
    coeffs = pl.BlockSpec((STEPS, ROWS, GL), lambda j, w: (0, 0, j))
    depth = pl.BlockSpec((1, 2 * KZ, LANES), lambda j, w: (w[1], 0, 0))
    wide = pl.BlockSpec((1, 2, XL, KX), lambda j, w: (w[1], 0, 0, 0))
    return columns, coeffs, depth, wide


COEFFS = jax.ShapeDtypeStruct((STEPS, ROWS, WIDE), BF)
COLUMNS = jax.ShapeDtypeStruct((CH, XL, YL * NZ), BF)
BLOCKS = [
    pltpu.VMEM((2 * KZ * YB, LANES), BF),
    pltpu.VMEM((2 * GL, GL), BF),
    pltpu.VMEM((GL, 2 * GL), BF),
]
TOTAL = pltpu.VMEM((STEPS, GROUP, XL, LANES), F32)
PARAMS = pltpu.CompilerParams(vmem_limit_bytes=56 * 1024 * 1024)
ALONE = pltpu.CompilerParams(vmem_limit_bytes=67_043_328)


def bypass_columns(source, mixer, shift):
    columns = pl.BlockSpec((CH, XL, LANES), lambda i: (0, 0, i))
    return pl.pallas_call(
        bypass_kernel,
        grid=(STEPS,),
        in_specs=[
            pl.BlockSpec(memory_space=pltpu.SMEM),
            columns,
            pl.BlockSpec((CH * XB, CH * XB), lambda i: (0, 0)),
        ],
        out_specs=columns,
        out_shape=COLUMNS,
        compiler_params=PARAMS,
        cost_estimate=cost(6),
        name="bypass_columns",
    )(shift, source, mixer)


def start_columns(where, field):
    columns, coeffs, depth, wide = column_specs()
    return pl.pallas_call(
        start_kernel,
        grid_spec=pltpu.PrefetchScalarGridSpec(
            num_scalar_prefetch=1,
            grid=(GROUPS,),
            in_specs=[columns, depth, wide],
            out_specs=[coeffs] * 4,
            scratch_shapes=BLOCKS,
        ),
        out_shape=[COEFFS] * 4,
        compiler_params=PARAMS,
        cost_estimate=cost(8),
        name="start_columns",
    )(where, field, jnp.asarray(DEPTH), jnp.asarray(WIDTH))


def middle_columns(where, coeffs_in, bypass, upstream):
    columns, coeffs, depth, wide = column_specs()
    return pl.pallas_call(
        middle_kernel,
        grid_spec=pltpu.PrefetchScalarGridSpec(
            num_scalar_prefetch=1,
            grid=(GROUPS,),
            in_specs=[coeffs] * 4 + [columns, columns, depth, wide],
            out_specs=[columns, columns] + [coeffs] * 4,
            scratch_shapes=BLOCKS + [TOTAL],
        ),
        out_shape=[COLUMNS, COLUMNS] + [COEFFS] * 4,
        compiler_params=PARAMS,
        cost_estimate=cost(19),
        name="middle_columns",
    )(where, *coeffs_in, bypass, upstream, jnp.asarray(DEPTH), jnp.asarray(WIDTH))


def end_columns(where, coeffs_in, bypass):
    columns, coeffs, depth, wide = column_specs()
    return pl.pallas_call(
        end_kernel,
        grid_spec=pltpu.PrefetchScalarGridSpec(
            num_scalar_prefetch=1,
            grid=(GROUPS,),
            in_specs=[coeffs] * 4 + [columns, depth, wide],
            out_specs=columns,
            scratch_shapes=BLOCKS,
        ),
        out_shape=COLUMNS,
        compiler_params=ALONE,
        cost_estimate=cost(10),
        name="end_columns",
    )(where, *coeffs_in, bypass, jnp.asarray(DEPTH), jnp.asarray(WIDTH))


def order_table(where_ref, table_ref, order_ref):
    for k in range(GY):
        owner = ((where_ref[2] + (k & 6)) & 7) ^ (k & 1)
        start = pl.multiple_of(owner * 48, 16)
        order_ref[48 * k : 48 * (k + 1)] = table_ref[0, pl.ds(start, 48), :]


def line_kernel(where_ref, a_ref, b_ref, c_ref, table_ref, out_ref):
    for j in range(GROUPS):
        lanes = slice(GL * j, GL * (j + 1))
        parts = [ref[:, :, lanes].astype(F32) for ref in (a_ref, b_ref, c_ref)]
        rows = (parts[0] + parts[1] + parts[2]).astype(BF).reshape(STEPS * ROWS, GL)
        out_ref[:, :, lanes] = dot(table_ref[0], rows).astype(BF).reshape(GY, 48, GL)


def unline_kernel(where_ref, modes_ref, table_ref, out_ref):
    for j in range(GROUPS):
        lanes = slice(GL * j, GL * (j + 1))
        rows = modes_ref[:, :, lanes].reshape(GY * 48, GL)
        out_ref[:, :, lanes] = dot(table_ref[0], rows, 0, 0).astype(BF).reshape(STEPS, ROWS, GL)


def unline_set_kernel(where_ref, *refs):
    *modes_refs, table_ref, out_ref, order_ref = refs
    for k in range(GY):
        owner = ((where_ref[2] + (k & 6)) & 7) ^ (k & 1)
        start = pl.multiple_of(owner * 48, 16)
        order_ref[48 * k : 48 * (k + 1)] = table_ref[0, pl.ds(start, 48), :]
    for j in range(GROUPS):
        lanes = slice(GL * j, GL * (j + 1))
        rows = jnp.concatenate([ref[:, lanes] for ref in modes_refs], axis=0)
        out_ref[:, :, lanes] = dot(order_ref[...], rows, 0, 0).astype(BF).reshape(STEPS, ROWS, GL)


def line_call(kernel, name, where, ins, out, scratch=()):
    whole = pl.BlockSpec(ins[0].shape, lambda i, w: (0,) * ins[0].ndim)
    table = pl.BlockSpec((1, GY * 48, STEPS * ROWS), lambda i, w: (w[2], 0, 0))
    return pl.pallas_call(
        kernel,
        grid_spec=pltpu.PrefetchScalarGridSpec(
            num_scalar_prefetch=1,
            grid=(1,),
            in_specs=[whole] * len(ins) + [table],
            out_specs=pl.BlockSpec(out.shape, lambda i, w: (0, 0, 0)),
            scratch_shapes=list(scratch),
        ),
        out_shape=out,
        compiler_params=ALONE,
        cost_estimate=cost(3),
        name=name,
    )(where, *ins, jnp.asarray(LINE))


def to_lines(where, *parts):
    out = jax.ShapeDtypeStruct((GY, 48, WIDE), BF)
    return line_call(line_kernel, "to_lines", where, parts, out)


def from_lines(where, modes):
    return line_call(unline_kernel, "from_lines", where, (modes,), COEFFS)


def from_line_set(where, modes):
    order = pltpu.VMEM((GY * 48, STEPS * ROWS), BF)
    return line_call(unline_set_kernel, "from_line_set", where, modes, COEFFS, [order])


UNROLL = 10
SETS = GX * KB
PAIR = 2 * CH
HALF = KX


def low_lanes():
    return lax.broadcasted_iota(jnp.int32, (SETS, 2 * HALF), 1) < HALF


def gather_modes(arrived, sum_ref, modes_ref, scale=None):
    total = arrived[0].astype(F32)
    for i in range(1, GY):
        total = total + arrived[i].astype(F32)
    sum_ref[...] = total.astype(BF).astype(F32)
    low = low_lanes()
    for j in range(CH // 2):
        lanes = slice(2 * HALF * j, 2 * HALF * (j + 1))
        for part in range(2):
            first = sum_ref[part * SETS : (part + 1) * SETS, lanes]
            second = sum_ref[(2 + part) * SETS : (3 + part) * SETS, lanes]
            if scale is not None:
                first = first * scale
                second = second * scale
            even = jnp.where(low, first, pltpu.roll(second, HALF, 1))
            odd = jnp.where(low, pltpu.roll(first, HALF, 1), second)
            modes_ref[pl.ds(4 * j + part, SETS, stride=PAIR), :] = even
            modes_ref[pl.ds(4 * j + 2 + part, SETS, stride=PAIR), :] = odd


def spread_modes(modes_ref, sum_ref, out_ref, scale=None):
    low = low_lanes()
    for j in range(CH // 2):
        lanes = slice(2 * HALF * j, 2 * HALF * (j + 1))
        for part in range(2):
            even = modes_ref[pl.ds(4 * j + part, SETS, stride=PAIR), :]
            odd = modes_ref[pl.ds(4 * j + 2 + part, SETS, stride=PAIR), :]
            if scale is not None:
                even = even * scale
                odd = odd * scale
            sum_ref[part * SETS : (part + 1) * SETS, lanes] = jnp.where(
                low, even, pltpu.roll(odd, HALF, 1)
            )
            sum_ref[(2 + part) * SETS : (3 + part) * SETS, lanes] = jnp.where(
                low, pltpu.roll(even, HALF, 1), odd
            )
    modes = sum_ref[...].astype(BF)
    for copy in range(out_ref.shape[0]):
        out_ref[copy] = modes


def fold_scale(where_ref):
    kz = where_ref[1] * KB + lax.broadcasted_iota(jnp.int32, (SETS, 2 * HALF), 0) % KB
    return jnp.where(kz == 0, 1.0, 2.0).astype(F32) / float(NX * NY * NZ)


def turned(rows):
    even = lax.broadcasted_iota(jnp.int32, rows.shape, 0) % 2 == 0
    up = pltpu.roll(rows, PAIR - 1, 0)
    down = pltpu.roll(rows, 1, 0)
    return jnp.where(even, -up, down)


def hand_out(where_ref, modes_ref, outs):
    for k in range(DP):
        chunk = lax.rem(where_ref[0] + k, DP)
        start = pl.multiple_of(chunk * KB * PAIR, 8)
        outs[k][...] = modes_ref[pl.ds(start, KB * PAIR), :].astype(BF)


def set_row(where_ref, k):
    block = (lax.rem(where_ref[0] + k, DP) ^ (2 * (where_ref[1] & 1))) * KB + pl.program_id(0)
    return pl.multiple_of(block * PAIR, 8)


def mix_kernel(
    where_ref, arrived_ref, w0, w1, w2, w3, out_ref, u0, u1, u2, u3,
    sum_ref, in_ref, mix_ref,
):
    step = pl.program_id(0)

    @pl.when(step == 0)
    def _():
        gather_modes(arrived_ref, sum_ref, in_ref)
        hand_out(where_ref, in_ref, [ref.at[0] for ref in (u0, u1, u2, u3)])

    for k, weight_ref in enumerate((w0, w1, w2, w3)):
        base = set_row(where_ref, k)

        def add(i, totals, weight_ref=weight_ref, base=base):
            by_real, by_imag = totals
            for r in range(UNROLL):
                c = i * UNROLL + r
                weight = weight_ref[0, c].astype(F32)
                by_real = by_real + weight * in_ref[pl.ds(base + 2 * c, 1), :]
                by_imag = by_imag + weight * in_ref[pl.ds(base + 2 * c + 1, 1), :]
            return by_real, by_imag

        zero = jnp.zeros((PAIR, 2 * HALF), F32)
        by_real, by_imag = lax.fori_loop(0, CH // UNROLL, add, (zero, zero))
        mix_ref[pl.ds(base, PAIR), :] = (by_real + turned(by_imag)).astype(BF).astype(F32)

    @pl.when(step == KB - 1)
    def _():
        spread_modes(mix_ref, sum_ref, out_ref, fold_scale(where_ref))


def back_kernel(
    where_ref, arrived_ref, w0, w1, w2, w3, s0, s1, s2, s3, out_ref, u0, u1, u2, u3,
    sum_ref, in_ref, mix_ref,
):
    step = pl.program_id(0)

    @pl.when(step == 0)
    def _():
        gather_modes(arrived_ref, sum_ref, in_ref, fold_scale(where_ref))
        hand_out(where_ref, in_ref, [ref.at[1] for ref in (u0, u1, u2, u3)])
        for spec_ref, ref in zip((s0, s1, s2, s3), (u0, u1, u2, u3)):
            ref[0] = spec_ref[0]

    for k, weight_ref in enumerate((w0, w1, w2, w3)):
        base = set_row(where_ref, k)
        grad = in_ref[pl.ds(base, PAIR), :]
        other = -turned(grad)

        @pl.loop(0, CH // UNROLL)
        def _(i, weight_ref=weight_ref, base=base, grad=grad, other=other):
            for r in range(UNROLL):
                c = i * UNROLL + r
                weight = weight_ref[0, c].astype(F32)
                mix_ref[pl.ds(base + 2 * c, 1), :] = jnp.sum(weight * grad, axis=0, keepdims=True)
                mix_ref[pl.ds(base + 2 * c + 1, 1), :] = jnp.sum(
                    weight * other, axis=0, keepdims=True
                )

    @pl.when(step == KB - 1)
    def _():
        spread_modes(mix_ref, sum_ref, out_ref)


def mode_call(kernel, name, where, arrived, weights, spectra=()):
    sets, copies = (2, GY) if spectra else (1, 1)

    def chunk(n):
        return pl.BlockSpec((n, KB * PAIR, 2 * HALF), lambda i, w: (0, 0, 0))

    return pl.pallas_call(
        kernel,
        grid_spec=pltpu.PrefetchScalarGridSpec(
            num_scalar_prefetch=1,
            grid=(KB,),
            in_specs=[pl.BlockSpec((GY, 48, WIDE), lambda i, w: (0, 0, 0))]
            + [pl.BlockSpec((1, CH, PAIR, 2 * HALF), lambda i, w: (i, 0, 0, 0))] * 4
            + [chunk(1)] * len(spectra),
            out_specs=[pl.BlockSpec((copies, 48, WIDE), lambda i, w: (0, 0, 0))]
            + [chunk(sets)] * 4,
            scratch_shapes=[
                pltpu.VMEM((48, WIDE), F32),
                pltpu.VMEM((SETS * PAIR, 2 * HALF), F32),
                pltpu.VMEM((SETS * PAIR, 2 * HALF), F32),
            ],
        ),
        out_shape=[jax.ShapeDtypeStruct((copies, 48, WIDE), BF)]
        + [jax.ShapeDtypeStruct((sets, KB * PAIR, 2 * HALF), BF)] * 4,
        compiler_params=ALONE,
        cost_estimate=cost(5),
        name=name,
    )(where, arrived, *weights, *spectra)


def outer_kernel(p0, p1, p2, p3, out_ref, spec_ref):
    pairs = (p0, p1, p2, p3)
    for k, ref in enumerate(pairs):
        spec_ref[k] = ref[0].astype(F32)
    for i in range(KB):
        grads = []
        others = []
        for ref in pairs:
            grad = ref[1].astype(F32)[i * PAIR : (i + 1) * PAIR]
            grads.append(grad)
            others.append(-turned(grad))

        @pl.loop(0, CH)
        def _(c):
            row = i * PAIR + 2 * c
            total = jnp.zeros((PAIR, 2 * HALF), F32)
            for k in range(DP):
                total = total + spec_ref[k, pl.ds(row, 1), :] * grads[k]
                total = total + spec_ref[k, pl.ds(row + 1, 1), :] * others[k]
            out_ref[i, c] = total


def outer_sum(pairs):
    return pl.pallas_call(
        outer_kernel,
        out_shape=jax.ShapeDtypeStruct((KB, CH, PAIR, 2 * HALF), F32),
        scratch_shapes=[pltpu.VMEM((DP, KB * PAIR, 2 * HALF), F32)],
        cost_estimate=cost(3),
        name="outer_sum",
    )(*pairs)


def swap(values, bit):
    return lax.ppermute(values, "gx", [(i, i ^ bit) for i in range(GX)])


def start_slabs(pieces, beside):
    own, far, near, across = pieces
    far_sum = (far.astype(F32) + swap(across, 1).astype(F32)).astype(BF)
    arrived, beside = lax.optimization_barrier((swap(far_sum, 2), beside))
    return (own, swap(near, 1), arrived), beside


def share_slabs(own, *beside):
    far, *beside = lax.optimization_barrier((swap(own, 2), *beside))
    return own, far, swap(own, 1), swap(far, 1), *beside


def gather_weights(weight):
    held = [weight]
    for k in range(1, DP):
        held.append(lax.ppermute(weight, "dp", [((a + k) % DP, a) for a in range(DP)]))
    return [part.reshape(KB, CH, PAIR, 2 * HALF) for part in held]


def gather_lines(modes):
    held = [modes, lax.ppermute(modes, "gy", [(g ^ 1, g) for g in range(GY)])]
    for step in range(2, GY, 2):
        pairs = [((g + step) % GY, g) for g in range(GY)]
        held += [lax.ppermute(part, "gy", pairs) for part in held[:2]]
    return held


def exchange_lines(parts):
    return lax.all_to_all(parts, "gy", split_axis=0, concat_axis=0, tiled=True)


def to_owners(chunks):
    moved = []
    for k, chunk in enumerate(chunks):
        pairs = [
            (a * GX + b, b * GX + (a + k) % DP) for a in range(DP) for b in range(GX)
        ]
        moved.append(lax.ppermute(chunk, ("dp", "gx"), pairs))
    return moved


def per_device(field, spectral_weight, bypass_weight, bias, cotangent):
    where = jnp.stack(
        [lax.axis_index("dp"), lax.axis_index("gx"), lax.axis_index("gy")]
    ).astype(jnp.int32)
    turn = [(a * GX + b, (b ^ (2 * (a % 2))) * GX + a) for a in range(DP) for b in range(GX)]
    weight = lax.ppermute(spectral_weight, ("dp", "gx"), turn)
    spread = jnp.asarray(SPREAD)

    def mixer_of(matrix):
        wide = dot(dot(spread, matrix).astype(BF), spread, 1, 1)
        return wide.astype(BF) * jnp.asarray(SAME)

    values = field[0]
    *pieces, weight = lax.optimization_barrier((*start_columns(where, values), weight))
    parts, bypass = start_slabs(pieces, bypass_columns(values, mixer_of(bypass_weight), bias))
    weights = gather_weights(weight)
    lines, weights[1], weights[3] = lax.optimization_barrier(
        (to_lines(where, *parts), weights[1], weights[3])
    )
    arrived = exchange_lines(lines)
    modes, *spectra = mode_call(mix_kernel, "mix_modes", where, arrived, weights)
    coeffs = share_slabs(from_line_set(where, gather_lines(modes[0])))
    activation, grad, *pieces = middle_columns(where, coeffs, bypass, cotangent[0])
    mixer = mixer_of(bypass_weight.T)
    parts, bypass = start_slabs(pieces, bypass_columns(grad, mixer, jnp.zeros_like(bias)))
    arrived = exchange_lines(to_lines(where, *parts))
    modes, *pairs = mode_call(back_kernel, "back_modes", where, arrived, weights, spectra)
    pairs = to_owners(pairs)
    modes, *pairs[:2] = lax.optimization_barrier((exchange_lines(modes), *pairs[:2]))
    *coeffs, weight_grad = share_slabs(from_lines(where, modes), outer_sum(pairs))
    field_grad = end_columns(where, coeffs, bypass)
    return (
        activation[None],
        field_grad[None],
        weight_grad.reshape(KB, CH, CH, 2, 2 * HALF),
    )


def solution(mesh):
    placed = (
        P("dp", None, "gx", "gy"),
        P("dp", None, None, None, ("gx", "gy")),
        P(),
        P(),
        P("dp", None, "gx", "gy"),
    )
    return jax.shard_map(
        per_device,
        mesh=mesh,
        in_specs=placed,
        out_specs=(
            P("dp", None, "gx", "gy"),
            P("dp", None, "gx", "gy"),
            P("dp", None, None, None, ("gx", "gy")),
        ),
        check_vma=False,
    )
```

```python
import functools
import math

import jax
import jax.numpy as jnp
import ml_dtypes
import numpy as np
from jax import lax
from jax.experimental import pallas as pl
from jax.experimental.pallas import tpu as pltpu
from jax.sharding import PartitionSpec as P

CH = 20
NX = 256
NY = 256
NZ = 64
KX = 64
KY = 64
KZ = 12
GX = 4
GY = 8
DP = 4
XL = NX // GX
YL = NY // GY
YB = 8
STEPS = YL // YB
LANES = YB * NZ
KB = KZ // GX
ROWS = 2 * KB * YB
GROUP = 4
GROUPS = CH // GROUP
GL = GROUP * KX
WIDE = CH * KX
XB = 8
EB = 16
ORDER = (0, 2, 1, 3)

BF = jnp.bfloat16
F32 = jnp.float32


def wave(freqs, points, length):
    offsets = np.mod(freqs[:, None] * points[None, :], length)
    angle = offsets.astype(np.float32) * np.float32(2.0 * math.pi / length)
    return np.cos(angle), np.sin(angle)


def kept(count):
    index = np.arange(count)
    return np.where(index < count // 2, index, index - count)


def depth_tables():
    out = np.zeros((GX, 2, GX, KB, LANES), np.float32)
    for b in range(GX):
        for pos, delta in enumerate(ORDER):
            freqs = (b ^ delta) * KB + np.arange(KB)
            cosine, sine = wave(freqs, np.arange(NZ), NZ)
            out[b, 0, pos] = np.tile(cosine, (1, YB))
            out[b, 1, pos] = np.tile(-sine, (1, YB))
    return out.reshape(GX, 2 * KZ, LANES).astype(ml_dtypes.bfloat16)


def width_tables():
    out = np.zeros((GX, 2, XL, KX), np.float32)
    for b in range(GX):
        cosine, sine = wave(kept(KX), b * XL + np.arange(XL), NX)
        out[b, 0] = cosine.T
        out[b, 1] = sine.T
    return out.astype(ml_dtypes.bfloat16)


def line_tables():
    out = np.zeros((GY, GY, 2, 2, GX, KB, STEPS, 2, KB, YB), np.float32)
    fy = kept(KY)
    for g in range(GY):
        cosine, sine = wave(fy, g * YL + np.arange(YL), NY)
        cosine = cosine.reshape(GX, GY, 2, STEPS, YB)
        sine = sine.reshape(GX, GY, 2, STEPS, YB)
        for i in range(KB):
            for owner in range(GY):
                for q in range(2):
                    c = cosine[:, owner, q]
                    s = sine[:, owner, q]
                    out[g, owner, q, 0, :, i, :, 0, i] = c
                    out[g, owner, q, 0, :, i, :, 1, i] = s
                    out[g, owner, q, 1, :, i, :, 0, i] = -s
                    out[g, owner, q, 1, :, i, :, 1, i] = c
    return out.reshape(GY, GY * 48, STEPS * ROWS).astype(ml_dtypes.bfloat16)


DEPTH = depth_tables()
WIDTH = width_tables()
LINE = line_tables()
SPREAD = np.kron(np.eye(CH), np.ones((XB, 1))).astype(ml_dtypes.bfloat16)
SAME = np.kron(np.ones((CH, CH)), np.eye(XB)).astype(ml_dtypes.bfloat16)


def dot(left, right, left_dim=1, right_dim=0):
    return lax.dot_general(
        left, right, (((left_dim,), (right_dim,)), ((), ())), preferred_element_type=F32
    )


def fill_tables(strip_ref, wide_ref, depth_ref, tall_ref, long_ref):
    strips = jnp.broadcast_to(strip_ref[0].astype(F32)[:, None, :], (2 * KZ, YB, LANES))
    row = lax.broadcasted_iota(jnp.int32, (2 * KZ, YB, LANES), 1)
    column = lax.broadcasted_iota(jnp.int32, (2 * KZ, YB, LANES), 2) // NZ
    blocks = jnp.where(row == column, strips, 0.0)
    depth_ref[...] = blocks.reshape(2 * KZ * YB, LANES).astype(BF)
    rows = lax.broadcasted_iota(jnp.int32, (GL, GL), 0) // XL
    columns = lax.broadcasted_iota(jnp.int32, (GL, GL), 1) // KX
    for part in range(2):
        strip = wide_ref[0, part].astype(F32)
        full = jnp.concatenate([jnp.concatenate([strip] * GROUP, axis=1)] * GROUP, axis=0)
        block = jnp.where(rows == columns, full, 0.0).astype(BF)
        tall_ref[GL * part : GL * (part + 1), :] = block
        long_ref[:, GL * part : GL * (part + 1)] = block


def forward_runs(source_ref, depth_ref, tall_ref, outs, runs):
    half = KZ * YB
    part = KB * YB
    sides = []
    for y in runs:
        planes = dot(depth_ref[...], run_rows(source_ref, y), 1, 1)
        real = planes[:half]
        imag = planes[half:]
        sides.append(jnp.concatenate([real, imag], axis=1).astype(BF))
        sides.append(jnp.concatenate([imag, -real], axis=1).astype(BF))
    lines = dot(jnp.concatenate(sides, axis=0), tall_ref[...])
    for n, y in enumerate(runs):
        for pos in range(GX):
            lo = 2 * half * n + pos * part
            piece = jnp.concatenate(
                [lines[lo : lo + part], lines[half + lo : half + lo + part]], axis=0
            )
            outs[pos][y] = piece.astype(BF)


def inverse_runs(ins, depth_ref, long_ref, runs):
    part = KB * YB
    planes = []
    for y in runs:
        pieces = [ref[y].astype(F32) for ref in ins]
        real = jnp.concatenate([piece[:part] for piece in pieces], axis=0)
        imag = jnp.concatenate([piece[part:] for piece in pieces], axis=0)
        sides = jnp.concatenate(
            [jnp.concatenate([real, -imag], axis=1), jnp.concatenate([imag, real], axis=1)],
            axis=0,
        ).astype(BF)
        planes.append(dot(long_ref[...], sides, 1, 1).astype(BF))
    return dot(jnp.concatenate(planes, axis=0), depth_ref[...])


def run_rows(ref, y):
    return ref[:, :, LANES * y : LANES * (y + 1)].reshape(GROUP * XL, LANES)


def bypass_kernel(shift_ref, source_ref, mixer_ref, out_ref):
    for i in range(XL // XB):
        span = slice(i * XB, (i + 1) * XB)
        rows = source_ref[:, span, :].reshape(CH * XB, LANES)
        mixed = dot(mixer_ref[...], rows).reshape(CH, XB, LANES)
        for channel in range(CH):
            out_ref[channel, span, :] = (mixed[channel] + shift_ref[channel]).astype(BF)


def start_kernel(
    where_ref, field_ref, strip_ref, wide_ref, o0, o1, o2, o3, depth_ref, tall_ref, long_ref
):
    @pl.when(pl.program_id(0) == 0)
    def _():
        fill_tables(strip_ref, wide_ref, depth_ref, tall_ref, long_ref)

    forward_runs(field_ref, depth_ref, tall_ref, (o0, o1, o2, o3), range(STEPS))


ROOT = math.sqrt(2.0 / math.pi)
CUBE = 0.044715


def activate(upstream_ref, total_ref, act_ref, grad_ref, y):
    lanes = slice(LANES * y, LANES * (y + 1))
    for channel in range(GROUP):
        for i in range(XL // EB):
            span = slice(i * EB, (i + 1) * EB)
            x = total_ref[y, channel, span, :]
            square = x * x
            t = jnp.tanh(x * (ROOT + (ROOT * CUBE) * square))
            h = 0.5 * t + 0.5
            act = x * h
            slope = h + act * (1.0 - h) * (2.0 * ROOT + (6.0 * ROOT * CUBE) * square)
            act_ref[channel, span, lanes] = act.astype(BF)
            grad_ref[channel, span, lanes] = upstream_ref[channel, span, lanes] * slope.astype(BF)


def middle_kernel(
    where_ref, i0, i1, i2, i3, bypass_ref, upstream_ref, strip_ref, wide_ref,
    act_ref, grad_ref, o0, o1, o2, o3, depth_ref, tall_ref, long_ref, total_ref,
):
    @pl.when(pl.program_id(0) == 0)
    def _():
        fill_tables(strip_ref, wide_ref, depth_ref, tall_ref, long_ref)

    def inverse(*runs):
        values = inverse_runs((i0, i1, i2, i3), depth_ref, long_ref, runs)
        for n, y in enumerate(runs):
            lanes = slice(LANES * y, LANES * (y + 1))
            own = values[GL * n : GL * (n + 1)].reshape(GROUP, XL, LANES)
            total_ref[y] = bypass_ref[:, :, lanes].astype(F32) + own

    def forward(*runs):
        forward_runs(grad_ref, depth_ref, tall_ref, (o0, o1, o2, o3), runs)

    def activation(y):
        activate(upstream_ref, total_ref, act_ref, grad_ref, y)

    inverse(0, 1)
    activation(0)
    inverse(2, 3)
    activation(1)
    activation(2)
    forward(0, 1)
    activation(3)
    forward(2, 3)


def end_kernel(
    where_ref, i0, i1, i2, i3, bypass_ref, strip_ref, wide_ref, out_ref,
    depth_ref, tall_ref, long_ref,
):
    @pl.when(pl.program_id(0) == 0)
    def _():
        fill_tables(strip_ref, wide_ref, depth_ref, tall_ref, long_ref)

    for first in range(0, STEPS, 2):
        runs = (first, first + 1)
        values = inverse_runs((i0, i1, i2, i3), depth_ref, long_ref, runs)
        for n, y in enumerate(runs):
            lanes = slice(LANES * y, LANES * (y + 1))
            own = values[GL * n : GL * (n + 1)].reshape(GROUP, XL, LANES)
            out_ref[:, :, lanes] = (bypass_ref[:, :, lanes].astype(F32) + own).astype(BF)


def cost(micros):
    return pl.CostEstimate(flops=0, bytes_accessed=micros * 3_000_000, transcendentals=0)


def column_specs():
    columns = pl.BlockSpec((GROUP, XL, YL * NZ), lambda j, w: (j, 0, 0))
    coeffs = pl.BlockSpec((STEPS, ROWS, GL), lambda j, w: (0, 0, j))
    depth = pl.BlockSpec((1, 2 * KZ, LANES), lambda j, w: (w[1], 0, 0))
    wide = pl.BlockSpec((1, 2, XL, KX), lambda j, w: (w[1], 0, 0, 0))
    return columns, coeffs, depth, wide


COEFFS = jax.ShapeDtypeStruct((STEPS, ROWS, WIDE), BF)
COLUMNS = jax.ShapeDtypeStruct((CH, XL, YL * NZ), BF)
BLOCKS = [
    pltpu.VMEM((2 * KZ * YB, LANES), BF),
    pltpu.VMEM((2 * GL, GL), BF),
    pltpu.VMEM((GL, 2 * GL), BF),
]
TOTAL = pltpu.VMEM((STEPS, GROUP, XL, LANES), F32)
PARAMS = pltpu.CompilerParams(vmem_limit_bytes=56 * 1024 * 1024)
ALONE = pltpu.CompilerParams(vmem_limit_bytes=67_043_328)


def bypass_columns(source, mixer, shift):
    columns = pl.BlockSpec((CH, XL, LANES), lambda i: (0, 0, i))
    return pl.pallas_call(
        bypass_kernel,
        grid=(STEPS,),
        in_specs=[
            pl.BlockSpec(memory_space=pltpu.SMEM),
            columns,
            pl.BlockSpec((CH * XB, CH * XB), lambda i: (0, 0)),
        ],
        out_specs=columns,
        out_shape=COLUMNS,
        compiler_params=PARAMS,
        cost_estimate=cost(6),
        name="bypass_columns",
    )(shift, source, mixer)


def start_columns(where, field):
    columns, coeffs, depth, wide = column_specs()
    return pl.pallas_call(
        start_kernel,
        grid_spec=pltpu.PrefetchScalarGridSpec(
            num_scalar_prefetch=1,
            grid=(GROUPS,),
            in_specs=[columns, depth, wide],
            out_specs=[coeffs] * 4,
            scratch_shapes=BLOCKS,
        ),
        out_shape=[COEFFS] * 4,
        compiler_params=PARAMS,
        cost_estimate=cost(8),
        name="start_columns",
    )(where, field, jnp.asarray(DEPTH), jnp.asarray(WIDTH))


def middle_columns(where, coeffs_in, bypass, upstream):
    columns, coeffs, depth, wide = column_specs()
    return pl.pallas_call(
        middle_kernel,
        grid_spec=pltpu.PrefetchScalarGridSpec(
            num_scalar_prefetch=1,
            grid=(GROUPS,),
            in_specs=[coeffs] * 4 + [columns, columns, depth, wide],
            out_specs=[columns, columns] + [coeffs] * 4,
            scratch_shapes=BLOCKS + [TOTAL],
        ),
        out_shape=[COLUMNS, COLUMNS] + [COEFFS] * 4,
        compiler_params=ALONE,
        cost_estimate=cost(19),
        name="middle_columns",
    )(where, *coeffs_in, bypass, upstream, jnp.asarray(DEPTH), jnp.asarray(WIDTH))


def end_columns(where, coeffs_in, bypass):
    columns, coeffs, depth, wide = column_specs()
    return pl.pallas_call(
        end_kernel,
        grid_spec=pltpu.PrefetchScalarGridSpec(
            num_scalar_prefetch=1,
            grid=(GROUPS,),
            in_specs=[coeffs] * 4 + [columns, depth, wide],
            out_specs=columns,
            scratch_shapes=BLOCKS,
        ),
        out_shape=COLUMNS,
        compiler_params=ALONE,
        cost_estimate=cost(10),
        name="end_columns",
    )(where, *coeffs_in, bypass, jnp.asarray(DEPTH), jnp.asarray(WIDTH))


def order_table(where_ref, table_ref, order_ref):
    for k in range(GY):
        owner = ((where_ref[2] + (k & 6)) & 7) ^ (k & 1)
        start = pl.multiple_of(owner * 48, 16)
        order_ref[48 * k : 48 * (k + 1)] = table_ref[0, pl.ds(start, 48), :]


def line_kernel(where_ref, a_ref, b_ref, c_ref, table_ref, out_ref):
    for j in range(GROUPS):
        lanes = slice(GL * j, GL * (j + 1))
        parts = [ref[:, :, lanes].astype(F32) for ref in (a_ref, b_ref, c_ref)]
        rows = (parts[0] + parts[1] + parts[2]).astype(BF).reshape(STEPS * ROWS, GL)
        out_ref[:, :, lanes] = dot(table_ref[0], rows).astype(BF).reshape(GY, 48, GL)


def unline_kernel(where_ref, modes_ref, table_ref, out_ref):
    for j in range(GROUPS):
        lanes = slice(GL * j, GL * (j + 1))
        rows = modes_ref[:, :, lanes].reshape(GY * 48, GL)
        out_ref[:, :, lanes] = dot(table_ref[0], rows, 0, 0).astype(BF).reshape(STEPS, ROWS, GL)


def unline_set_kernel(where_ref, *refs):
    *modes_refs, table_ref, out_ref, order_ref = refs
    for k in range(GY):
        owner = ((where_ref[2] + (k & 6)) & 7) ^ (k & 1)
        start = pl.multiple_of(owner * 48, 16)
        order_ref[48 * k : 48 * (k + 1)] = table_ref[0, pl.ds(start, 48), :]
    for j in range(GROUPS):
        lanes = slice(GL * j, GL * (j + 1))
        rows = jnp.concatenate([ref[:, lanes] for ref in modes_refs], axis=0)
        out_ref[:, :, lanes] = dot(order_ref[...], rows, 0, 0).astype(BF).reshape(STEPS, ROWS, GL)


def line_call(kernel, name, where, ins, out, scratch=()):
    whole = pl.BlockSpec(ins[0].shape, lambda i, w: (0,) * ins[0].ndim)
    table = pl.BlockSpec((1, GY * 48, STEPS * ROWS), lambda i, w: (w[2], 0, 0))
    return pl.pallas_call(
        kernel,
        grid_spec=pltpu.PrefetchScalarGridSpec(
            num_scalar_prefetch=1,
            grid=(1,),
            in_specs=[whole] * len(ins) + [table],
            out_specs=pl.BlockSpec(out.shape, lambda i, w: (0, 0, 0)),
            scratch_shapes=list(scratch),
        ),
        out_shape=out,
        compiler_params=ALONE,
        cost_estimate=cost(3),
        name=name,
    )(where, *ins, jnp.asarray(LINE))


def to_lines(where, *parts):
    out = jax.ShapeDtypeStruct((GY, 48, WIDE), BF)
    return line_call(line_kernel, "to_lines", where, parts, out)


def from_lines(where, modes):
    return line_call(unline_kernel, "from_lines", where, (modes,), COEFFS)


def from_line_set(where, modes):
    order = pltpu.VMEM((GY * 48, STEPS * ROWS), BF)
    return line_call(unline_set_kernel, "from_line_set", where, modes, COEFFS, [order])


UNROLL = 20
SETS = GX * KB
PAIR = 2 * CH
HALF = KX


def low_lanes():
    return lax.broadcasted_iota(jnp.int32, (SETS, 2 * HALF), 1) < HALF


def gather_modes(arrived, sum_ref, modes_ref, scale=None):
    total = arrived[0].astype(F32)
    for i in range(1, GY):
        total = total + arrived[i].astype(F32)
    sum_ref[...] = total.astype(BF).astype(F32)
    low = low_lanes()
    for j in range(CH // 2):
        lanes = slice(2 * HALF * j, 2 * HALF * (j + 1))
        for part in range(2):
            first = sum_ref[part * SETS : (part + 1) * SETS, lanes]
            second = sum_ref[(2 + part) * SETS : (3 + part) * SETS, lanes]
            if scale is not None:
                first = first * scale
                second = second * scale
            even = jnp.where(low, first, pltpu.roll(second, HALF, 1))
            odd = jnp.where(low, pltpu.roll(first, HALF, 1), second)
            modes_ref[pl.ds(4 * j + part, SETS, stride=PAIR), :] = even
            modes_ref[pl.ds(4 * j + 2 + part, SETS, stride=PAIR), :] = odd


def spread_modes(modes_ref, sum_ref, out_ref, scale=None):
    low = low_lanes()
    for j in range(CH // 2):
        lanes = slice(2 * HALF * j, 2 * HALF * (j + 1))
        for part in range(2):
            even = modes_ref[pl.ds(4 * j + part, SETS, stride=PAIR), :]
            odd = modes_ref[pl.ds(4 * j + 2 + part, SETS, stride=PAIR), :]
            if scale is not None:
                even = even * scale
                odd = odd * scale
            sum_ref[part * SETS : (part + 1) * SETS, lanes] = jnp.where(
                low, even, pltpu.roll(odd, HALF, 1)
            )
            sum_ref[(2 + part) * SETS : (3 + part) * SETS, lanes] = jnp.where(
                low, pltpu.roll(even, HALF, 1), odd
            )
    modes = sum_ref[...].astype(BF)
    for copy in range(out_ref.shape[0]):
        out_ref[copy] = modes


def fold_scale(where_ref):
    kz = where_ref[1] * KB + lax.broadcasted_iota(jnp.int32, (SETS, 2 * HALF), 0) % KB
    return jnp.where(kz == 0, 1.0, 2.0).astype(F32) / float(NX * NY * NZ)


def turned(rows):
    even = lax.broadcasted_iota(jnp.int32, rows.shape, 0) % 2 == 0
    up = pltpu.roll(rows, PAIR - 1, 0)
    down = pltpu.roll(rows, 1, 0)
    return jnp.where(even, -up, down)


def hand_out(where_ref, modes_ref, outs):
    for k in range(DP):
        chunk = lax.rem(where_ref[0] + k, DP)
        start = pl.multiple_of(chunk * KB * PAIR, 8)
        outs[k][...] = modes_ref[pl.ds(start, KB * PAIR), :].astype(BF)


def set_row(where_ref, k):
    block = (lax.rem(where_ref[0] + k, DP) ^ (2 * (where_ref[1] & 1))) * KB + pl.program_id(0)
    return pl.multiple_of(block * PAIR, 8)


def mix_kernel(
    where_ref, arrived_ref, w0, w1, w2, w3, out_ref, u0, u1, u2, u3,
    sum_ref, in_ref, mix_ref,
):
    step = pl.program_id(0)

    @pl.when(step == 0)
    def _():
        gather_modes(arrived_ref, sum_ref, in_ref)
        hand_out(where_ref, in_ref, [ref.at[0] for ref in (u0, u1, u2, u3)])

    for k, weight_ref in enumerate((w0, w1, w2, w3)):
        base = set_row(where_ref, k)

        def add(i, totals, weight_ref=weight_ref, base=base):
            by_real, by_imag = totals
            for r in range(UNROLL):
                c = i * UNROLL + r
                weight = weight_ref[0, c].astype(F32)
                by_real = by_real + weight * in_ref[pl.ds(base + 2 * c, 1), :]
                by_imag = by_imag + weight * in_ref[pl.ds(base + 2 * c + 1, 1), :]
            return by_real, by_imag

        zero = jnp.zeros((PAIR, 2 * HALF), F32)
        by_real, by_imag = lax.fori_loop(0, CH // UNROLL, add, (zero, zero))
        mix_ref[pl.ds(base, PAIR), :] = (by_real + turned(by_imag)).astype(BF).astype(F32)

    @pl.when(step == KB - 1)
    def _():
        spread_modes(mix_ref, sum_ref, out_ref, fold_scale(where_ref))


def back_kernel(
    where_ref, arrived_ref, w0, w1, w2, w3, s0, s1, s2, s3, out_ref, u0, u1, u2, u3,
    sum_ref, in_ref, mix_ref,
):
    step = pl.program_id(0)

    @pl.when(step == 0)
    def _():
        gather_modes(arrived_ref, sum_ref, in_ref, fold_scale(where_ref))
        hand_out(where_ref, in_ref, [ref.at[1] for ref in (u0, u1, u2, u3)])
        for spec_ref, ref in zip((s0, s1, s2, s3), (u0, u1, u2, u3)):
            ref[0] = spec_ref[0]

    for k, weight_ref in enumerate((w0, w1, w2, w3)):
        base = set_row(where_ref, k)
        grad = in_ref[pl.ds(base, PAIR), :]
        other = -turned(grad)

        @pl.loop(0, CH // UNROLL)
        def _(i, weight_ref=weight_ref, base=base, grad=grad, other=other):
            for r in range(UNROLL):
                c = i * UNROLL + r
                weight = weight_ref[0, c].astype(F32)
                mix_ref[pl.ds(base + 2 * c, 1), :] = jnp.sum(weight * grad, axis=0, keepdims=True)
                mix_ref[pl.ds(base + 2 * c + 1, 1), :] = jnp.sum(
                    weight * other, axis=0, keepdims=True
                )

    @pl.when(step == KB - 1)
    def _():
        spread_modes(mix_ref, sum_ref, out_ref)


def mode_call(kernel, name, where, arrived, weights, spectra=()):
    sets, copies = (2, GY) if spectra else (1, 1)

    def chunk(n):
        return pl.BlockSpec((n, KB * PAIR, 2 * HALF), lambda i, w: (0, 0, 0))

    return pl.pallas_call(
        kernel,
        grid_spec=pltpu.PrefetchScalarGridSpec(
            num_scalar_prefetch=1,
            grid=(KB,),
            in_specs=[pl.BlockSpec((GY, 48, WIDE), lambda i, w: (0, 0, 0))]
            + [pl.BlockSpec((1, CH, PAIR, 2 * HALF), lambda i, w: (i, 0, 0, 0))] * 4
            + [chunk(1)] * len(spectra),
            out_specs=[pl.BlockSpec((copies, 48, WIDE), lambda i, w: (0, 0, 0))]
            + [chunk(sets)] * 4,
            scratch_shapes=[
                pltpu.VMEM((48, WIDE), F32),
                pltpu.VMEM((SETS * PAIR, 2 * HALF), F32),
                pltpu.VMEM((SETS * PAIR, 2 * HALF), F32),
            ],
        ),
        out_shape=[jax.ShapeDtypeStruct((copies, 48, WIDE), BF)]
        + [jax.ShapeDtypeStruct((sets, KB * PAIR, 2 * HALF), BF)] * 4,
        compiler_params=ALONE,
        cost_estimate=cost(5),
        name=name,
    )(where, arrived, *weights, *spectra)


def outer_kernel(p0, p1, p2, p3, out_ref, spec_ref):
    pairs = (p0, p1, p2, p3)
    for k, ref in enumerate(pairs):
        spec_ref[k] = ref[0].astype(F32)
    for i in range(KB):
        grads = []
        others = []
        for ref in pairs:
            grad = ref[1].astype(F32)[i * PAIR : (i + 1) * PAIR]
            grads.append(grad)
            others.append(-turned(grad))

        @pl.loop(0, CH)
        def _(c):
            row = i * PAIR + 2 * c
            total = jnp.zeros((PAIR, 2 * HALF), F32)
            for k in range(DP):
                total = total + spec_ref[k, pl.ds(row, 1), :] * grads[k]
                total = total + spec_ref[k, pl.ds(row + 1, 1), :] * others[k]
            out_ref[i, c] = total


def outer_sum(pairs):
    return pl.pallas_call(
        outer_kernel,
        out_shape=jax.ShapeDtypeStruct((KB, CH, PAIR, 2 * HALF), F32),
        scratch_shapes=[pltpu.VMEM((DP, KB * PAIR, 2 * HALF), F32)],
        cost_estimate=cost(3),
        name="outer_sum",
    )(*pairs)


def swap(values, bit):
    return lax.ppermute(values, "gx", [(i, i ^ bit) for i in range(GX)])


def start_slabs(pieces, beside):
    own, far, near, across = pieces
    far_sum = (far.astype(F32) + swap(across, 1).astype(F32)).astype(BF)
    arrived, beside = lax.optimization_barrier((swap(far_sum, 2), beside))
    return (own, swap(near, 1), arrived), beside


def share_slabs(own, *beside):
    far, *beside = lax.optimization_barrier((swap(own, 2), *beside))
    return own, far, swap(own, 1), swap(far, 1), *beside


def gather_weights(weight):
    held = [weight]
    for k in range(1, DP):
        held.append(lax.ppermute(weight, "dp", [((a + k) % DP, a) for a in range(DP)]))
    return [part.reshape(KB, CH, PAIR, 2 * HALF) for part in held]


def gather_lines(modes):
    held = [modes, lax.ppermute(modes, "gy", [(g ^ 1, g) for g in range(GY)])]
    for step in range(2, GY, 2):
        pairs = [((g + step) % GY, g) for g in range(GY)]
        held += [lax.ppermute(part, "gy", pairs) for part in held[:2]]
    return held


def exchange_lines(parts):
    return lax.all_to_all(parts, "gy", split_axis=0, concat_axis=0, tiled=True)


def to_owners(chunks):
    moved = []
    for k, chunk in enumerate(chunks):
        pairs = [
            (a * GX + b, b * GX + (a + k) % DP) for a in range(DP) for b in range(GX)
        ]
        moved.append(lax.ppermute(chunk, ("dp", "gx"), pairs))
    return moved


def per_device(field, spectral_weight, bypass_weight, bias, cotangent):
    where = jnp.stack(
        [lax.axis_index("dp"), lax.axis_index("gx"), lax.axis_index("gy")]
    ).astype(jnp.int32)
    turn = [(a * GX + b, (b ^ (2 * (a % 2))) * GX + a) for a in range(DP) for b in range(GX)]
    weight = lax.ppermute(spectral_weight, ("dp", "gx"), turn)
    spread = jnp.asarray(SPREAD)

    def mixer_of(matrix):
        wide = dot(dot(spread, matrix).astype(BF), spread, 1, 1)
        return wide.astype(BF) * jnp.asarray(SAME)

    values = field[0]
    *pieces, weight = lax.optimization_barrier((*start_columns(where, values), weight))
    parts, bypass = start_slabs(pieces, bypass_columns(values, mixer_of(bypass_weight), bias))
    weights = gather_weights(weight)
    lines, weights[1], weights[3] = lax.optimization_barrier(
        (to_lines(where, *parts), weights[1], weights[3])
    )
    arrived = exchange_lines(lines)
    modes, *spectra = mode_call(mix_kernel, "mix_modes", where, arrived, weights)
    coeffs = share_slabs(from_line_set(where, gather_lines(modes[0])))
    activation, grad, *pieces = middle_columns(where, coeffs, bypass, cotangent[0])
    mixer = mixer_of(bypass_weight.T)
    parts, bypass = start_slabs(pieces, bypass_columns(grad, mixer, jnp.zeros_like(bias)))
    arrived = exchange_lines(to_lines(where, *parts))
    modes, *pairs = mode_call(back_kernel, "back_modes", where, arrived, weights, spectra)
    modes, *pairs = lax.optimization_barrier((exchange_lines(modes), *to_owners(pairs)))
    *coeffs, weight_grad = share_slabs(from_lines(where, modes), outer_sum(pairs))
    field_grad = end_columns(where, coeffs, bypass)
    return (
        activation[None],
        field_grad[None],
        weight_grad.reshape(KB, CH, CH, 2, 2 * HALF),
    )


def solution(mesh):
    placed = (
        P("dp", None, "gx", "gy"),
        P("dp", None, None, None, ("gx", "gy")),
        P(),
        P(),
        P("dp", None, "gx", "gy"),
    )
    return jax.shard_map(
        per_device,
        mesh=mesh,
        in_specs=placed,
        out_specs=(
            P("dp", None, "gx", "gy"),
            P("dp", None, "gx", "gy"),
            P("dp", None, None, None, ("gx", "gy")),
        ),
        check_vma=False,
    )
```
